32 devices in a mesh: dp: 8 (over z, x), tensor: 4 (over y, core).
Axes of the slice: x: 2, y: 2, z: 4, core: 2. Of those that a mesh axis runs over, the one named last changes fastest.
Arguments:
- tokens: bfloat16 [20480, 768], P(('dp', 'tensor')), may hold values from -6 to 6
- segment_ids: int32 [20480], P('dp'), may hold values from 0 to 8, as said below
- lengths: int32 [40], P('dp'), may hold values from 410 to 512, as said below
- w_query: bfloat16 [768, 768], P(None, 'tensor'), may hold values from -0.21875 to 0.21875
- b_query: float32 [768], P('tensor'), may hold values from -3 to 3
- w_key: bfloat16 [768, 768], P(None, 'tensor'), may hold values from -0.21875 to 0.21875
- w_value: bfloat16 [768, 768], P(None, 'tensor'), may hold values from -0.21875 to 0.21875
- b_value: float32 [768], P('tensor'), may hold values from -3 to 3
- w_output: bfloat16 [768, 768], P('tensor'), may hold values from -1.5 to 1.5
- b_output: float32 [768], replicated, may hold values from -2 to 2
- first_gain: float32 [768], replicated, may hold values from 0.5 to 1.5
- first_shift: float32 [768], replicated, may hold values from -2 to 2
- w_inner: bfloat16 [768, 3072], P(None, 'tensor'), may hold values from -0.21875 to 0.21875
- b_inner: float32 [3072], P('tensor'), may hold values from -3 to 3
- w_outer: bfloat16 [3072, 768], P('tensor'), may hold values from -0.109375 to 0.109375
- b_outer: float32 [768], replicated, may hold values from -2 to 2
- second_gain: float32 [768], replicated, may hold values from 0.5 to 1.5
- second_shift: float32 [768], replicated, may hold values from -2 to 2
- cotangent: bfloat16 [20480, 768], P(('dp', 'tensor')), may hold values from -6 to 6
Outputs:
- output: bfloat16 [20480, 768], P(('dp', 'tensor'))
- grad_tokens: bfloat16 [20480, 768], P(('dp', 'tensor'))
- grad_w_query: float32 [768, 768], P(None, 'tensor')
- grad_b_query: float32 [768], P('tensor')
- grad_w_key: float32 [768, 768], P(None, 'tensor')
- grad_w_value: float32 [768, 768], P(None, 'tensor')
- grad_b_value: float32 [768], P('tensor')
- grad_w_output: float32 [768, 768], P('tensor')
- grad_b_output: float32 [768], P('tensor')
- grad_first_gain: float32 [768], P('tensor')
- grad_first_shift: float32 [768], P('tensor')
- grad_w_inner: float32 [768, 3072], P(None, 'tensor')
- grad_b_inner: float32 [3072], P('tensor')
- grad_w_outer: float32 [3072, 768], P('tensor')
- grad_b_outer: float32 [768], P('tensor')
- grad_second_gain: float32 [768], P('tensor')
- grad_second_shift: float32 [768], P('tensor')
The draws below stay inside these ranges and needn't reach their ends.
Inputs may be any that keep to these rules, and one draw needn't show every extreme that they name: `segment_ids`: along each packed sequence of 512 positions the ids start at 0, never fall, and rise by at most one a position; the first sequence reaches the largest id. `lengths`: live positions of each packed sequence; the first sequence is full.
All inputs are finite; a program needn't handle non-finite values.
Results may differ from the reference program's by a relative error of at most 0.019.
Values may be sent and summed in bfloat16 or wider, within the bound.
A program may use at most 128 MiB of HBM per device.

```python
import math
import jax
import jax.numpy as jnp
from jax import lax

D = 768
HEADS = 12
HD = 64
FF = 3072
LEN = 512
NSEQ = 40
TOKENS = 20480


def draw_lengths(key, part):
    spare = jax.random.randint(key, (NSEQ,), 0, LEN // 5 + 1)
    spare = spare.at[0].set(0)
    return (LEN - spare).astype(jnp.int32)


def draw_segment_ids(key, part):
    ceiling = max(LEN // 64, 1)
    marks = jax.random.randint(key, (NSEQ, LEN), 0, max(LEN // 4, 2))
    starts = (marks == 0).astype(jnp.int32)
    places = jnp.arange(LEN)
    step = max(LEN // (ceiling + 1), 1)
    leading = ((places % step == 0) & (places > 0)).astype(jnp.int32)
    starts = starts.at[0].set(leading)
    starts = starts.at[:, 0].set(0)
    ids = jnp.minimum(jnp.cumsum(starts, axis=1), ceiling)
    return ids.reshape(NSEQ * LEN).astype(jnp.int32)


def block_levels(key, dims, split, smallest, high):
    def one(dim, parts):
        heights = jax.random.uniform(jax.random.fold_in(jax.random.fold_in(key, 6), dim), (parts,), jnp.float32, smallest / len(split), high / len(split))
        return jnp.repeat(jnp.exp(heights), dims[dim] // parts).reshape((-1,) + (1,) * (len(dims) - dim - 1))

    level = one(*split[0])
    for cut in split[1:]:
        level = level * one(*cut)
    return level


def scatter_about(own_key, dims, deviation, most, cuts=(), dtype=jnp.bfloat16):
    factor_of = block_levels(own_key, dims, cuts, -0.22, 0.18) if cuts else 1.0
    values = jax.random.normal(own_key, dims, jnp.float32) * deviation * factor_of
    return jnp.minimum(jnp.maximum(values, -most), most).astype(dtype)


def setup_inputs(seed: int = 0) -> dict:
    arg_keys = jax.random.split(jax.random.key(seed), 20)
    return {
        "tokens": scatter_about(arg_keys[0], (TOKENS, D), 1.0, 6.0, ((0, 32),)),
        "segment_ids": draw_segment_ids(jax.random.fold_in(arg_keys[19], 71), 0),
        "lengths": draw_lengths(jax.random.fold_in(arg_keys[19], 71), 0),
        "w_query": scatter_about(arg_keys[3], (D, D), D ** -0.5, 0.21875, ((1, 4),)),
        "b_query": scatter_about(arg_keys[4], (D,), 0.5, 3.0, ((0, 4),), jnp.float32),
        "w_key": scatter_about(arg_keys[5], (D, D), D ** -0.5, 0.21875, ((1, 4),)),
        "w_value": scatter_about(arg_keys[6], (D, D), D ** -0.5, 0.21875, ((1, 4),)),
        "b_value": scatter_about(arg_keys[7], (D,), 0.5, 3.0, ((0, 4),), jnp.float32),
        "w_output": scatter_about(arg_keys[8], (D, D), (D // 48) ** -0.5, 1.5, ((0, 4),)),
        "b_output": scatter_about(arg_keys[9], (D,), 0.3, 2.0, (), jnp.float32),
        "first_gain": jnp.clip(1.0 + 0.1 * jax.random.normal(arg_keys[10], (D,), jnp.float32), 0.5, 1.5),
        "first_shift": scatter_about(arg_keys[11], (D,), 0.3, 2.0, (), jnp.float32),
        "w_inner": scatter_about(arg_keys[12], (D, FF), D ** -0.5, 0.21875, ((1, 4),)),
        "b_inner": scatter_about(arg_keys[13], (FF,), 0.5, 3.0, ((0, 4),), jnp.float32),
        "w_outer": scatter_about(arg_keys[14], (FF, D), FF ** -0.5, 0.109375, ((0, 4),)),
        "b_outer": scatter_about(arg_keys[15], (D,), 0.3, 2.0, (), jnp.float32),
        "second_gain": jnp.clip(1.0 + 0.1 * jax.random.normal(arg_keys[16], (D,), jnp.float32), 0.5, 1.5),
        "second_shift": scatter_about(arg_keys[17], (D,), 0.3, 2.0, (), jnp.float32),
        "cotangent": scatter_about(arg_keys[18], (TOKENS, D), 1.0, 6.0, ((0, 32),)),
    }


@jax.custom_vjp
def low(v):
    return lax.optimization_barrier(v.astype(jnp.bfloat16)).astype(jnp.float32)

@jax.custom_vjp
def low_back(v):
    return v

def low_keep(v):
    return (low(v), None)

def low_pass(kept, grad):
    return (grad,)

def back_keep(v):
    return (v, None)

def back_low(kept, grad):
    return (low(grad),)
low.defvjp(low_keep, low_pass)
low_back.defvjp(back_keep, back_low)
EPSILON = 1e-12
NEGATIVE = -1000000000.0

def matmul(left, right):
    return jnp.dot(left, right, precision=lax.Precision.HIGHEST)

def normalize(value, gain, shift):
    average = lax.optimization_barrier(jnp.mean(value, axis=-1, keepdims=True))
    centered = value - average
    variance = lax.optimization_barrier(jnp.mean(centered * centered, axis=-1, keepdims=True))
    return centered * lax.rsqrt(variance + EPSILON) * gain + shift

def gelu_value(inner):
    return 0.5 * inner * (1.0 + lax.erf(inner * (1.0 / math.sqrt(2.0))))

def attend(block):
    query_rows, key_rows, value_rows, segments, length = block
    query_heads = query_rows.reshape(LEN, HEADS, HD)
    key_heads = key_rows.reshape(LEN, HEADS, HD)
    value_heads = value_rows.reshape(LEN, HEADS, HD)
    scores = low_back(jnp.einsum('qhd,khd->hqk', query_heads, key_heads, precision=lax.Precision.HIGHEST))
    places = jnp.arange(LEN)
    allowed = (segments[:, None] == segments[None, :]) & (places[None, :] < length) | (places[:, None] == places[None, :])
    logits = jnp.where(allowed[None], scores * (1.0 / math.sqrt(HD)), NEGATIVE)
    peak = lax.optimization_barrier(jnp.max(logits, axis=-1, keepdims=True))
    powers = jnp.exp(logits - peak)
    weights = low(powers / lax.optimization_barrier(jnp.sum(powers, axis=-1, keepdims=True)))
    context = jnp.einsum('hqk,khd->qhd', weights, value_heads, precision=lax.Precision.HIGHEST)
    return context.reshape(LEN, D)

def block_forward(params, rows_in, segments, lengths):
    w_query, b_query, w_key, w_value, b_value, w_output, b_output, first_gain, first_shift, w_inner, b_inner, w_outer, b_outer, second_gain, second_shift = params
    count = rows_in.shape[0] // LEN
    queries = low_back(low(matmul(rows_in, w_query) + b_query))
    key_rows = low_back(low(matmul(rows_in, w_key)))
    value_rows = low_back(low(matmul(rows_in, w_value) + b_value))
    context = lax.map(jax.checkpoint(attend), (queries.reshape(count, LEN, D), key_rows.reshape(count, LEN, D), value_rows.reshape(count, LEN, D), segments.reshape(count, LEN), lengths))
    context = low_back(low(context.reshape(count * LEN, D)))
    branch = low_back(matmul(context, w_output) + b_output)
    first = low(normalize(rows_in + branch, first_gain, first_shift))
    inner = low_back(matmul(first, w_inner) + b_inner)
    hidden = low(gelu_value(inner))
    feed = low_back(matmul(hidden, w_outer) + b_outer)
    return normalize(first + feed, second_gain, second_shift)

def add_pair(left, right):
    return left + right

def reference(tokens, segment_ids, lengths, w_query, b_query, w_key, w_value, b_value, w_output, b_output, first_gain, first_shift, w_inner, b_inner, w_outer, b_outer, second_gain, second_shift, cotangent):
    params = tuple((item.astype(jnp.float32) for item in (w_query, b_query, w_key, w_value, b_value, w_output, b_output, first_gain, first_shift, w_inner, b_inner, w_outer, b_outer, second_gain, second_shift)))
    per_block = math.gcd(NSEQ, max(1, 4096 // LEN))
    blocks = NSEQ // per_block
    block_rows = per_block * LEN

    def one_block(totals, pieces):
        rows_in, segments, lens, grads = pieces

        def forward(params_in, rows_float):
            return block_forward(params_in, rows_float, segments, lens)
        result, pullback = jax.vjp(forward, params, rows_in.astype(jnp.float32))
        param_grads, row_grads = pullback(grads.astype(jnp.float32))
        totals = jax.tree.map(add_pair, totals, param_grads)
        return (totals, (result.astype(jnp.bfloat16), row_grads.astype(jnp.bfloat16)))
    zeros = jax.tree.map(jnp.zeros_like, params)
    totals, (output, grad_tokens) = lax.scan(one_block, zeros, (tokens.reshape(blocks, block_rows, D), segment_ids.reshape(blocks, block_rows), lengths.reshape(blocks, per_block), cotangent.reshape(blocks, block_rows, D)))
    return (output.reshape(TOKENS, D), grad_tokens.reshape(TOKENS, D), totals[0], totals[1], totals[2], totals[3], totals[4], totals[5], totals[6], totals[7], totals[8], totals[9], totals[10], totals[11], totals[12], totals[13], totals[14])
```

```python
import math

import jax
import jax.numpy as jnp
from jax import lax
from jax.experimental import pallas as pl
from jax.experimental.pallas import tpu as pltpu
from jax.sharding import PartitionSpec as P

HD = 64
LEN = 512
HALF = LEN // 2
EPSILON = 1e-12
NEGATIVE = -1000000000.0
SCALE = 1.0 / math.sqrt(HD)
LOG2E = math.log2(math.e)
F32 = jnp.float32
BF16 = jnp.bfloat16
NN = (((1,), (0,)), ((), ()))
NT = (((1,), (1,)), ((), ()))
TN = (((0,), (0,)), ((), ()))


def dg(left, right, dims=NN):
    return lax.dot_general(left, right, dims, preferred_element_type=F32)


def norm_forward(value):
    average = jnp.mean(value, axis=-1, keepdims=True)
    centered = value - average
    variance = jnp.mean(centered * centered, axis=-1, keepdims=True)
    inverse = lax.rsqrt(variance + EPSILON)
    return centered * inverse, inverse


def norm_backward(grad, unit, inverse, gain):
    scaled = grad * gain
    first_mean = jnp.mean(scaled, axis=-1, keepdims=True)
    second_mean = jnp.mean(scaled * unit, axis=-1, keepdims=True)
    return inverse * (scaled - first_mean - unit * second_mean)


def gelu_and_slope(inner):
    cumulative = 0.5 * (1.0 + lax.erf(inner * (1.0 / math.sqrt(2.0))))
    slope = cumulative + inner * jnp.exp(-0.5 * inner * inner) * (1.0 / math.sqrt(2.0 * math.pi))
    return inner * cumulative, slope


def attend_forward(q_ref, k_ref, v_ref, bias_ref, ctx_ref, lse_ref, kc, vc):
    side = lax.axis_index("tensor") // 2
    a, b = side * HALF, side * HALF + LEN
    c = (1 - side) * 2 * LEN
    rows = q_ref.shape[0]
    c = pl.multiple_of(c, HALF)
    kc[pl.ds(0, HALF), :] = k_ref[pl.ds(c, HALF), :]
    kc[pl.ds(HALF, HALF), :] = k_ref[pl.ds(rows, HALF), :]
    vc[pl.ds(0, HALF), :] = v_ref[pl.ds(c, HALF), :]
    vc[pl.ds(HALF, HALF), :] = v_ref[pl.ds(rows, HALF), :]

    def pair(j, _):
        lanes = pl.ds(pl.multiple_of(j * 2 * HD, 2 * HD), 2 * HD)
        for start, at, count in ((a, 0, LEN), (b, LEN, LEN), (c, 2 * LEN, HALF)):
            start = pl.multiple_of(start, HALF)
            queries = q_ref[pl.ds(start, count), lanes]
            if count == LEN:
                keys = k_ref[pl.ds(start, LEN), lanes]
                values = v_ref[pl.ds(start, LEN), lanes]
            else:
                keys = kc[:, lanes]
                values = vc[:, lanes]
            bias = bias_ref[:, pl.ds(at, count)]
            outs = []
            for h in range(2):
                cols = slice(h * HD, (h + 1) * HD)
                logits = dg(keys[:, cols], queries[:, cols], NT) * (SCALE * LOG2E) + bias
                peak = jnp.max(logits, axis=0, keepdims=True)
                powers = jnp.exp2(logits - peak)
                total = jnp.sum(powers, axis=0, keepdims=True)
                weights = (powers * (1.0 / total)).astype(BF16)
                outs.append(dg(weights, values[:, cols], TN).astype(BF16))
                lse_ref[pl.ds(j * 2 + h, 1), pl.ds(at, count)] = peak + jnp.log2(total)
            ctx_ref[pl.ds(start, count), lanes] = jnp.concatenate(outs, axis=1)
        return 0

    lax.fori_loop(0, q_ref.shape[1] // (2 * HD), pair, 0)


def attend_backward(q_ref, k_ref, v_ref, g_ref, bias_ref, lse_ref, dq_ref, dk_ref, dv_ref, kc, vc):
    side = lax.axis_index("tensor") // 2
    a, b = side * HALF, side * HALF + LEN
    c = (1 - side) * 2 * LEN
    rows = q_ref.shape[0]
    c = pl.multiple_of(c, HALF)
    kc[pl.ds(0, HALF), :] = k_ref[pl.ds(c, HALF), :]
    kc[pl.ds(HALF, HALF), :] = k_ref[pl.ds(rows, HALF), :]
    vc[pl.ds(0, HALF), :] = v_ref[pl.ds(c, HALF), :]
    vc[pl.ds(HALF, HALF), :] = v_ref[pl.ds(rows, HALF), :]

    def pair(j, _):
        lanes = pl.ds(pl.multiple_of(j * 2 * HD, 2 * HD), 2 * HD)
        for start, at, count in ((a, 0, LEN), (b, LEN, LEN), (c, 2 * LEN, HALF)):
            start = pl.multiple_of(start, HALF)
            queries = q_ref[pl.ds(start, count), lanes]
            grads = g_ref[pl.ds(start, count), lanes]
            if count == LEN:
                keys = k_ref[pl.ds(start, LEN), lanes]
                values = v_ref[pl.ds(start, LEN), lanes]
            else:
                keys = kc[:, lanes]
                values = vc[:, lanes]
            bias = bias_ref[:, pl.ds(at, count)]
            dqs, dks, dvs = [], [], []
            for h in range(2):
                cols = slice(h * HD, (h + 1) * HD)
                row = lse_ref[pl.ds(j * 2 + h, 1), pl.ds(at, count)]
                logits = dg(keys[:, cols], queries[:, cols], NT) * (SCALE * LOG2E) + bias
                probs = jnp.exp2(logits - row)
                dprobs = dg(values[:, cols], grads[:, cols], NT)
                across = jnp.sum(probs * dprobs, axis=0, keepdims=True)
                dscores = (probs * (dprobs - across) * SCALE).astype(BF16)
                dvs.append(dg(probs.astype(BF16), grads[:, cols], NN).astype(BF16))
                dks.append(dg(dscores, queries[:, cols], NN).astype(BF16))
                dqs.append(dg(dscores, keys[:, cols], TN).astype(BF16))
            dq_ref[pl.ds(start, count), lanes] = jnp.concatenate(dqs, axis=1)
            dk, dv = jnp.concatenate(dks, axis=1), jnp.concatenate(dvs, axis=1)
            if count == LEN:
                dk_ref[pl.ds(start, LEN), lanes] = dk
                dv_ref[pl.ds(start, LEN), lanes] = dv
            else:
                dk_ref[pl.ds(start, HALF), lanes] = dk[:HALF]
                dv_ref[pl.ds(start, HALF), lanes] = dv[:HALF]
                dk_ref[pl.ds(rows, HALF), lanes] = dk[HALF:]
                dv_ref[pl.ds(rows, HALF), lanes] = dv[HALF:]
        return 0

    lax.fori_loop(0, q_ref.shape[1] // (2 * HD), pair, 0)


IN_VMEM = pl.BlockSpec(memory_space=pltpu.VMEM)


def local_call(kernel, outs, scratch, flops, operands):
    moved = sum(o.size * o.dtype.itemsize for o in operands)
    return pl.pallas_call(
        kernel,
        out_shape=outs,
        in_specs=[IN_VMEM] * len(operands),
        out_specs=[IN_VMEM] * len(outs),
        scratch_shapes=scratch,
        cost_estimate=pl.CostEstimate(flops=flops, bytes_accessed=moved, transcendentals=0),
        compiler_params=pltpu.CompilerParams(vmem_limit_bytes=48 << 20),
    )(*operands)


def interleave(own, other):
    rows, width = own.shape
    heads = width // HD
    both = jnp.stack([own.reshape(rows, heads, HD), other.reshape(rows, heads, HD)], axis=2)
    return both.reshape(rows, 2 * width)


def split_pairs(joined):
    rows, width = joined.shape
    both = joined.reshape(rows, width // (2 * HD), 2, HD)
    return both[:, :, 0].reshape(rows, width // 2), both[:, :, 1].reshape(rows, width // 2)


def mask_bias(segment_ids, lengths, side):
    segments = segment_ids.reshape(-1, LEN)
    ahead = jnp.arange(LEN)
    blocks = []
    for which in range(3):
        index = 3 * side + which if which < 2 else 2
        row = lax.dynamic_index_in_dim(segments, index, 0, keepdims=False)
        length = lax.dynamic_index_in_dim(lengths, index, 0, keepdims=False)
        if which < 2:
            key_places, key_segments, count = ahead, row, LEN
        else:
            key_places = (ahead + side * HALF) % LEN
            key_segments = jnp.where(side == 0, row, jnp.roll(row, -HALF))
            count = HALF
        same = key_segments[:, None] == key_segments[None, :count]
        live = key_places[:, None] < length
        diagonal = key_places[:, None] == key_places[None, :count]
        blocks.append(jnp.where(same & live | diagonal, 0.0, NEGATIVE))
    return jnp.concatenate(blocks, axis=1).astype(F32)


def shards(
    tokens,
    segment_ids,
    lengths,
    w_query,
    b_query,
    w_key,
    w_value,
    b_value,
    w_output,
    b_output,
    first_gain,
    first_shift,
    w_inner,
    b_inner,
    w_outer,
    b_outer,
    second_gain,
    second_shift,
    cotangent,
):
    place = lax.axis_index("tensor")
    core, side = place % 2, place // 2
    own_rows, wide = tokens.shape
    width = w_query.shape[1]
    units = w_inner.shape[1]
    chip_rows = 2 * own_rows
    c_start = (1 - side) * 2 * LEN

    def to_core(value):
        return lax.ppermute(value, "tensor", [(i, i ^ 1) for i in range(4)])

    def to_side(value):
        return lax.ppermute(value, "tensor", [(i, i ^ 2) for i in range(4)])

    def both_cores(value):
        other = to_core(value)
        return jnp.where(core == 0, jnp.concatenate([value, other]), jnp.concatenate([other, value]))

    def sum_cores(partial):
        theirs = lax.dynamic_slice_in_dim(partial, (1 - core) * own_rows, own_rows, 0)
        mine = lax.dynamic_slice_in_dim(partial, core * own_rows, own_rows, 0)
        return mine + to_core(theirs.astype(BF16)).astype(F32)

    joined_own = jnp.concatenate([w_query, w_key, w_value], axis=1)
    joined_other = to_side(joined_own)
    rows = both_cores(tokens)
    c_rows = to_side(lax.dynamic_slice_in_dim(rows, c_start, HALF, 0))
    bias_own = jnp.concatenate([b_query, b_value, b_inner])
    bias_other = to_side(bias_own)
    w_output_other = to_side(w_output)
    w_inner_other = to_side(w_inner)
    w_outer_other = to_side(w_outer)

    bias = mask_bias(segment_ids, lengths, side)
    b_q = interleave(bias_own[None, :width], bias_other[None, :width])
    b_v = interleave(bias_own[None, width : 2 * width], bias_other[None, width : 2 * width])
    parts = [
        interleave(joined_own[:, i * width : (i + 1) * width], joined_other[:, i * width : (i + 1) * width])
        for i in range(3)
    ]
    extended = jnp.concatenate([rows, c_rows])
    queries = (dg(rows, parts[0]) + b_q).astype(BF16)
    keys = dg(extended, parts[1]).astype(BF16)
    values = (dg(extended, parts[2]) + b_v).astype(BF16)
    both = 2 * width
    pairs_scratch = [pltpu.VMEM((LEN, both), BF16), pltpu.VMEM((LEN, both), BF16)]
    context, lse = local_call(
        attend_forward,
        [jax.ShapeDtypeStruct((chip_rows, both), BF16), jax.ShapeDtypeStruct((8, chip_rows), F32)],
        pairs_scratch,
        4 * chip_rows * LEN * both,
        (queries, keys, values, bias),
    )
    w_out = interleave(w_output.T, w_output_other.T)
    attended = sum_cores(dg(context, w_out, NT))
    first_unit, first_inverse = norm_forward(tokens.astype(F32) + attended + b_output)
    first = (first_unit * first_gain + first_shift).astype(BF16)
    first_rows = both_cores(first)
    w_in = jnp.concatenate([w_inner, w_inner_other], axis=1)
    b_in = jnp.concatenate([bias_own[2 * width :], bias_other[2 * width :]])
    inner = dg(first_rows, w_in) + b_in
    hidden, slope = gelu_and_slope(inner)
    hidden = hidden.astype(BF16)
    slope = slope.astype(BF16)
    w_down = jnp.concatenate([w_outer, w_outer_other], axis=0)
    feed = sum_cores(dg(hidden, w_down))
    second_unit, second_inverse = norm_forward(first.astype(F32) + feed + b_outer)
    output = (second_unit * second_gain + second_shift).astype(BF16)
    upstream = cotangent.astype(F32)
    grad_second = norm_backward(upstream, second_unit, second_inverse, second_gain)
    grad_second_gain = jnp.sum(upstream * second_unit, axis=0)
    grad_second_shift = jnp.sum(upstream, axis=0)
    grad_feed = grad_second.astype(BF16)
    grad_b_outer = jnp.sum(grad_feed.astype(F32), axis=0)
    feed_rows = both_cores(grad_feed)
    grad_w_down = dg(hidden, feed_rows, TN).astype(BF16)
    outer_away = to_side(grad_w_down[units:])
    grad_inner = (dg(feed_rows, w_down, NT) * slope.astype(F32)).astype(BF16)
    grad_b_in = jnp.sum(grad_inner.astype(F32), axis=0)
    grad_w_in = dg(first_rows, grad_inner, TN).astype(BF16)
    inner_away = to_side(grad_w_in[:, units:])
    grad_first = grad_second + sum_cores(dg(grad_inner, w_in, NT))
    grad_branch = norm_backward(grad_first, first_unit, first_inverse, first_gain)
    grad_first_gain = jnp.sum(grad_first * first_unit, axis=0)
    grad_first_shift = jnp.sum(grad_first, axis=0)
    grad_attended = grad_branch.astype(BF16)
    grad_b_output = jnp.sum(grad_attended.astype(F32), axis=0)
    branch_rows = both_cores(grad_attended)
    grad_w_out = dg(branch_rows, context, TN).astype(BF16)
    grad_context = dg(branch_rows, w_out).astype(BF16)
    grad_queries, grad_keys, grad_values = local_call(
        attend_backward,
        [
            jax.ShapeDtypeStruct((chip_rows, both), BF16),
            jax.ShapeDtypeStruct((chip_rows + HALF, both), BF16),
            jax.ShapeDtypeStruct((chip_rows + HALF, both), BF16),
        ],
        pairs_scratch,
        10 * chip_rows * LEN * both,
        (queries, keys, values, grad_context, bias, lse),
    )
    away = to_side(jnp.concatenate([grad_keys[chip_rows:], grad_values[chip_rows:]], axis=1))

    def add_c(grads, share):
        mine = lax.dynamic_slice_in_dim(grads, c_start, HALF, 0)
        summed = (mine.astype(F32) + share.astype(F32)).astype(BF16)
        return lax.dynamic_update_slice_in_dim(grads[:chip_rows], summed, c_start, 0)

    away_keys = interleave(*reversed(split_pairs(away[:, :both])))
    away_values = interleave(*reversed(split_pairs(away[:, both:])))
    grad_joined = jnp.concatenate(
        [grad_queries, add_c(grad_keys, away_keys), add_c(grad_values, away_values)], axis=1
    )
    weights_joined = jnp.concatenate(parts, axis=1)
    grad_w_joined = dg(rows, grad_joined, TN).astype(BF16)
    grad_bias = jnp.sum(grad_joined.astype(F32), axis=0, keepdims=True)
    grad_tokens = (grad_branch + sum_cores(dg(grad_joined, weights_joined, NT))).astype(BF16)

    pieces = [split_pairs(grad_w_joined[:, i * both : (i + 1) * both]) for i in range(3)]
    pieces.append(split_pairs(grad_w_out))
    attention_own = jnp.concatenate([p[0] for p in pieces], axis=1)
    attention_away = to_side(jnp.concatenate([p[1] for p in pieces], axis=1))

    def over_groups(own, theirs):
        return lax.psum((own.astype(F32) + theirs.astype(F32)).astype(BF16), "dp").astype(F32)

    outer_sum = over_groups(grad_w_down[:units], outer_away)
    inner_sum = over_groups(grad_w_in[:, :units], inner_away)
    attention_sum = over_groups(attention_own, attention_away)

    small = jnp.stack(
        [
            grad_b_output,
            grad_first_gain,
            grad_first_shift,
            grad_b_outer,
            grad_second_gain,
            grad_second_shift,
        ]
    )
    small_flat = small.reshape(6, 4, wide // 4).transpose(1, 0, 2).reshape(4, -1)
    biases = [split_pairs(grad_bias[:, :both]), split_pairs(grad_bias[:, 2 * both :])]
    bias_rows = [
        jnp.concatenate([biases[0][i][0], biases[1][i][0], grad_b_in[i * units : (i + 1) * units]]) for i in range(2)
    ]
    index = jnp.arange(4)[:, None]
    bias_flat = jnp.where(index == place, bias_rows[0], jnp.where(index == place ^ 2, bias_rows[1], 0.0))
    totals = lax.psum(jnp.concatenate([small_flat, bias_flat], axis=1), ("dp", "tensor"))
    total = lax.dynamic_index_in_dim(totals, place, 0, keepdims=False)
    shares = total[: 6 * width].reshape(6, width)
    rest = total[6 * width :]
    return (
        output,
        grad_tokens,
        attention_sum[:, :width],
        rest[:width],
        attention_sum[:, width : 2 * width],
        attention_sum[:, 2 * width : 3 * width],
        rest[width : 2 * width],
        attention_sum[:, 3 * width :].T,
        shares[0],
        shares[1],
        shares[2],
        inner_sum,
        rest[2 * width :],
        outer_sum,
        shares[3],
        shares[4],
        shares[5],
    )


def solution(mesh):
    in_specs = (
        P(("dp", "tensor"), None),
        P("dp"),
        P("dp"),
        P(None, "tensor"),
        P("tensor"),
        P(None, "tensor"),
        P(None, "tensor"),
        P("tensor"),
        P("tensor", None),
        P(),
        P(),
        P(),
        P(None, "tensor"),
        P("tensor"),
        P("tensor", None),
        P(),
        P(),
        P(),
        P(("dp", "tensor"), None),
    )
    out_specs = (
        P(("dp", "tensor"), None),
        P(("dp", "tensor"), None),
        P(None, "tensor"),
        P("tensor"),
        P(None, "tensor"),
        P(None, "tensor"),
        P("tensor"),
        P("tensor", None),
        P("tensor"),
        P("tensor"),
        P("tensor"),
        P(None, "tensor"),
        P("tensor"),
        P("tensor", None),
        P("tensor"),
        P("tensor"),
        P("tensor"),
    )
    return jax.shard_map(shards, mesh=mesh, in_specs=in_specs, out_specs=out_specs, check_vma=False)
```

```python
import functools
import math

import jax
import jax.numpy as jnp
from jax import lax
from jax.experimental import pallas as pl
from jax.experimental.pallas import tpu as pltpu
from jax.sharding import PartitionSpec as P

HD = 64
LEN = 512
HALF = LEN // 2
EPSILON = 1e-12
NEGATIVE = -1000000000.0
SCALE = 1.0 / math.sqrt(HD)
LOG2E = math.log2(math.e)
F32 = jnp.float32
BF16 = jnp.bfloat16
NN = (((1,), (0,)), ((), ()))
NT = (((1,), (1,)), ((), ()))
TN = (((0,), (0,)), ((), ()))


def dg(left, right, dims=NN):
    return lax.dot_general(left, right, dims, preferred_element_type=F32)


def norm_forward(value):
    average = jnp.mean(value, axis=-1, keepdims=True)
    centered = value - average
    variance = jnp.mean(centered * centered, axis=-1, keepdims=True)
    inverse = lax.rsqrt(variance + EPSILON)
    return centered * inverse, inverse


def norm_backward(grad, unit, inverse, gain):
    scaled = grad * gain
    first_mean = jnp.mean(scaled, axis=-1, keepdims=True)
    second_mean = jnp.mean(scaled * unit, axis=-1, keepdims=True)
    return inverse * (scaled - first_mean - unit * second_mean)


def gelu_and_slope(inner):
    cumulative = 0.5 * (1.0 + lax.erf(inner * (1.0 / math.sqrt(2.0))))
    slope = cumulative + inner * jnp.exp(-0.5 * inner * inner) * (1.0 / math.sqrt(2.0 * math.pi))
    return inner * cumulative, slope


def attend_forward(q_ref, k_ref, v_ref, bias_ref, ctx_ref, lse_ref, kc, vc):
    side = lax.axis_index("tensor") // 2
    a, b = side * HALF, side * HALF + LEN
    c = (1 - side) * 2 * LEN
    rows = q_ref.shape[0]
    c = pl.multiple_of(c, HALF)
    kc[pl.ds(0, HALF), :] = k_ref[pl.ds(c, HALF), :]
    kc[pl.ds(HALF, HALF), :] = k_ref[pl.ds(rows, HALF), :]
    vc[pl.ds(0, HALF), :] = v_ref[pl.ds(c, HALF), :]
    vc[pl.ds(HALF, HALF), :] = v_ref[pl.ds(rows, HALF), :]

    def pair(j, _):
        lanes = pl.ds(pl.multiple_of(j * 2 * HD, 2 * HD), 2 * HD)
        for start, at, count in ((a, 0, LEN), (b, LEN, LEN), (c, 2 * LEN, HALF)):
            start = pl.multiple_of(start, HALF)
            queries = q_ref[pl.ds(start, count), lanes]
            if count == LEN:
                keys = k_ref[pl.ds(start, LEN), lanes]
                values = v_ref[pl.ds(start, LEN), lanes]
            else:
                keys = kc[:, lanes]
                values = vc[:, lanes]
            bias = bias_ref[:, pl.ds(at, count)]
            outs = []
            for h in range(2):
                cols = slice(h * HD, (h + 1) * HD)
                logits = dg(keys[:, cols], queries[:, cols], NT) * (SCALE * LOG2E) + bias
                peak = jnp.max(logits, axis=0, keepdims=True)
                powers = jnp.exp2(logits - peak)
                total = jnp.sum(powers, axis=0, keepdims=True)
                weights = (powers * (1.0 / total)).astype(BF16)
                outs.append(dg(weights, values[:, cols], TN).astype(BF16))
                lse_ref[pl.ds(j * 2 + h, 1), pl.ds(at, count)] = peak + jnp.log2(total)
            ctx_ref[pl.ds(start, count), lanes] = jnp.concatenate(outs, axis=1)
        return 0

    lax.fori_loop(0, q_ref.shape[1] // (2 * HD), pair, 0)


MESH = pl.DeviceIdType.MESH


class Unit:
    def __init__(self, own, other, from_side, from_x, from_z, total):
        self.own, self.other, self.total = own, other, total
        self.from_side, self.from_x, self.from_z = from_side, from_x, from_z


class Rounds:
    def __init__(self, units, groups, sems, far, f_out, f_in):
        self.units = units
        self.from_far, self.f_out, self.f_in = far, f_out, f_in
        self.place = lax.axis_index("tensor")
        group = lax.axis_index("dp")
        self.x, self.z, self.far = group % 2, (group // 2) % 4, group // 8
        self.more = groups // 8
        (self.y_out, self.y_in, self.x_out, self.x_in, self.z_out, self.z_in) = sems[:6]
        (self.g_out, self.g_in, self.h_out, self.h_in) = sems[6:10]
        self.sent = []

    def dp_at(self, x, z):
        return {"dp": self.far * 8 + z * 2 + x}

    def copy(self, source, target, out, into, device):
        return pltpu.make_async_remote_copy(
            src_ref=source, dst_ref=target, send_sem=out, recv_sem=into, device_id=device, device_id_type=MESH
        )

    def start(self, copy):
        copy.start()
        self.sent.append(copy)

    def y_copy(self, u):
        unit = self.units[u]
        side = {"tensor": (self.place + 2) % 4}
        return self.copy(unit.other(pl.ds(0, 8)), unit.from_side, self.y_out.at[u], self.y_in.at[u], side)

    def x_copy(self, u):
        unit = self.units[u]
        away = unit.own(pl.ds((1 - self.x) * 4, 4))
        return self.copy(away, unit.from_x, self.x_out.at[u], self.x_in.at[u], self.dp_at(1 - self.x, self.z))

    def z_copy(self, u, step):
        unit = self.units[u]
        there = (self.z + step) % 4
        away = unit.own(self.x * 4 + there)
        slot = unit.from_z(step - 1)
        return self.copy(
            away, slot, self.z_out.at[u, step - 1], self.z_in.at[u, step - 1], self.dp_at(self.x, there)
        )

    def g_copy(self, u, step, origin):
        unit = self.units[u]
        there = (self.z + step) % 4
        piece = unit.total(self.x * 4 + origin)
        return self.copy(
            piece, piece, self.g_out.at[u, step - 1], self.g_in.at[u, step - 1], self.dp_at(self.x, there)
        )

    def h_copy(self, u, half):
        unit = self.units[u]
        piece = unit.total(pl.ds(half * 4, 4))
        return self.copy(piece, piece, self.h_out.at[u], self.h_in.at[u], self.dp_at(1 - self.x, self.z))

    def y_start(self, u):
        self.start(self.y_copy(u))

    def x_start(self, u):
        unit = self.units[u]
        self.y_copy(u).wait_recv()
        for i in range(8):
            own = unit.own(i)
            own[...] = (own[...].astype(F32) + unit.from_side.at[i][...].astype(F32)).astype(BF16)
        self.start(self.x_copy(u))

    def z_start(self, u):
        unit = self.units[u]
        self.x_copy(u).wait_recv()
        for i in range(4):
            own = unit.own(self.x * 4 + i)
            own[...] = (own[...].astype(F32) + unit.from_x.at[i][...].astype(F32)).astype(BF16)
        for step in (1, 2, 3):
            self.start(self.z_copy(u, step))

    def g_start(self, u):
        unit = self.units[u]
        value = unit.own(self.x * 4 + self.z)[...].astype(F32)
        for step in (1, 2, 3):
            self.z_copy(u, step).wait_recv()
            value = value + unit.from_z(step - 1)[...].astype(F32)
        if self.more > 1:
            value = self.far_sum(u, value)
        unit.total(self.x * 4 + self.z)[...] = value.astype(BF16)
        for step in (1, 2, 3):
            self.start(self.g_copy(u, step, self.z))

    def far_sum(self, u, value):
        unit = self.units[u]
        own = unit.own(self.x * 4 + self.z)
        own[...] = value.astype(BF16)
        slots = self.from_far.at[u]
        copies = []
        for step in range(1, self.more):
            peer = {"dp": ((self.far + step) % self.more) * 8 + self.z * 2 + self.x}
            slot = slots.at[step - 1, pl.ds(0, own.shape[0]), pl.ds(0, own.shape[1])]
            copies.append(self.copy(own, slot, self.f_out.at[u, step - 1], self.f_in.at[u, step - 1], peer))
            self.start(copies[-1])
        for step in range(1, self.more):
            copies[step - 1].wait_recv()
            value = value + slots[step - 1, pl.ds(0, own.shape[0]), pl.ds(0, own.shape[1])].astype(F32)
        return value

    def h_start(self, u):
        for step in (1, 2, 3):
            self.g_copy(u, step, (self.z - step + 4) % 4).wait_recv()
        self.start(self.h_copy(u, self.x))

    def end(self, u):
        self.h_copy(u, 1 - self.x).wait_recv()

    def drain(self):
        for copy in self.sent:
            copy.wait_send()


def attend_back(q, k, v, g, bias, row):
    logits = dg(k, q, NT) * (SCALE * LOG2E) + bias
    probs = jnp.exp2(logits - row)
    dprobs = dg(v, g, NT)
    across = jnp.sum(probs * dprobs, axis=0, keepdims=True)
    dscores = (probs * (dprobs - across) * SCALE).astype(BF16)
    dv = dg(probs.astype(BF16), g, NN).astype(BF16)
    dk = dg(dscores, q, NN).astype(BF16)
    dq = dg(dscores, k, TN).astype(BF16)
    return dq, dk, dv


def pair_back(q, k, v, g, bias, rows):
    done = []
    for h in range(2):
        cols = slice(h * HD, (h + 1) * HD)
        done.append(attend_back(q[:, cols], k[:, cols], v[:, cols], g[:, cols], bias, rows[h]))
    return [jnp.concatenate([done[0][i], done[1][i]], axis=1) for i in range(3)]


def swap_halves(value):
    return jnp.concatenate([value[:, HD:], value[:, :HD]], axis=1)


def rear_kernel(
    groups,
    q_ref,
    k_ref,
    v_ref,
    g_ref,
    bias_ref,
    lse_ref,
    x_ref,
    ctx_ref,
    branch_ref,
    w_ref,
    residual_ref,
    inner_own,
    inner_other,
    outer_own,
    outer_other,
    small_ref,
    inner_total,
    outer_total,
    attention_total,
    tokens_out,
    small_out,
    kc,
    vc,
    dq,
    dk,
    dv,
    away,
    back,
    pair_own,
    pair_other,
    wide_y,
    wide_x,
    wide_z,
    pair_y,
    pair_x,
    pair_z,
    far,
    partial,
    partial_in,
    tiny,
    tiny_t,
    tiny_d,
    y_out,
    y_in,
    x_out,
    x_in,
    z_out,
    z_in,
    g_out,
    g_in,
    h_out,
    h_in,
    f_out,
    f_in,
    c_out,
    c_in,
    p_out,
    p_in,
    t_out,
    t_in,
    d_out,
    d_in,
):
    place = lax.axis_index("tensor")
    group = lax.axis_index("dp")
    core, side = place % 2, place // 2
    rows = q_ref.shape[0]
    own_rows = rows // 2
    pairs = q_ref.shape[1] // (2 * HD)
    a = side * HALF
    c = pl.multiple_of((1 - side) * 2 * LEN, HALF)

    barrier = pltpu.get_barrier_semaphore()
    for step in (1, 2, 3):
        pl.semaphore_signal(barrier, inc=1, device_id={"tensor": (place + step) % 4}, device_id_type=MESH)

    def greet(step, _):
        peer = (group + step) % groups
        pl.semaphore_signal(barrier, inc=1, device_id={"dp": peer}, device_id_type=MESH)
        return 0

    lax.fori_loop(1, groups, greet, 0)
    pl.semaphore_wait(barrier, 3 + groups - 1)

    units = []
    for own, other, total, base in ((outer_own, outer_other, outer_total, 0), (inner_own, inner_other, inner_total, 3)):
        for i in range(3):
            units.append(
                Unit(
                    lambda s, r=own, i=i: r.at[s, i],
                    lambda s, r=other, i=i: r.at[s, i],
                    wide_y.at[base + i],
                    wide_x.at[base + i],
                    lambda s, n=base + i: wide_z.at[n, s],
                    lambda s, r=total, i=i: r.at[s, i],
                )
            )
    for j in range(pairs):
        units.append(
            Unit(
                lambda s, j=j: pair_own.at[j, s],
                lambda s, j=j: pair_other.at[j, s],
                pair_y.at[j],
                pair_x.at[j],
                lambda s, j=j: pair_z.at[j, s],
                lambda s, j=j: attention_total.at[j, s],
            )
        )
    sems = (y_out, y_in, x_out, x_in, z_out, z_in, g_out, g_in, h_out, h_in)
    rounds = Rounds(units, groups, sems, far, f_out, f_in)

    kc[pl.ds(0, HALF), :] = k_ref[pl.ds(c, HALF), :]
    kc[pl.ds(HALF, HALF), :] = k_ref[pl.ds(rows, HALF), :]
    vc[pl.ds(0, HALF), :] = v_ref[pl.ds(c, HALF), :]
    vc[pl.ds(HALF, HALF), :] = v_ref[pl.ds(rows, HALF), :]

    def lanes_of(j):
        return pl.ds(pl.multiple_of(j * 2 * HD, 2 * HD), 2 * HD)

    def half_pair(j, _):
        lanes = lanes_of(j)
        at = pl.ds(2 * LEN, HALF)
        stats = [lse_ref[pl.ds(j * 2 + h, 1), at] for h in range(2)]
        mine = pl.ds(c, HALF)
        d_q, d_k, d_v = pair_back(
            q_ref[mine, lanes], kc[:, lanes], vc[:, lanes], g_ref[mine, lanes], bias_ref[:, at], stats
        )
        dq[mine, lanes] = d_q
        dk[mine, lanes] = d_k[:HALF]
        dv[mine, lanes] = d_v[:HALF]
        away[0, :, lanes] = d_k[HALF:]
        away[1, :, lanes] = d_v[HALF:]
        return 0

    lax.fori_loop(0, pairs, half_pair, 0)
    swap = rounds.copy(away, back, c_out, c_in, {"tensor": (place + 2) % 4})
    rounds.start(swap)
    for u in range(6):
        rounds.y_start(u)

    def whole_pair(j):
        def body(i, _):
            lanes = lanes_of(j)
            mine = pl.ds(pl.multiple_of(a + i * LEN, HALF), LEN)
            at = pl.ds(pl.multiple_of(i * LEN, LEN), LEN)
            stats = [lse_ref[pl.ds(j * 2 + h, 1), at] for h in range(2)]
            d_q, d_k, d_v = pair_back(
                q_ref[mine, lanes], k_ref[mine, lanes], v_ref[mine, lanes], g_ref[mine, lanes], bias_ref[:, at], stats
            )
            dq[mine, lanes] = d_q
            dk[mine, lanes] = d_k
            dv[mine, lanes] = d_v
            return 0

        lax.fori_loop(0, 2, body, 0)

    def add_share(j):
        lanes = lanes_of(j)
        mine = pl.ds(c, HALF)
        for i, grads in ((0, dk), (1, dv)):
            share = swap_halves(back[i, :, lanes]).astype(F32)
            grads[mine, lanes] = (grads[mine, lanes].astype(F32) + share).astype(BF16)

    def weight_pair(j):
        lanes = lanes_of(j)
        block = x_ref.shape[1] // 2

        def body(i, _):
            columns = pl.ds(pl.multiple_of(i * block, 128), block)
            left = x_ref[:, columns]
            parts = [dg(left, grads[:, lanes], TN) for grads in (dq, dk, dv)]
            parts.append(dg(branch_ref[:, columns], ctx_ref[:, lanes], TN))
            own = jnp.concatenate([p[:, :HD] for p in parts], axis=1).astype(BF16)
            other = jnp.concatenate([p[:, HD:] for p in parts], axis=1).astype(BF16)
            where = pl.ds(i * 4, 4)
            pair_own[j, where] = own.reshape(4, block // 4, 4 * HD)
            pair_other[j, where] = other.reshape(4, block // 4, 4 * HD)
            return 0

        lax.fori_loop(0, 2, body, 0)
        rounds.y_start(6 + j)

    def input_rows(start):
        both = pairs * 2 * HD
        mine = pl.ds(pl.multiple_of(start, 128), own_rows)
        value = dg(dq[mine, :], w_ref[:, pl.ds(0, both)], NT)
        value = value + dg(dk[mine, :], w_ref[:, pl.ds(both, both)], NT)
        return value + dg(dv[mine, :], w_ref[:, pl.ds(2 * both, both)], NT)

    whole_pair(0)
    rounds.x_start(0)
    swap.wait_recv()
    for j in range(pairs):
        add_share(j)
    weight_pair(0)
    rounds.x_start(1)
    rounds.z_start(0)
    whole_pair(1)
    rounds.g_start(0)
    rounds.z_start(1)
    rounds.x_start(2)
    weight_pair(1)
    rounds.h_start(0)
    rounds.g_start(1)
    rounds.z_start(2)
    whole_pair(2)
    rounds.x_start(3)
    weight_pair(2)
    rounds.h_start(1)
    rounds.g_start(2)

    width = 3 * HD
    tiny[...] = small_ref[...]

    def bias_sum(grads):
        total = jnp.sum(grads[...].astype(F32), axis=0, keepdims=True)
        heads = [total[:, i * HD : (i + 1) * HD] for i in range(2 * pairs)]
        return jnp.concatenate(heads[0::2], axis=1), jnp.concatenate(heads[1::2], axis=1)

    for grads, at in ((dq, 2 * width), (dv, 3 * width)):
        mine, theirs = bias_sum(grads)
        tiny[place, pl.ds(1, 1), pl.ds(at, width)] = mine
        tiny[(place + 2) % 4, pl.ds(1, 1), pl.ds(at, width)] = theirs
    tiny_copies = []
    for step in (1, 2, 3):
        peer = (place + step) % 4
        tiny_copies.append(
            rounds.copy(tiny.at[peer], tiny_t.at[step - 1], t_out.at[step - 1], t_in.at[step - 1], {"tensor": peer})
        )
        rounds.start(tiny_copies[-1])

    partial[...] = input_rows((1 - core) * own_rows).astype(BF16)
    trade = rounds.copy(partial, partial_in, p_out, p_in, {"tensor": place + 1 - 2 * core})
    rounds.start(trade)
    mine = input_rows(core * own_rows) + residual_ref[...]
    trade.wait_recv()
    tokens_out[...] = (mine + partial_in[...].astype(F32)).astype(BF16)

    total = tiny[place]
    for step in (1, 2, 3):
        tiny_copies[step - 1].wait_recv()
        total = total + tiny_t[step - 1]
    tiny_d[0] = total

    def tell(step, _):
        peer = (group + step) % groups
        rounds.copy(tiny_d.at[0], tiny_d.at[step], d_out.at[step], d_in.at[step], {"dp": peer}).start()
        return 0

    lax.fori_loop(1, groups, tell, 0)

    rounds.x_start(4)
    rounds.z_start(3)
    rounds.h_start(2)
    rounds.x_start(5)
    rounds.z_start(4)
    rounds.g_start(3)
    rounds.x_start(6)
    rounds.z_start(5)
    rounds.g_start(4)
    rounds.h_start(3)
    rounds.x_start(7)
    rounds.z_start(6)
    rounds.g_start(5)
    rounds.h_start(4)
    rounds.x_start(8)
    rounds.z_start(7)
    rounds.g_start(6)
    rounds.h_start(5)
    rounds.z_start(8)
    rounds.g_start(7)
    rounds.h_start(6)
    rounds.g_start(8)
    rounds.h_start(7)
    rounds.h_start(8)

    def hear(step, total):
        copy = rounds.copy(tiny_d.at[0], tiny_d.at[step], d_out.at[step], d_in.at[step], {"dp": group})
        copy.wait_recv()
        copy.wait_send()
        return total + tiny_d[step]

    small_out[...] = lax.fori_loop(1, groups, hear, tiny_d[0])
    for u in range(9):
        rounds.end(u)
    rounds.drain()


IN_VMEM = pl.BlockSpec(memory_space=pltpu.VMEM)


def local_call(kernel, outs, scratch, flops, operands):
    moved = sum(o.size * o.dtype.itemsize for o in operands)
    return pl.pallas_call(
        kernel,
        out_shape=outs,
        in_specs=[IN_VMEM] * len(operands),
        out_specs=[IN_VMEM] * len(outs),
        scratch_shapes=scratch,
        cost_estimate=pl.CostEstimate(flops=flops, bytes_accessed=moved, transcendentals=0),
        compiler_params=pltpu.CompilerParams(vmem_limit_bytes=48 << 20),
    )(*operands)


def rear_call(groups, operands):
    q, k, residual, owned = operands[0], operands[1], operands[10], operands[11]
    rows, both = q.shape
    own_rows, wide = residual.shape
    pairs = both // (2 * HD)
    eighth = wide // 8
    more = groups // 8
    dma = pltpu.SemaphoreType.DMA
    outs = [
        jax.ShapeDtypeStruct(owned.shape, BF16),
        jax.ShapeDtypeStruct(owned.shape, BF16),
        jax.ShapeDtypeStruct((pairs, 8, eighth, 4 * HD), BF16),
        jax.ShapeDtypeStruct((own_rows, wide), BF16),
        jax.ShapeDtypeStruct((3, wide), F32),
    ]
    third = owned.shape[2]
    scratch = [
        pltpu.VMEM((LEN, both), BF16),
        pltpu.VMEM((LEN, both), BF16),
        pltpu.VMEM((rows, both), BF16),
        pltpu.VMEM((rows, both), BF16),
        pltpu.VMEM((rows, both), BF16),
        pltpu.VMEM((2, HALF, both), BF16),
        pltpu.VMEM((2, HALF, both), BF16),
        pltpu.VMEM((pairs, 8, eighth, 4 * HD), BF16),
        pltpu.VMEM((pairs, 8, eighth, 4 * HD), BF16),
        pltpu.VMEM((6, 8, third, wide), BF16),
        pltpu.VMEM((6, 4, third, wide), BF16),
        pltpu.VMEM((6, 3, third, wide), BF16),
        pltpu.VMEM((pairs, 8, eighth, 4 * HD), BF16),
        pltpu.VMEM((pairs, 4, eighth, 4 * HD), BF16),
        pltpu.VMEM((pairs, 3, eighth, 4 * HD), BF16),
        pltpu.VMEM((9, more - 1, eighth, wide) if more > 1 else (1, 1, 16, 128), BF16),
        pltpu.VMEM((own_rows, wide), BF16),
        pltpu.VMEM((own_rows, wide), BF16),
        pltpu.VMEM((4, 3, wide), F32),
        pltpu.VMEM((3, 3, wide), F32),
        pltpu.VMEM((groups, 3, wide), F32),
        dma((9,)),
        dma((9,)),
        dma((9,)),
        dma((9,)),
        dma((9, 3)),
        dma((9, 3)),
        dma((9, 3)),
        dma((9, 3)),
        dma((9,)),
        dma((9,)),
        dma((9, max(more - 1, 1))),
        dma((9, max(more - 1, 1))),
        dma,
        dma,
        dma,
        dma,
        dma((3,)),
        dma((3,)),
        dma((groups,)),
        dma((groups,)),
    ]
    return pl.pallas_call(
        functools.partial(rear_kernel, groups),
        out_shape=outs,
        in_specs=[IN_VMEM] * len(operands),
        out_specs=[IN_VMEM] * len(outs),
        scratch_shapes=scratch,
        compiler_params=pltpu.CompilerParams(
            collective_id=0, has_side_effects=True, vmem_limit_bytes=62 << 20
        ),
    )(*operands)


def interleave(own, other):
    rows, width = own.shape
    heads = width // HD
    both = jnp.stack([own.reshape(rows, heads, HD), other.reshape(rows, heads, HD)], axis=2)
    return both.reshape(rows, 2 * width)


def split_pairs(joined):
    rows, width = joined.shape
    both = joined.reshape(rows, width // (2 * HD), 2, HD)
    return both[:, :, 0].reshape(rows, width // 2), both[:, :, 1].reshape(rows, width // 2)


def mask_bias(segment_ids, lengths, side):
    segments = segment_ids.reshape(-1, LEN)
    ahead = jnp.arange(LEN)
    blocks = []
    for which in range(3):
        index = 3 * side + which if which < 2 else 2
        row = lax.dynamic_index_in_dim(segments, index, 0, keepdims=False)
        length = lax.dynamic_index_in_dim(lengths, index, 0, keepdims=False)
        if which < 2:
            key_places, key_segments, count = ahead, row, LEN
        else:
            key_places = (ahead + side * HALF) % LEN
            key_segments = jnp.where(side == 0, row, jnp.roll(row, -HALF))
            count = HALF
        same = key_segments[:, None] == key_segments[None, :count]
        live = key_places[:, None] < length
        diagonal = key_places[:, None] == key_places[None, :count]
        blocks.append(jnp.where(same & live | diagonal, 0.0, NEGATIVE))
    return jnp.concatenate(blocks, axis=1).astype(F32)


def shards(
    tokens,
    segment_ids,
    lengths,
    w_query,
    b_query,
    w_key,
    w_value,
    b_value,
    w_output,
    b_output,
    first_gain,
    first_shift,
    w_inner,
    b_inner,
    w_outer,
    b_outer,
    second_gain,
    second_shift,
    cotangent,
):
    groups = lax.axis_size("dp")
    place = lax.axis_index("tensor")
    core, side = place % 2, place // 2
    own_rows, wide = tokens.shape
    width = w_query.shape[1]
    units = w_inner.shape[1]
    chip_rows = 2 * own_rows
    c_start = (1 - side) * 2 * LEN

    def to_core(value):
        return lax.ppermute(value, "tensor", [(i, i ^ 1) for i in range(4)])

    def to_side(value):
        return lax.ppermute(value, "tensor", [(i, i ^ 2) for i in range(4)])

    def both_cores(value):
        other = to_core(value)
        return jnp.where(core == 0, jnp.concatenate([value, other]), jnp.concatenate([other, value]))

    def sum_cores(partial):
        theirs = lax.dynamic_slice_in_dim(partial, (1 - core) * own_rows, own_rows, 0)
        mine = lax.dynamic_slice_in_dim(partial, core * own_rows, own_rows, 0)
        return mine + to_core(theirs.astype(BF16)).astype(F32)

    joined_own = jnp.concatenate([w_query, w_key, w_value], axis=1)
    joined_other = to_side(joined_own)
    rows = both_cores(tokens)
    c_rows = to_side(lax.dynamic_slice_in_dim(rows, c_start, HALF, 0))
    bias_own = jnp.concatenate([b_query, b_value, b_inner])
    bias_other = to_side(bias_own)
    w_output_other = to_side(w_output)
    w_inner_other = to_side(w_inner)
    w_outer_other = to_side(w_outer)

    bias = mask_bias(segment_ids, lengths, side)
    b_q = interleave(bias_own[None, :width], bias_other[None, :width])
    b_v = interleave(bias_own[None, width : 2 * width], bias_other[None, width : 2 * width])
    parts = [
        interleave(joined_own[:, i * width : (i + 1) * width], joined_other[:, i * width : (i + 1) * width])
        for i in range(3)
    ]
    extended = jnp.concatenate([rows, c_rows])
    queries = (dg(rows, parts[0]) + b_q).astype(BF16)
    keys = dg(extended, parts[1]).astype(BF16)
    values = (dg(extended, parts[2]) + b_v).astype(BF16)
    both = 2 * width
    pairs_scratch = [pltpu.VMEM((LEN, both), BF16), pltpu.VMEM((LEN, both), BF16)]
    context, lse = local_call(
        attend_forward,
        [jax.ShapeDtypeStruct((chip_rows, both), BF16), jax.ShapeDtypeStruct((8, chip_rows), F32)],
        pairs_scratch,
        4 * chip_rows * LEN * both,
        (queries, keys, values, bias),
    )
    w_out = interleave(w_output.T, w_output_other.T)
    attended = sum_cores(dg(context, w_out, NT))
    first_unit, first_inverse = norm_forward(tokens.astype(F32) + attended + b_output)
    first = (first_unit * first_gain + first_shift).astype(BF16)
    first_rows = both_cores(first)
    w_in = jnp.concatenate([w_inner, w_inner_other], axis=1)
    b_in = jnp.concatenate([bias_own[2 * width :], bias_other[2 * width :]])
    inner = dg(first_rows, w_in) + b_in
    hidden, slope = gelu_and_slope(inner)
    hidden = hidden.astype(BF16)
    slope = slope.astype(BF16)
    w_down = jnp.concatenate([w_outer, w_outer_other], axis=0)
    feed = sum_cores(dg(hidden, w_down))
    second_unit, second_inverse = norm_forward(first.astype(F32) + feed + b_outer)
    output = (second_unit * second_gain + second_shift).astype(BF16)
    upstream = cotangent.astype(F32)
    grad_second = norm_backward(upstream, second_unit, second_inverse, second_gain)
    grad_second_gain = jnp.sum(upstream * second_unit, axis=0)
    grad_second_shift = jnp.sum(upstream, axis=0)
    grad_feed = grad_second.astype(BF16)
    grad_b_outer = jnp.sum(grad_feed.astype(F32), axis=0)
    feed_rows = both_cores(grad_feed)
    grad_w_down = dg(hidden, feed_rows, TN).astype(BF16)
    grad_inner = (dg(feed_rows, w_down, NT) * slope.astype(F32)).astype(BF16)
    grad_b_in = jnp.sum(grad_inner.astype(F32), axis=0)
    grad_w_in = dg(first_rows, grad_inner, TN).astype(BF16)
    grad_first = grad_second + sum_cores(dg(grad_inner, w_in, NT))
    grad_branch = norm_backward(grad_first, first_unit, first_inverse, first_gain)
    grad_first_gain = jnp.sum(grad_first * first_unit, axis=0)
    grad_first_shift = jnp.sum(grad_first, axis=0)
    grad_attended = grad_branch.astype(BF16)
    grad_b_output = jnp.sum(grad_attended.astype(F32), axis=0)
    branch_rows = both_cores(grad_attended)
    grad_context = dg(branch_rows, w_out).astype(BF16)
    weights_joined = jnp.concatenate(parts, axis=1)
    small = jnp.stack(
        [grad_b_output, grad_first_gain, grad_first_shift, grad_b_outer, grad_second_gain, grad_second_shift]
    )
    small = small.reshape(6, 4, width).transpose(1, 0, 2).reshape(4, 6 * width)
    index = jnp.arange(4)[:, None]
    bias_flat = jnp.where(
        index == place, grad_b_in[:units], jnp.where(index == (place + 2) % 4, grad_b_in[units:], 0.0)
    )
    small = jnp.concatenate([small, jnp.zeros((4, 2 * width), F32), bias_flat], axis=1).reshape(4, 3, wide)
    by_owner = (8, 3, wide // 24, wide)
    inner_sum, outer_sum, attention_sum, grad_tokens, total = rear_call(
        groups,
        (
            queries,
            keys,
            values,
            grad_context,
            bias,
            lse,
            rows,
            context,
            branch_rows,
            weights_joined,
            grad_branch,
            grad_w_in[:, :units].reshape(by_owner),
            grad_w_in[:, units:].reshape(by_owner),
            grad_w_down[:units].reshape(by_owner),
            grad_w_down[units:].reshape(by_owner),
            small,
        ),
    )
    attention_sum = attention_sum.reshape(3, wide, 4, HD).transpose(2, 1, 0, 3).reshape(4, wide, width)
    attention_sum = attention_sum.astype(F32)
    total = total.reshape(-1)
    shares = total[: 6 * width].reshape(6, width)
    rest = total[6 * width :]
    return (
        output,
        grad_tokens,
        attention_sum[0],
        rest[:width],
        attention_sum[1],
        attention_sum[2],
        rest[width : 2 * width],
        attention_sum[3].T,
        shares[0],
        shares[1],
        shares[2],
        inner_sum.reshape(wide, units).astype(F32),
        rest[2 * width :],
        outer_sum.reshape(units, wide).astype(F32),
        shares[3],
        shares[4],
        shares[5],
    )


def solution(mesh):
    in_specs = (
        P(("dp", "tensor"), None),
        P("dp"),
        P("dp"),
        P(None, "tensor"),
        P("tensor"),
        P(None, "tensor"),
        P(None, "tensor"),
        P("tensor"),
        P("tensor", None),
        P(),
        P(),
        P(),
        P(None, "tensor"),
        P("tensor"),
        P("tensor", None),
        P(),
        P(),
        P(),
        P(("dp", "tensor"), None),
    )
    out_specs = (
        P(("dp", "tensor"), None),
        P(("dp", "tensor"), None),
        P(None, "tensor"),
        P("tensor"),
        P(None, "tensor"),
        P(None, "tensor"),
        P("tensor"),
        P("tensor", None),
        P("tensor"),
        P("tensor"),
        P("tensor"),
        P(None, "tensor"),
        P("tensor"),
        P("tensor", None),
        P("tensor"),
        P("tensor"),
        P("tensor"),
    )
    return jax.shard_map(shards, mesh=mesh, in_specs=in_specs, out_specs=out_specs, check_vma=False)
```

```python
import functools
import math
import types

import jax
import jax.numpy as jnp
from jax import lax
from jax.experimental import pallas as pl
from jax.experimental.pallas import tpu as pltpu
from jax.sharding import PartitionSpec as P

HD = 64
LEN = 512
HALF = LEN // 2
EPSILON = 1e-12
NEGATIVE = -1000000000.0
SCALE = 1.0 / math.sqrt(HD)
LOG2E = math.log2(math.e)
F32 = jnp.float32
BF16 = jnp.bfloat16
NN = (((1,), (0,)), ((), ()))
NT = (((1,), (1,)), ((), ()))
TN = (((0,), (0,)), ((), ()))
MESH = pl.DeviceIdType.MESH
PARTS = 4
OWNERS = 8
PAIRS = 3
PIECES = 18


def dg(left, right, dims=NN):
    return lax.dot_general(left, right, dims, preferred_element_type=F32)


def normalize(value):
    average = jnp.mean(value, axis=-1, keepdims=True)
    centered = value - average
    variance = jnp.mean(centered * centered, axis=-1, keepdims=True)
    inverse = lax.rsqrt(variance + EPSILON)
    return centered * inverse, inverse


def norm_backward(grad, unit, inverse, gain):
    scaled = grad * gain
    first_mean = jnp.mean(scaled, axis=-1, keepdims=True)
    second_mean = jnp.mean(scaled * unit, axis=-1, keepdims=True)
    return inverse * (scaled - first_mean - unit * second_mean)


def gelu_and_slope(inner):
    cumulative = 0.5 * (1.0 + lax.erf(inner * (1.0 / math.sqrt(2.0))))
    slope = cumulative + inner * jnp.exp(-0.5 * inner * inner) * (1.0 / math.sqrt(2.0 * math.pi))
    return inner * cumulative, slope


def column_sum(value):
    return jnp.sum(value, axis=0, keepdims=True)


def attend_front(q, k, v, bias):
    logits = dg(k, q, NT) * (SCALE * LOG2E) + bias
    peak = jnp.max(logits, axis=0, keepdims=True)
    powers = jnp.exp2(logits - peak)
    total = jnp.sum(powers, axis=0, keepdims=True)
    weights = (powers * (1.0 / total)).astype(BF16)
    return dg(weights, v, TN).astype(BF16), peak + jnp.log2(total)


def attend_back(q, k, v, g, bias, row):
    logits = dg(k, q, NT) * (SCALE * LOG2E) + bias
    probs = jnp.exp2(logits - row)
    dprobs = dg(v, g, NT)
    across = jnp.sum(probs * dprobs, axis=0, keepdims=True)
    dscores = (probs * (dprobs - across) * SCALE).astype(BF16)
    dv = dg(probs.astype(BF16), g, NN).astype(BF16)
    dk = dg(dscores, q, NN).astype(BF16)
    dq = dg(dscores, k, TN).astype(BF16)
    return dq, dk, dv


def pair_back(q, k, v, g, bias, rows):
    done = []
    for h in range(2):
        cols = slice(h * HD, (h + 1) * HD)
        done.append(attend_back(q[:, cols], k[:, cols], v[:, cols], g[:, cols], bias, rows[h]))
    return [jnp.concatenate([done[0][i], done[1][i]], axis=1) for i in range(3)]


def swap_halves(value):
    return jnp.concatenate([value[:, HD:], value[:, :HD]], axis=1)


def pair_lanes(j):
    return pl.ds(pl.multiple_of(j * 2 * HD, 2 * HD), 2 * HD)


def remote(source, target, out, into, device):
    return pltpu.make_async_remote_copy(
        src_ref=source, dst_ref=target, send_sem=out, recv_sem=into, device_id=device, device_id_type=MESH
    )


class Rounds:
    def __init__(self, r, groups):
        self.r = r
        self.place = lax.axis_index("tensor")
        group = lax.axis_index("dp")
        self.x, self.z, self.far = group % 2, (group // 2) % 4, group // OWNERS
        self.more = groups // OWNERS
        self.sent = []

    def dp_at(self, x, z):
        return {"dp": self.far * OWNERS + z * 2 + x}

    def start(self, copy):
        copy.start()
        self.sent.append(copy)
        return copy

    def settle(self, copy):
        copy.wait_send()
        self.sent = [other for other in self.sent if other is not copy]

    def y_copy(self, u):
        r = self.r
        side = {"tensor": (self.place + 2) % 4}
        return remote(r.grads_other.at[u], r.from_side.at[u], r.y_out.at[u], r.y_in.at[u], side)

    def x_copy(self, u):
        r = self.r
        away = r.grads_own.at[u, pl.ds((1 - self.x) * 4, 4)]
        return remote(away, r.from_x.at[u], r.x_out.at[u], r.x_in.at[u], self.dp_at(1 - self.x, self.z))

    def z_copy(self, u, step):
        r = self.r
        there = (self.z + step) % 4
        away = r.grads_own.at[u, self.x * 4 + there]
        out, into = r.z_out.at[u, step - 1], r.z_in.at[u, step - 1]
        return remote(away, r.from_z.at[u, step - 1], out, into, self.dp_at(self.x, there))

    def f_copy(self, u, step):
        r = self.r
        peer = {"dp": ((self.far + step) % self.more) * OWNERS + self.z * 2 + self.x}
        own = r.grads_own.at[u, self.x * 4 + self.z]
        return remote(own, r.from_far.at[u, step - 1], r.f_out.at[u, step - 1], r.f_in.at[u, step - 1], peer)

    def g_copy(self, u, step, origin):
        r = self.r
        piece = r.total.at[u, self.x * 4 + origin]
        out, into = r.g_out.at[u, step - 1], r.g_in.at[u, step - 1]
        return remote(piece, piece, out, into, self.dp_at(self.x, (self.z + step) % 4))

    def h_copy(self, u, half):
        r = self.r
        piece = r.total.at[u, pl.ds(half * 4, 4)]
        return remote(piece, piece, r.h_out.at[u], r.h_in.at[u], self.dp_at(1 - self.x, self.z))

    def y_start(self, u):
        self.y_copy(u).start()

    def x_start(self, u):
        r = self.r
        self.y_copy(u).wait_recv()
        r.grads_own[u] = (r.grads_own[u].astype(F32) + r.from_side[u].astype(F32)).astype(BF16)
        self.x_copy(u).start()

    def z_start(self, u):
        r = self.r
        self.x_copy(u).wait_recv()
        kept = pl.ds(self.x * 4, 4)
        r.grads_own[u, kept] = (r.grads_own[u, kept].astype(F32) + r.from_x[u].astype(F32)).astype(BF16)
        for step in (1, 2, 3):
            self.z_copy(u, step).start()

    def g_start(self, u):
        r = self.r
        own = self.x * 4 + self.z
        value = r.grads_own[u, own].astype(F32)
        for step in (1, 2, 3):
            self.z_copy(u, step).wait_recv()
            value = value + r.from_z[u, step - 1].astype(F32)
        if self.more > 1:
            r.grads_own[u, own] = value.astype(BF16)
            for step in range(1, self.more):
                self.f_copy(u, step).start()
            for step in range(1, self.more):
                self.f_copy(u, step).wait_recv()
                value = value + r.from_far[u, step - 1].astype(F32)
        r.total[u, own] = value.astype(BF16)
        for step in (1, 2, 3):
            self.g_copy(u, step, self.z).start()

    def h_start(self, u):
        for step in (1, 2, 3):
            self.g_copy(u, step, (self.z - step + 4) % 4).wait_recv()
        self.h_copy(u, self.x).start()

    def advance(self, n):
        stages = (self.h_start, self.g_start, self.z_start, self.x_start)
        for behind, stage in zip((3, 2, 1, 0), stages):
            if not isinstance(n, int) or 0 <= n - behind < PIECES:
                stage(n - behind)

    def finish(self):
        def settle(u, _):
            self.h_copy(u, 1 - self.x).wait_recv()
            for copy in (self.y_copy(u), self.x_copy(u), self.h_copy(u, self.x)):
                copy.wait_send()
            for step in (1, 2, 3):
                self.z_copy(u, step).wait_send()
                self.g_copy(u, step, self.z).wait_send()
            for step in range(1, self.more):
                self.f_copy(u, step).wait_send()
            return 0

        lax.fori_loop(0, PIECES, settle, 0)
        for copy in self.sent:
            copy.wait_send()


def layer_kernel(groups, names, *refs):
    r = types.SimpleNamespace(**dict(zip(names, refs)))
    place = lax.axis_index("tensor")
    group = lax.axis_index("dp")
    core, side = place % 2, place // 2
    rows = r.q.shape[0]
    own_rows = rows // 2
    wide = r.x_rows.shape[1]
    both = r.q.shape[1]
    width = both // 2
    units = r.w_inner.shape[1]
    chunk = own_rows // 2
    strip = own_rows // 8
    mine = core * own_rows
    theirs = (1 - core) * own_rows
    c_start = pl.multiple_of((1 - side) * 2 * LEN, HALF)
    core_peer = {"tensor": place + 1 - 2 * core}
    side_peer = {"tensor": (place + 2) % 4}

    barrier = pltpu.get_barrier_semaphore()
    for step in (1, 2, 3):
        pl.semaphore_signal(barrier, inc=1, device_id={"tensor": (place + step) % 4}, device_id_type=MESH)

    def greet(step, _):
        peer = (group + step) % groups
        pl.semaphore_signal(barrier, inc=1, device_id={"dp": peer}, device_id_type=MESH)
        return 0

    lax.fori_loop(1, groups, greet, 0)

    def at_rows(start, count):
        return pl.ds(pl.multiple_of(start, 16), count)

    own_at = at_rows(mine, own_rows)
    loads = {}
    sources = [
        ("tokens", r.tokens, r.x_rows.at[own_at]),
        ("q", r.w_query, r.w_att.at[0, :, 0]),
        ("k", r.w_key, r.w_att.at[1, :, 0]),
        ("v", r.w_value, r.w_att.at[2, :, 0]),
        ("o", r.w_output, r.w_att.at[3, :, 0]),
        ("in", r.w_inner, r.in_own),
        ("down", r.w_outer, r.down_own),
        ("cotangent", r.cotangent, r.grad_tokens),
    ]
    for n, (name, source, target) in enumerate(sources):
        loads[name] = pltpu.make_async_copy(source, target, r.l_sem.at[n])
        loads[name].start()

    pl.semaphore_wait(barrier, 3 + groups - 1)
    rounds = Rounds(r, groups)
    x, z = rounds.x, rounds.z
    x_peer = rounds.dp_at(1 - x, z)

    lanes = wide // 2
    block = units // 8

    def by_heads(source, i):
        def view(ref, half):
            return ref.at[:, :, pl.ds(half * lanes, lanes)]

        return source, r.w_att.at[i, :, 1], view

    def by_rows(source, target, n):
        def view(ref, half):
            return ref.at[at_rows(half * 4 * block + n * 2 * block, 2 * block)]

        return source, target, view

    fetches = [by_heads(w, i) for i, w in enumerate((r.w_query, r.w_key, r.w_value, r.w_output))]
    fetches += [by_rows(r.w_inner, r.in_other, n) for n in range(2)]
    fetches += [by_rows(r.w_outer, r.down_other, n) for n in range(2)]

    def fetch_copy(n):
        source, target, view = fetches[n]
        return remote(view(source, x), view(target, x), r.w_out_sem.at[n], r.w_in_sem.at[n], side_peer)

    def pass_copy(n, which):
        _, target, view = fetches[n]
        return remote(view(target, which), view(target, which), r.p_out_sem.at[n], r.p_in_sem.at[n], x_peer)

    def fetch(*which):
        for n in which:
            rounds.start(fetch_copy(n))

    def hand_on(*which):
        for n in which:
            fetch_copy(n).wait_recv()
            rounds.start(pass_copy(n, x))

    def fetched(*which):
        for n in which:
            pass_copy(n, 1 - x).wait_recv()

    token_copy = rounds.start(remote(r.tokens, r.x_rows.at[own_at], r.s_out.at[0], r.s_in.at[0], core_peer))
    token_wait = remote(r.tokens, r.x_rows.at[at_rows(theirs, own_rows)], r.s_out.at[0], r.s_in.at[0], core_peer)
    fetch(0, 1, 2)
    vector_copy = rounds.start(remote(r.biases, r.biases_other, r.s_out.at[1], r.s_in.at[1], side_peer))

    def project(shard, which, start, count, size):
        shifts = (r.biases, r.biases_other)[shard]
        for i in which:
            target = (r.q, r.k, r.v)[i]
            weights = r.w_att[i, :, shard].reshape(width, wide)

            def body(n, _):
                block = at_rows(start + n * size, size)
                value = dg(r.x_rows[block, :], weights, NT)
                if i == 0:
                    value = value + shifts[0:1, 0:width]
                if i == 2:
                    value = value + shifts[1:2, 0:width]
                value = value.astype(BF16)
                for j in range(PAIRS):
                    lane = (2 * j + shard) * HD
                    target[block, lane : lane + HD] = value[:, j * HD : (j + 1) * HD]
                return 0

            lax.fori_loop(0, count // size, body, 0)

    loads["tokens"].wait()
    for name in ("q", "k", "v"):
        loads[name].wait()
    project(0, (0, 1, 2), mine, own_rows, chunk)

    token_wait.wait_recv()
    quarter = HALF // 2
    far_at = at_rows(rows + core * quarter, quarter)
    far_there = at_rows(rows + (1 - core) * quarter, quarter)
    near_at = at_rows(c_start + core * quarter, quarter)
    far_copy = rounds.start(
        remote(r.x_rows.at[near_at], r.x_rows.at[far_at], r.s_out.at[2], r.s_in.at[2], side_peer)
    )
    fetch(3, 4, 5, 6, 7)
    project(0, (0, 1, 2), theirs, own_rows, chunk)
    hand_on(0)

    def mask_block(at, row, places, length, count):
        column = jnp.transpose(jnp.broadcast_to(row.astype(F32), (128, LEN)))[:, 0:1]
        same = column == row.astype(F32)[:, :count]
        live = places < length
        first = lax.broadcasted_iota(jnp.int32, (LEN, count), 0)
        second = lax.broadcasted_iota(jnp.int32, (LEN, count), 1)
        allowed = same & live | (first == second)
        r.bias[:, at : at + count] = jnp.where(allowed, 0.0, NEGATIVE)

    ahead = lax.broadcasted_iota(jnp.int32, (LEN, 1), 0)
    for which in range(2):
        index = 3 * side + which
        mask_block(which * LEN, r.segments[pl.ds(index, 1), :], ahead, r.lengths[index], LEN)
    near = r.segments[2:3, pl.ds(pl.multiple_of(side * HALF, HALF), HALF)]
    away_row = r.segments[2:3, pl.ds(pl.multiple_of((1 - side) * HALF, HALF), HALF)]
    turned = jnp.where(ahead < HALF, ahead + side * HALF, ahead - side * HALF)
    mask_block(2 * LEN, jnp.concatenate([near, away_row], axis=1), turned, r.lengths[2], HALF)
    hand_on(1)

    def front_store(shard, block, lanes, out):
        if shard == 0:
            r.ctx[block, lanes] = jnp.concatenate([out, jnp.zeros_like(out)], axis=1)
        else:
            r.ctx[block, lanes] = jnp.concatenate([r.ctx[block, lanes][:, :HD], out], axis=1)

    def front_whole(shard, first_pair, last_pair):
        cols = slice(shard * HD, (shard + 1) * HD)

        def body(n, _):
            j, i = n // 2, n % 2
            lanes = pair_lanes(j)
            block = at_rows(side * HALF + i * LEN, LEN)
            at = pl.ds(pl.multiple_of(i * LEN, LEN), LEN)
            out, row = attend_front(
                r.q[block, lanes][:, cols], r.k[block, lanes][:, cols], r.v[block, lanes][:, cols], r.bias[:, at]
            )
            front_store(shard, block, lanes, out)
            r.lse[pl.ds(2 * j + shard, 1), at] = row
            return 0

        lax.fori_loop(2 * first_pair, 2 * last_pair, body, 0)

    def front_half(shard):
        cols = slice(shard * HD, (shard + 1) * HD)

        def body(j, _):
            lanes = pair_lanes(j)
            block = pl.ds(c_start, HALF)
            at = pl.ds(2 * LEN, HALF)
            out, row = attend_front(
                r.q[block, lanes][:, cols], r.kc[:, lanes][:, cols], r.vc[:, lanes][:, cols], r.bias[:, at]
            )
            front_store(shard, block, lanes, out)
            r.lse[pl.ds(2 * j + shard, 1), at] = row
            return 0

        lax.fori_loop(0, PAIRS, body, 0)

    front_whole(0, 0, 1)
    hand_on(2)
    front_whole(0, 1, 3)
    far_copy.wait_recv()
    far_pass = rounds.start(
        remote(r.x_rows.at[far_at], r.x_rows.at[far_at], r.s_out.at[3], r.s_in.at[3], core_peer)
    )
    far_wait = remote(r.x_rows.at[far_there], r.x_rows.at[far_there], r.s_out.at[3], r.s_in.at[3], core_peer)
    vector_copy.wait_recv()
    fetched(0)
    project(1, (0,), 0, rows, chunk)
    fetched(1)
    project(1, (1,), 0, rows, chunk)
    hand_on(3)
    fetched(2)
    project(1, (2,), 0, rows, chunk)
    far_wait.wait_recv()
    for shard in range(2):
        project(shard, (1, 2), rows, HALF, HALF)
    for own, near_far in ((r.k, r.kc), (r.v, r.vc)):
        near_far[pl.ds(0, HALF), :] = own[pl.ds(c_start, HALF), :]
        near_far[pl.ds(HALF, HALF), :] = own[pl.ds(rows, HALF), :]
    front_whole(1, 0, 3)
    front_half(0)
    front_half(1)
    hand_on(4)

    loads["o"].wait()
    fetched(3)

    def pairs_of(i):
        return r.w_att[i].reshape(both, wide)

    def each(start, count, size, body):
        def step(n, _):
            body(at_rows(start + n * size, size), at_rows(n * size, size))
            return 0

        lax.fori_loop(0, count // size, step, 0)

    trades = []

    def trade_rows(compute, keep):
        def away_body(block, local):
            r.partial[local, :] = compute(block).astype(BF16)

        each(theirs, own_rows, chunk, away_body)
        n = len(trades)
        trades.append(
            rounds.start(remote(r.partial, r.partial_in, r.t_out.at[n], r.t_in.at[n], core_peer))
        )

        def own_body(block, local):
            keep(local, compute(block))

        each(mine, own_rows, chunk, own_body)
        trades[n].wait_recv()
        rounds.settle(trades[n])

    def gather_rows(ref, n):
        copy = rounds.start(remote(ref.at[own_at], ref.at[own_at], r.a_out.at[n], r.a_in.at[n], core_peer))
        there = ref.at[at_rows(theirs, own_rows)]
        return copy, remote(there, there, r.a_out.at[n], r.a_in.at[n], core_peer)

    def keep_acc(local, value):
        r.acc[local, :] = value

    trade_rows(lambda block: dg(r.ctx[block, :], pairs_of(3)), keep_acc)
    b_output, first_gain, first_shift = (r.vectors[i : i + 1, :] for i in range(3))
    b_outer, second_gain, second_shift = (r.vectors[i : i + 1, :] for i in range(3, 6))

    def first_norm(block, local):
        value = r.x_rows[block, :].astype(F32) + r.acc[local, :] + r.partial_in[local, :].astype(F32) + b_output
        unit, inverse = normalize(value)
        r.acc[local, :] = unit
        r.inverse[local, :] = inverse
        r.first[block, :] = (unit * first_gain + first_shift).astype(BF16)

    each(mine, own_rows, strip, first_norm)
    first_copy, first_wait = gather_rows(r.first, 0)
    hand_on(5)

    def expand(shard, start):
        weights = (r.in_own, r.in_other)[shard]
        shifts = (r.biases, r.biases_other)[shard]
        hidden, slope = ((r.hidden_own, r.slope_own), (r.hidden_other, r.slope_other))[shard]

        def body(block, _):
            value, gradient = gelu_and_slope(dg(r.first[block, :], weights[...]) + shifts[2:3, :])
            hidden[block, :] = value.astype(BF16)
            slope[block, :] = gradient.astype(BF16)

        each(start, own_rows, chunk, body)

    loads["in"].wait()
    expand(0, mine)
    first_wait.wait_recv()
    expand(0, theirs)
    hand_on(6)
    fetched(4, 5)
    expand(1, theirs)
    expand(1, mine)
    loads["down"].wait()
    hand_on(7)
    fetched(6, 7)

    def keep_second(local, value):
        r.second[local, :] = value

    trade_rows(
        lambda block: dg(r.hidden_own[block, :], r.down_own[...]) + dg(r.hidden_other[block, :], r.down_other[...]),
        keep_second,
    )
    loads["cotangent"].wait()
    zero = jnp.zeros((1, wide), F32)

    def second_norm(n, carry):
        block, local = at_rows(mine + n * strip, strip), at_rows(n * strip, strip)
        value = r.first[block, :].astype(F32) + r.second[local, :] + r.partial_in[local, :].astype(F32) + b_outer
        unit, inverse = normalize(value)
        r.output[local, :] = (unit * second_gain + second_shift).astype(BF16)
        upstream = r.grad_tokens[local, :].astype(F32)
        grad = norm_backward(upstream, unit, inverse, second_gain)
        r.second[local, :] = grad
        low = grad.astype(BF16)
        r.feed[block, :] = low
        gain, shift, lows = carry
        return gain + column_sum(upstream * unit), shift + column_sum(upstream), lows + column_sum(low.astype(F32))

    sum_second_gain, sum_second_shift, sum_b_outer = lax.fori_loop(
        0, own_rows // strip, second_norm, (zero, zero, zero)
    )
    feed_copy, feed_wait = gather_rows(r.feed, 1)

    def contract(shard, start, carry):
        weights = (r.down_own, r.down_other)[shard]
        slope = (r.slope_own, r.slope_other)[shard]

        def body(n, total):
            block = at_rows(start + n * chunk, chunk)
            value = dg(r.feed[block, :], weights[...], NT) * slope[block, :].astype(F32)
            low = value.astype(BF16)
            slope[block, :] = low
            return total + column_sum(low.astype(F32))

        return lax.fori_loop(0, own_rows // chunk, body, carry)

    sum_own = contract(0, mine, jnp.zeros((1, units), F32))
    sum_other = contract(1, mine, jnp.zeros((1, units), F32))
    feed_wait.wait_recv()

    def weight_blocks(target, first_piece, left, right, send):
        columns = left.shape[1] // 3

        def body(u, _):
            value = dg(left[:, pl.ds(pl.multiple_of(u * columns, 128), columns)], right[...], TN).astype(BF16)
            at = first_piece + 2 * u
            target[pl.ds(at, 2)] = value.reshape(2, OWNERS, columns // (2 * OWNERS), value.shape[1])
            if send:
                rounds.y_start(at)
                rounds.y_start(at + 1)
            return 0

        lax.fori_loop(0, 3, body, 0)

    weight_blocks(r.grads_other, 0, r.hidden_other, r.feed, True)
    weight_blocks(r.grads_own, 0, r.hidden_own, r.feed, False)
    sum_own = contract(0, theirs, sum_own)
    sum_other = contract(1, theirs, sum_other)
    rounds.advance(0)

    def keep_first(local, value):
        r.second[local, :] = r.second[local, :] + value

    trade_rows(
        lambda block: dg(r.slope_own[block, :], r.in_own[...], NT) + dg(r.slope_other[block, :], r.in_other[...], NT),
        keep_first,
    )
    rounds.settle(feed_copy)

    def first_back(n, carry):
        block, local = at_rows(mine + n * strip, strip), at_rows(n * strip, strip)
        grad_first = r.second[local, :] + r.partial_in[local, :].astype(F32)
        unit = r.acc[local, :]
        grad = norm_backward(grad_first, unit, r.inverse[local, :], first_gain)
        r.second[local, :] = grad
        low = grad.astype(BF16)
        r.feed[block, :] = low
        gain, shift, lows = carry
        return gain + column_sum(grad_first * unit), shift + column_sum(grad_first), lows + column_sum(low.astype(F32))

    sum_first_gain, sum_first_shift, sum_b_output = lax.fori_loop(0, own_rows // strip, first_back, (zero, zero, zero))
    branch_copy, branch_wait = gather_rows(r.feed, 2)
    weight_blocks(r.grads_other, 6, r.first, r.slope_other, True)
    rounds.advance(1)
    weight_blocks(r.grads_own, 6, r.first, r.slope_own, False)
    rounds.advance(2)
    branch_wait.wait_recv()

    dq = r.hidden_own.at[:, pl.ds(0, both)]
    dk = r.hidden_own.at[:, pl.ds(both, both)]
    dv = r.hidden_other.at[:, pl.ds(0, both)]
    gc = r.hidden_other.at[:, pl.ds(both, both)]

    def context_back(block, _):
        gc[block, :] = dg(r.feed[block, :], pairs_of(3), NT).astype(BF16)

    each(0, rows, chunk, context_back)

    def back_half(j, _):
        lanes = pair_lanes(j)
        at = pl.ds(2 * LEN, HALF)
        stats = [r.lse[pl.ds(j * 2 + h, 1), at] for h in range(2)]
        block = pl.ds(c_start, HALF)
        d_q, d_k, d_v = pair_back(
            r.q[block, lanes], r.kc[:, lanes], r.vc[:, lanes], gc[block, lanes], r.bias[:, at], stats
        )
        dq[block, lanes] = d_q
        dk[block, lanes] = d_k[:HALF]
        dv[block, lanes] = d_v[:HALF]
        r.away[0, :, lanes] = d_k[HALF:]
        r.away[1, :, lanes] = d_v[HALF:]
        return 0

    lax.fori_loop(0, PAIRS, back_half, 0)
    rounds.advance(3)

    grad_out = dg(r.ctx[...], r.feed[...], TN).astype(BF16)
    for j in range(PAIRS):
        for shard, target in ((0, r.grads_own), (1, r.grads_other)):
            lane = (2 * j + shard) * HD
            target[12 + 2 * j + 1, 4:] = grad_out[lane : lane + HD].reshape(4, HD // 4, wide)

    def back_whole(j):
        def body(i, _):
            lanes = pair_lanes(j)
            block = at_rows(side * HALF + i * LEN, LEN)
            at = pl.ds(pl.multiple_of(i * LEN, LEN), LEN)
            stats = [r.lse[pl.ds(j * 2 + h, 1), at] for h in range(2)]
            d_q, d_k, d_v = pair_back(
                r.q[block, lanes], r.k[block, lanes], r.v[block, lanes], gc[block, lanes], r.bias[:, at], stats
            )
            dq[block, lanes] = d_q
            dk[block, lanes] = d_k
            dv[block, lanes] = d_v
            return 0

        lax.fori_loop(0, 2, body, 0)

    def weight_pair(j):
        lanes = pair_lanes(j)
        left = jnp.concatenate([dq[:, lanes], dk[:, lanes], dv[:, lanes]], axis=1)
        value = dg(left, r.x_rows[pl.ds(0, rows), :], TN)
        far_left = jnp.concatenate([r.away[0, :, lanes], r.away[1, :, lanes]], axis=1)
        far = dg(far_left, r.x_rows[pl.ds(rows, HALF), :], TN)
        first = value[: 2 * HD].astype(BF16)
        rest = (value[2 * HD :] + far).astype(BF16)
        at = 12 + 2 * j
        for shard, target in ((0, r.grads_own), (1, r.grads_other)):
            cut = slice(shard * HD, (shard + 1) * HD)
            pieces = [v[cut].reshape(4, HD // 4, wide) for v in (first, rest[: 2 * HD], rest[2 * HD :])]
            target[at, 0:4] = pieces[0]
            target[at, 4:8] = pieces[1]
            target[at + 1, 0:4] = pieces[2]
        rounds.y_start(at)
        rounds.y_start(at + 1)

    def back_pair(j, _):
        back_whole(j)
        weight_pair(j)
        rounds.advance(4 + j)
        return 0

    lax.fori_loop(0, PAIRS, back_pair, 0)

    def bias_sum(*grads):
        total = sum(column_sum(part) for part in grads)
        heads = [total[:, i * HD : (i + 1) * HD] for i in range(2 * PAIRS)]
        return jnp.concatenate(heads[0::2], axis=1), jnp.concatenate(heads[1::2], axis=1)

    sums = (sum_b_output, sum_first_gain, sum_first_shift, sum_b_outer, sum_second_gain, sum_second_shift)
    for t in range(PARTS):
        shares = [value[:, t * width : (t + 1) * width] for value in sums]
        r.tiny[t, 0:1, :] = jnp.concatenate(shares[:4], axis=1)
        r.tiny[t, 1:2, :] = jnp.concatenate(shares[4:] + [jnp.zeros((1, 2 * width), F32)], axis=1)
        r.tiny[t, 2:3, :] = jnp.zeros((1, units), F32)
    queries, values = bias_sum(dq[...].astype(F32)), bias_sum(dv[...].astype(F32), r.away[1].astype(F32))
    for target, n, inner in ((place, 0, sum_own), ((place + 2) % 4, 1, sum_other)):
        r.tiny[target, 1:2, 2 * width :] = jnp.concatenate([queries[n], values[n]], axis=1)
        r.tiny[target, 2:3, :] = inner
    tiny_copies = []
    for step in (1, 2, 3):
        peer = (place + step) % 4
        out, into = r.i_out.at[step - 1], r.i_in.at[step - 1]
        tiny_copies.append(rounds.start(remote(r.tiny.at[peer], r.tiny_side.at[step - 1], out, into, {"tensor": peer})))

    def input_rows(block):
        value = dg(dq[block, :], pairs_of(0))
        value = value + dg(dk[block, :], pairs_of(1))
        return value + dg(dv[block, :], pairs_of(2))

    r.far_part[...] = (dg(r.away[0], pairs_of(1)) + dg(r.away[1], pairs_of(2))).astype(BF16)
    give = at_rows((1 - core) * quarter, quarter)
    keep = at_rows(core * quarter, quarter)
    far_trade = rounds.start(
        remote(r.far_part.at[give], r.far_half, r.s_out.at[4], r.s_in.at[4], core_peer)
    )
    far_trade.wait_recv()
    r.far_send[...] = (r.far_part[keep, :].astype(F32) + r.far_half[...].astype(F32)).astype(BF16)
    owner = {"tensor": (1 - side) * 2 + side}
    rounds.start(remote(r.far_send, r.far_in.at[core], r.o_out, r.o_in.at[core], owner))

    trade_rows(input_rows, keep_first)

    for n in (7, 8, 9, 10):
        rounds.advance(n)

    @pl.when(core == 1 - side)
    def _():
        start = (1 - side) * (own_rows - HALF)
        for n in range(2):
            remote(r.far_send, r.far_in.at[n], r.o_out, r.o_in.at[n], owner).wait_recv()
            block = at_rows(start + n * quarter, quarter)
            r.second[block, :] = r.second[block, :] + r.far_in[n].astype(F32)

    def finish(block, local):
        r.grad_tokens[local, :] = (r.second[local, :] + r.partial_in[local, :].astype(F32)).astype(BF16)

    each(mine, own_rows, strip, finish)

    total = r.tiny[place]
    for step in (1, 2, 3):
        tiny_copies[step - 1].wait_recv()
        total = total + r.tiny_side[step - 1]
    r.tiny_all[0] = total

    def tell(step, _):
        peer = {"dp": (group + step) % groups}
        remote(r.tiny_all.at[0], r.tiny_all.at[step], r.d_out.at[step], r.d_in.at[step], peer).start()
        return 0

    lax.fori_loop(1, groups, tell, 0)
    def hear(step, total):
        peer = {"dp": (group + step) % groups}
        copy = remote(r.tiny_all.at[0], r.tiny_all.at[step], r.d_out.at[step], r.d_in.at[step], peer)
        copy.wait()
        return total + r.tiny_all[step]

    r.small[...] = lax.fori_loop(1, groups, hear, r.tiny_all[0])

    def pump(n, _):
        rounds.advance(n)
        return 0

    lax.fori_loop(11, PIECES, pump, 0)
    for n in range(PIECES, PIECES + 3):
        rounds.advance(n)
    rounds.finish()


def layer(groups, named):
    dma = pltpu.SemaphoreType.DMA
    own_rows, wide = named["tokens"].shape
    units = named["w_inner"].shape[1]
    heads = named["w_query"].shape
    rows, both = 2 * own_rows, 2 * heads[0] * heads[1]
    more = groups // OWNERS
    share = wide // 6 // OWNERS
    outs = {
        "output": ((own_rows, wide), BF16),
        "grad_tokens": ((own_rows, wide), BF16),
        "total": ((PIECES, OWNERS, share, wide), BF16),
        "small": ((3, wide), F32),
    }
    room = {
        "x_rows": ((rows + HALF, wide), BF16),
        "w_att": ((4, PAIRS, 2, HD, wide), BF16),
        "in_own": ((wide, units), BF16),
        "in_other": ((wide, units), BF16),
        "down_own": ((units, wide), BF16),
        "down_other": ((units, wide), BF16),
        "biases_other": ((8, wide), F32),
        "bias": ((LEN, rows), F32),
        "q": ((rows, both), BF16),
        "k": ((rows + HALF, both), BF16),
        "v": ((rows + HALF, both), BF16),
        "kc": ((LEN, both), BF16),
        "vc": ((LEN, both), BF16),
        "ctx": ((rows, both), BF16),
        "lse": ((8, rows), F32),
        "partial": ((own_rows, wide), BF16),
        "partial_in": ((own_rows, wide), BF16),
        "acc": ((own_rows, wide), F32),
        "inverse": ((own_rows, 1), F32),
        "first": ((rows, wide), BF16),
        "hidden_own": ((rows, units), BF16),
        "hidden_other": ((rows, units), BF16),
        "slope_own": ((rows, units), BF16),
        "slope_other": ((rows, units), BF16),
        "second": ((own_rows, wide), F32),
        "feed": ((rows, wide), BF16),
        "away": ((2, HALF, both), BF16),
        "far_part": ((HALF, wide), BF16),
        "far_half": ((HALF // 2, wide), BF16),
        "far_send": ((HALF // 2, wide), BF16),
        "far_in": ((2, HALF // 2, wide), BF16),
        "grads_own": ((PIECES, OWNERS, share, wide), BF16),
        "grads_other": ((PIECES, OWNERS, share, wide), BF16),
        "from_side": ((PIECES, OWNERS, share, wide), BF16),
        "from_x": ((PIECES, 4, share, wide), BF16),
        "from_z": ((PIECES, 3, share, wide), BF16),
        "from_far": ((PIECES, more - 1, share, wide) if more > 1 else (1, 1, 16, 128), BF16),
        "tiny": ((PARTS, 3, wide), F32),
        "tiny_side": ((3, 3, wide), F32),
        "tiny_all": ((groups, 3, wide), F32),
    }
    sems = {
        "l_sem": (8,),
        "s_out": (5,),
        "s_in": (5,),
        "w_out_sem": (8,),
        "w_in_sem": (8,),
        "p_out_sem": (8,),
        "p_in_sem": (8,),
        "t_out": (4,),
        "t_in": (4,),
        "a_out": (3,),
        "a_in": (3,),
        "y_out": (PIECES,),
        "y_in": (PIECES,),
        "x_out": (PIECES,),
        "x_in": (PIECES,),
        "z_out": (PIECES, 3),
        "z_in": (PIECES, 3),
        "g_out": (PIECES, 3),
        "g_in": (PIECES, 3),
        "h_out": (PIECES,),
        "h_in": (PIECES,),
        "f_out": (PIECES, max(more - 1, 1)),
        "f_in": (PIECES, max(more - 1, 1)),
        "i_out": (3,),
        "i_in": (3,),
        "d_out": (groups,),
        "d_in": (groups,),
        "o_out": (),
        "o_in": (2,),
    }
    names = list(named) + list(outs) + list(room) + list(sems)
    in_vmem = pl.BlockSpec(memory_space=pltpu.VMEM)
    spaces = {"lengths": pltpu.SMEM, "vectors": pltpu.VMEM, "biases": pltpu.VMEM, "segments": pltpu.VMEM}
    results = pl.pallas_call(
        functools.partial(layer_kernel, groups, names),
        out_shape=[jax.ShapeDtypeStruct(*spec) for spec in outs.values()],
        in_specs=[pl.BlockSpec(memory_space=spaces.get(name, pl.ANY)) for name in named],
        out_specs=[in_vmem] * len(outs),
        scratch_shapes=[pltpu.VMEM(*spec) for spec in room.values()] + [dma(shape) for shape in sems.values()],
        compiler_params=pltpu.CompilerParams(
            collective_id=0, has_side_effects=True, vmem_limit_bytes=67043328
        ),
    )(*named.values())
    return dict(zip(outs, results))


def shards(
    tokens,
    segment_ids,
    lengths,
    w_query,
    b_query,
    w_key,
    w_value,
    b_value,
    w_output,
    b_output,
    first_gain,
    first_shift,
    w_inner,
    b_inner,
    w_outer,
    b_outer,
    second_gain,
    second_shift,
    cotangent,
):
    groups = lax.axis_size("dp")
    wide, width = w_query.shape
    units = w_inner.shape[1]
    by_head = (width // HD, HD, wide)
    spare = jnp.zeros((wide - width,), F32)
    rest = jnp.zeros((wide,), F32)
    vectors = jnp.stack([b_output, first_gain, first_shift, b_outer, second_gain, second_shift, rest, rest])
    biases = jnp.stack(
        [jnp.concatenate([b_query, spare]), jnp.concatenate([b_value, spare]), b_inner, rest, rest, rest, rest, rest]
    )
    done = layer(
        groups,
        {
            "tokens": tokens,
            "w_query": w_query.T.reshape(by_head),
            "w_key": w_key.T.reshape(by_head),
            "w_value": w_value.T.reshape(by_head),
            "w_output": w_output.reshape(by_head),
            "w_inner": w_inner,
            "w_outer": w_outer,
            "cotangent": cotangent,
            "vectors": vectors,
            "biases": biases,
            "segments": segment_ids.reshape(-1, LEN),
            "lengths": lengths,
        },
    )
    sums = done["total"]
    attention = sums[12:].reshape(PAIRS, 4, HD, wide)
    query, key, value, out = (attention[:, i].reshape(width, wide).astype(F32) for i in range(4))
    total = done["small"].reshape(-1)
    shares = total[: 6 * width].reshape(6, width)
    rest = total[6 * width :]
    return (
        done["output"],
        done["grad_tokens"],
        query.T,
        rest[:width],
        key.T,
        value.T,
        rest[width : 2 * width],
        out,
        shares[0],
        shares[1],
        shares[2],
        sums[6:12].reshape(wide, units).astype(F32),
        rest[2 * width :],
        sums[:6].reshape(units, wide).astype(F32),
        shares[3],
        shares[4],
        shares[5],
    )


def solution(mesh):
    in_specs = (
        P(("dp", "tensor"), None),
        P("dp"),
        P("dp"),
        P(None, "tensor"),
        P("tensor"),
        P(None, "tensor"),
        P(None, "tensor"),
        P("tensor"),
        P("tensor", None),
        P(),
        P(),
        P(),
        P(None, "tensor"),
        P("tensor"),
        P("tensor", None),
        P(),
        P(),
        P(),
        P(("dp", "tensor"), None),
    )
    out_specs = (
        P(("dp", "tensor"), None),
        P(("dp", "tensor"), None),
        P(None, "tensor"),
        P("tensor"),
        P(None, "tensor"),
        P(None, "tensor"),
        P("tensor"),
        P("tensor", None),
        P("tensor"),
        P("tensor"),
        P("tensor"),
        P(None, "tensor"),
        P("tensor"),
        P("tensor", None),
        P("tensor"),
        P("tensor"),
        P("tensor"),
    )
    return jax.shard_map(shards, mesh=mesh, in_specs=in_specs, out_specs=out_specs, check_vma=False)
```

```python
import functools
import math
import types

import jax
import jax.numpy as jnp
from jax import lax
from jax.experimental import pallas as pl
from jax.experimental.pallas import tpu as pltpu
from jax.sharding import PartitionSpec as P

HD = 64
LEN = 512
HALF = LEN // 2
EPSILON = 1e-12
NEGATIVE = -1000000000.0
SCALE = 1.0 / math.sqrt(HD)
LOG2E = math.log2(math.e)
F32 = jnp.float32
BF16 = jnp.bfloat16
NN = (((1,), (0,)), ((), ()))
NT = (((1,), (1,)), ((), ()))
TN = (((0,), (0,)), ((), ()))
MESH = pl.DeviceIdType.MESH
PARTS = 4
OWNERS = 8
PAIRS = 3
PIECES = 18
LAGS = (6, 4, 2, 0)


def dg(left, right, dims=NN):
    return lax.dot_general(left, right, dims, preferred_element_type=F32)


def normalize(value):
    average = jnp.mean(value, axis=-1, keepdims=True)
    centered = value - average
    variance = jnp.mean(centered * centered, axis=-1, keepdims=True)
    inverse = lax.rsqrt(variance + EPSILON)
    return centered * inverse, inverse


def norm_backward(grad, unit, inverse, gain):
    scaled = grad * gain
    first_mean = jnp.mean(scaled, axis=-1, keepdims=True)
    second_mean = jnp.mean(scaled * unit, axis=-1, keepdims=True)
    return inverse * (scaled - first_mean - unit * second_mean)


def gelu_and_slope(inner):
    cumulative = 0.5 * (1.0 + lax.erf(inner * (1.0 / math.sqrt(2.0))))
    slope = cumulative + inner * jnp.exp(-0.5 * inner * inner) * (1.0 / math.sqrt(2.0 * math.pi))
    return inner * cumulative, slope


def column_sum(value):
    return jnp.sum(value, axis=0, keepdims=True)


def attend_front(q, k, v, bias):
    logits = dg(k, q, NT) * (SCALE * LOG2E) + bias
    peak = jnp.max(logits, axis=0, keepdims=True)
    powers = jnp.exp2(logits - peak)
    total = jnp.sum(powers, axis=0, keepdims=True)
    weights = (powers * (1.0 / total)).astype(BF16)
    return dg(weights, v, TN).astype(BF16), peak + jnp.log2(total)


def attend_back(q, k, v, g, bias, row):
    logits = dg(k, q, NT) * (SCALE * LOG2E) + bias
    probs = jnp.exp2(logits - row)
    dprobs = dg(v, g, NT)
    across = jnp.sum(probs * dprobs, axis=0, keepdims=True)
    dscores = (probs * (dprobs - across) * SCALE).astype(BF16)
    dv = dg(probs.astype(BF16), g, NN).astype(BF16)
    dk = dg(dscores, q, NN).astype(BF16)
    dq = dg(dscores, k, TN).astype(BF16)
    return dq, dk, dv


def pair_back(q, k, v, g, bias, rows):
    done = []
    for h in range(2):
        cols = slice(h * HD, (h + 1) * HD)
        done.append(attend_back(q[:, cols], k[:, cols], v[:, cols], g[:, cols], bias, rows[h]))
    return [jnp.concatenate([done[0][i], done[1][i]], axis=1) for i in range(3)]


def swap_halves(value):
    return jnp.concatenate([value[:, HD:], value[:, :HD]], axis=1)


def pair_lanes(j):
    return pl.ds(pl.multiple_of(j * 2 * HD, 2 * HD), 2 * HD)


def remote(source, target, out, into, device):
    return pltpu.make_async_remote_copy(
        src_ref=source, dst_ref=target, send_sem=out, recv_sem=into, device_id=device, device_id_type=MESH
    )


class Rounds:
    def __init__(self, r, groups):
        self.r = r
        self.place = lax.axis_index("tensor")
        group = lax.axis_index("dp")
        self.x, self.z, self.far = group % 2, (group // 2) % 4, group // OWNERS
        self.more = groups // OWNERS
        self.sent = []

    def dp_at(self, x, z):
        return {"dp": self.far * OWNERS + z * 2 + x}

    def start(self, copy):
        copy.start()
        self.sent.append(copy)
        return copy

    def settle(self, copy):
        copy.wait_send()
        self.sent = [other for other in self.sent if other is not copy]

    @staticmethod
    def where(u):
        if isinstance(u, int):
            return 2 * (u // 6) + u % 2, u % 6 // 2
        return 2 * lax.div(u, 6) + lax.rem(u, 2), lax.div(lax.rem(u, 6), 2)

    def y_copy(self, u):
        r = self.r
        b, j = self.where(u)
        side = {"tensor": (self.place + 2) % 4}
        both = pl.ds(0, 2)
        return remote(r.grads_other.at[b, both, j], r.from_side.at[b, both, j], r.y_out.at[u], r.y_in.at[u], side)

    def x_copy(self, u):
        r = self.r
        b, j = self.where(u)
        away = r.grads_own.at[b, 1 - self.x, j]
        return remote(away, r.from_x.at[b, j], r.x_out.at[u], r.x_in.at[u], self.dp_at(1 - self.x, self.z))

    def z_copy(self, u, step):
        r = self.r
        b, j = self.where(u)
        there = (self.z + step) % 4
        away = r.grads_own.at[b, self.x, j, there]
        out, into = r.z_out.at[u, step - 1], r.z_in.at[u, step - 1]
        return remote(away, r.from_z.at[b, j, step - 1], out, into, self.dp_at(self.x, there))

    def f_copy(self, u, step):
        r = self.r
        b, j = self.where(u)
        peer = {"dp": ((self.far + step) % self.more) * OWNERS + self.z * 2 + self.x}
        own = r.grads_own.at[b, self.x, j, self.z]
        return remote(own, r.from_far.at[u, step - 1], r.f_out.at[u, step - 1], r.f_in.at[u, step - 1], peer)

    def g_copy(self, u, step, origin):
        r = self.r
        b, j = self.where(u)
        piece = r.total.at[b, self.x, j, origin]
        out, into = r.g_out.at[u, step - 1], r.g_in.at[u, step - 1]
        return remote(piece, piece, out, into, self.dp_at(self.x, (self.z + step) % 4))

    def h_copy(self, u, half):
        r = self.r
        b, j = self.where(u)
        piece = r.total.at[b, half, j]
        return remote(piece, piece, r.h_out.at[u], r.h_in.at[u], self.dp_at(1 - self.x, self.z))

    def y_start(self, u):
        self.y_copy(u).start()

    def x_start(self, u):
        r = self.r
        b, j = self.where(u)
        self.y_copy(u).wait_recv()
        for half in range(2):
            summed = r.grads_own[b, half, j].astype(F32) + r.from_side[b, half, j].astype(F32)
            r.grads_own[b, half, j] = summed.astype(BF16)
        self.x_copy(u).start()

    def z_start(self, u):
        r = self.r
        b, j = self.where(u)
        self.x_copy(u).wait_recv()
        summed = r.grads_own[b, self.x, j].astype(F32) + r.from_x[b, j].astype(F32)
        r.grads_own[b, self.x, j] = summed.astype(BF16)
        for step in (1, 2, 3):
            self.z_copy(u, step).start()

    def g_start(self, u):
        r = self.r
        b, j = self.where(u)
        value = r.grads_own[b, self.x, j, self.z].astype(F32)
        for step in (1, 2, 3):
            self.z_copy(u, step).wait_recv()
            value = value + r.from_z[b, j, step - 1].astype(F32)
        if self.more > 1:
            r.grads_own[b, self.x, j, self.z] = value.astype(BF16)
            for step in range(1, self.more):
                self.f_copy(u, step).start()
            for step in range(1, self.more):
                self.f_copy(u, step).wait_recv()
                value = value + r.from_far[u, step - 1].astype(F32)
        r.total[b, self.x, j, self.z] = value.astype(BF16)
        for step in (1, 2, 3):
            self.g_copy(u, step, self.z).start()

    def h_start(self, u):
        for step in (1, 2, 3):
            self.g_copy(u, step, (self.z - step + 4) % 4).wait_recv()
        self.h_copy(u, self.x).start()

    def advance(self, n, least=0):
        stages = (self.h_start, self.g_start, self.z_start, self.x_start)
        for behind, stage in zip(LAGS, stages):
            if isinstance(n, int):
                if 0 <= n - behind < PIECES:
                    stage(n - behind)
            elif least >= behind:
                stage(n - behind)
            else:
                pl.when(n >= behind)(functools.partial(stage, n - behind))

    def finish(self):
        def settle(u, _):
            self.h_copy(u, 1 - self.x).wait_recv()
            for copy in (self.y_copy(u), self.x_copy(u), self.h_copy(u, self.x)):
                copy.wait_send()
            for step in (1, 2, 3):
                self.z_copy(u, step).wait_send()
                self.g_copy(u, step, self.z).wait_send()
            for step in range(1, self.more):
                self.f_copy(u, step).wait_send()
            return 0

        lax.fori_loop(0, PIECES, settle, 0)
        for copy in self.sent:
            copy.wait_send()


def layer_kernel(groups, names, *refs):
    r = types.SimpleNamespace(**dict(zip(names, refs)))
    place = lax.axis_index("tensor")
    group = lax.axis_index("dp")
    core, side = place % 2, place // 2
    rows = r.q.shape[0]
    own_rows = rows // 2
    wide = r.x_rows.shape[1]
    both = r.q.shape[1]
    width = both // 2
    units = r.w_inner.shape[1]
    chunk = own_rows // 2
    strip = own_rows // 8
    mine = core * own_rows
    theirs = (1 - core) * own_rows
    c_start = pl.multiple_of((1 - side) * 2 * LEN, HALF)
    core_peer = {"tensor": place + 1 - 2 * core}
    side_peer = {"tensor": (place + 2) % 4}

    barrier = pltpu.get_barrier_semaphore()
    for step in (1, 2, 3):
        pl.semaphore_signal(barrier, inc=1, device_id={"tensor": (place + step) % 4}, device_id_type=MESH)

    def greet(step, _):
        peer = (group + step) % groups
        pl.semaphore_signal(barrier, inc=1, device_id={"dp": peer}, device_id_type=MESH)
        return 0

    lax.fori_loop(1, groups, greet, 0)

    def at_rows(start, count):
        return pl.ds(pl.multiple_of(start, 16), count)

    own_at = at_rows(mine, own_rows)
    loads = {}
    sources = [
        ("tokens", r.tokens, r.x_rows.at[own_at]),
        ("q", r.w_query, r.w_att.at[0, :, 0]),
        ("k", r.w_key, r.w_att.at[1, :, 0]),
        ("v", r.w_value, r.w_att.at[2, :, 0]),
        ("o", r.w_output, r.w_att.at[3, :, 0]),
        ("in", r.w_inner, r.in_own),
        ("down", r.w_outer, r.down_own),
        ("cotangent", r.cotangent, r.grad_tokens),
    ]
    sources += [("shift", r.b_query, r.narrow.at[0]), ("shift", r.b_value, r.narrow.at[1])]
    sources += [("shift", r.b_inner, r.biases.at[0])]
    gains = (r.b_output, r.first_gain, r.first_shift, r.b_outer, r.second_gain, r.second_shift)
    sources += [("gain", ref, r.vectors.at[i]) for i, ref in enumerate(gains)]
    sources += [("segment", r.segment_ids.at[pl.ds(i * LEN, LEN)], r.segments.at[i]) for i in range(5)]
    for n, (name, source, target) in enumerate(sources):
        copy = pltpu.make_async_copy(source, target, r.l_sem.at[n])
        copy.start()
        loads.setdefault(name, []).append(copy)

    def loaded(*wanted):
        for name in wanted:
            for copy in loads[name]:
                copy.wait()

    pl.semaphore_wait(barrier, 3 + groups - 1)
    rounds = Rounds(r, groups)
    x, z = rounds.x, rounds.z
    x_peer = rounds.dp_at(1 - x, z)

    lanes = wide // 2
    block = units // 8

    def by_heads(source, i):
        def view(ref, half):
            return ref.at[:, :, pl.ds(half * lanes, lanes)]

        return source, r.w_att.at[i, :, 1], view

    def by_rows(source, target, n):
        def view(ref, half):
            return ref.at[at_rows((half * 4 + n) * block, block)]

        return source, target, view

    fetches = [by_heads(w, i) for i, w in enumerate((r.w_query, r.w_key, r.w_value, r.w_output))]
    fetches += [by_rows(r.w_inner, r.in_other, n) for n in range(4)]
    fetches += [by_rows(r.w_outer, r.down_other, n) for n in range(4)]

    def fetch_copy(n):
        source, target, view = fetches[n]
        return remote(view(source, x), view(target, x), r.w_out_sem.at[n], r.w_in_sem.at[n], side_peer)

    def pass_copy(n, which):
        _, target, view = fetches[n]
        return remote(view(target, which), view(target, which), r.p_out_sem.at[n], r.p_in_sem.at[n], x_peer)

    def fetch(*which):
        for n in which:
            rounds.start(fetch_copy(n))

    def hand_on(*which):
        for n in which:
            fetch_copy(n).wait_recv()
            rounds.start(pass_copy(n, x))

    def fetched(*which):
        for n in which:
            pass_copy(n, 1 - x).wait_recv()

    token_copy = rounds.start(remote(r.tokens, r.x_rows.at[own_at], r.s_out.at[0], r.s_in.at[0], core_peer))
    token_wait = remote(r.tokens, r.x_rows.at[at_rows(theirs, own_rows)], r.s_out.at[0], r.s_in.at[0], core_peer)
    fetch(0, 1, 2)
    loaded("shift")
    vector_copies = [
        rounds.start(remote(r.biases, r.biases_other, r.s_out.at[1], r.s_in.at[1], side_peer)),
        rounds.start(remote(r.narrow, r.narrow_other, r.s_out.at[5], r.s_in.at[5], side_peer)),
    ]

    def project(shard, which, start, count, size):
        shifts = (r.narrow, r.narrow_other)[shard]
        for i in which:
            target = (r.q, r.k, r.v)[i]
            weights = r.w_att[i, :, shard].reshape(width, wide)

            def body(n, _):
                block = at_rows(start + n * size, size)
                value = dg(r.x_rows[block, :], weights, NT)
                if i == 0:
                    value = value + shifts[0:1, :]
                if i == 2:
                    value = value + shifts[1:2, :]
                value = value.astype(BF16)
                for j in range(PAIRS):
                    lane = (2 * j + shard) * HD
                    target[block, lane : lane + HD] = value[:, j * HD : (j + 1) * HD]
                return 0

            lax.fori_loop(0, count // size, body, 0)

    loaded("tokens")
    loaded("q", "k", "v")
    project(0, (0, 1, 2), mine, own_rows, chunk)

    token_wait.wait_recv()
    quarter = HALF // 2
    far_at = at_rows(rows + core * quarter, quarter)
    far_there = at_rows(rows + (1 - core) * quarter, quarter)
    near_at = at_rows(c_start + core * quarter, quarter)
    far_copy = rounds.start(
        remote(r.x_rows.at[near_at], r.x_rows.at[far_at], r.s_out.at[2], r.s_in.at[2], side_peer)
    )
    fetch(*range(3, 12))
    project(0, (0, 1, 2), theirs, own_rows, chunk)
    hand_on(0)

    loaded("segment")

    def mask_block(at, row, places, length, count):
        column = jnp.transpose(jnp.broadcast_to(row.astype(F32), (128, LEN)))[:, 0:1]
        same = column == row.astype(F32)[:, :count]
        live = places < length
        first = lax.broadcasted_iota(jnp.int32, (LEN, count), 0)
        second = lax.broadcasted_iota(jnp.int32, (LEN, count), 1)
        allowed = same & live | (first == second)
        r.bias[:, at : at + count] = jnp.where(allowed, 0.0, NEGATIVE)

    ahead = lax.broadcasted_iota(jnp.int32, (LEN, 1), 0)
    for which in range(2):
        index = 3 * side + which
        mask_block(which * LEN, r.segments[pl.ds(index, 1), :], ahead, r.lengths[index], LEN)
    near = r.segments[2:3, pl.ds(pl.multiple_of(side * HALF, HALF), HALF)]
    away_row = r.segments[2:3, pl.ds(pl.multiple_of((1 - side) * HALF, HALF), HALF)]
    turned = jnp.where(ahead < HALF, ahead + side * HALF, ahead - side * HALF)
    mask_block(2 * LEN, jnp.concatenate([near, away_row], axis=1), turned, r.lengths[2], HALF)
    hand_on(1)

    def front_store(shard, block, lanes, out):
        if shard == 0:
            r.ctx[block, lanes] = jnp.concatenate([out, jnp.zeros_like(out)], axis=1)
        else:
            r.ctx[block, lanes] = jnp.concatenate([r.ctx[block, lanes][:, :HD], out], axis=1)

    def front_whole(shard, first_pair, last_pair):
        cols = slice(shard * HD, (shard + 1) * HD)

        def body(j, _):
            lanes = pair_lanes(j)
            for i in range(2):
                block = at_rows(side * HALF + i * LEN, LEN)
                at = pl.ds(i * LEN, LEN)
                out, row = attend_front(
                    r.q[block, lanes][:, cols], r.k[block, lanes][:, cols], r.v[block, lanes][:, cols], r.bias[:, at]
                )
                front_store(shard, block, lanes, out)
                r.lse[pl.ds(2 * j + shard, 1), at] = row
            return 0

        lax.fori_loop(first_pair, last_pair, body, 0)

    def front_half():
        def body(j, _):
            lanes = pair_lanes(j)
            block = pl.ds(c_start, HALF)
            at = pl.ds(2 * LEN, HALF)
            q, k, v = r.q[block, lanes], r.kc[:, lanes], r.vc[:, lanes]
            outs = []
            for shard in range(2):
                cols = slice(shard * HD, (shard + 1) * HD)
                out, row = attend_front(q[:, cols], k[:, cols], v[:, cols], r.bias[:, at])
                outs.append(out)
                r.lse[pl.ds(2 * j + shard, 1), at] = row
            r.ctx[block, lanes] = jnp.concatenate(outs, axis=1)
            return 0

        lax.fori_loop(0, PAIRS, body, 0)

    front_whole(0, 0, 2)
    hand_on(2)
    front_whole(0, 2, 3)
    far_copy.wait_recv()
    far_pass = rounds.start(
        remote(r.x_rows.at[far_at], r.x_rows.at[far_at], r.s_out.at[3], r.s_in.at[3], core_peer)
    )
    far_wait = remote(r.x_rows.at[far_there], r.x_rows.at[far_there], r.s_out.at[3], r.s_in.at[3], core_peer)
    for copy in vector_copies:
        copy.wait_recv()
    fetched(0)
    project(1, (0,), 0, rows, chunk)
    fetched(1)
    project(1, (1,), 0, rows, chunk)
    hand_on(3)
    fetched(2)
    project(1, (2,), 0, rows, chunk)
    far_wait.wait_recv()
    for shard in range(2):
        project(shard, (1, 2), rows, HALF, HALF)
    for own, near_far in ((r.k, r.kc), (r.v, r.vc)):
        near_far[pl.ds(0, HALF), :] = own[pl.ds(c_start, HALF), :]
        near_far[pl.ds(HALF, HALF), :] = own[pl.ds(rows, HALF), :]
    front_whole(1, 0, 2)
    hand_on(4)
    front_whole(1, 2, 3)
    hand_on(5)
    front_half()

    loaded("o")
    fetched(3)

    def pairs_of(i):
        return r.w_att[i].reshape(both, wide)

    def each(start, count, size, body):
        def step(n, _):
            body(at_rows(start + n * size, size), at_rows(n * size, size))
            return 0

        lax.fori_loop(0, count // size, step, 0)

    trades = []

    def trade_rows(compute, keep):
        def away_body(block, local):
            r.partial[local, :] = compute(block, local, True).astype(BF16)

        each(theirs, own_rows, chunk, away_body)
        n = len(trades)
        trades.append(
            rounds.start(remote(r.partial, r.partial_in, r.t_out.at[n], r.t_in.at[n], core_peer))
        )

        def own_body(block, local):
            keep(local, compute(block, local, False))

        each(mine, own_rows, chunk, own_body)
        trades[n].wait_recv()
        rounds.settle(trades[n])

    def gather_rows(ref, n):
        copy = rounds.start(remote(ref.at[own_at], ref.at[own_at], r.a_out.at[n], r.a_in.at[n], core_peer))
        there = ref.at[at_rows(theirs, own_rows)]
        return copy, remote(there, there, r.a_out.at[n], r.a_in.at[n], core_peer)

    def keep_acc(local, value):
        r.acc[local, :] = value

    trade_rows(lambda block, local, away: dg(r.ctx[block, :], pairs_of(3)), keep_acc)
    loaded("gain")
    b_output, first_gain, first_shift = (r.vectors[i : i + 1, :] for i in range(3))
    b_outer, second_gain, second_shift = (r.vectors[i : i + 1, :] for i in range(3, 6))

    def first_norm(block, local):
        value = r.x_rows[block, :].astype(F32) + r.acc[local, :] + r.partial_in[local, :].astype(F32) + b_output
        unit, inverse = normalize(value)
        r.acc[local, :] = unit
        r.inverse[local, :] = inverse
        r.first[block, :] = (unit * first_gain + first_shift).astype(BF16)

    each(mine, own_rows, strip, first_norm)
    first_copy, first_wait = gather_rows(r.first, 0)
    hand_on(6)

    def expand(shard, start, part=None):
        weights = (r.in_own, r.in_other)[shard]
        shifts = (r.biases, r.biases_other)[shard]
        hidden, slope = ((r.hidden_own, r.slope_own), (r.hidden_other, r.slope_other))[shard]

        def body(block, _):
            value, gradient = gelu_and_slope(dg(r.first[block, :], weights[...]) + shifts[0:1, :])
            hidden[block, :] = value.astype(BF16)
            slope[block, :] = gradient.astype(BF16)

        if part is None:
            each(start, own_rows, chunk, body)
        else:
            each(start + part * chunk, chunk, chunk, body)

    loaded("in")
    expand(0, mine)
    hand_on(7)
    first_wait.wait_recv()
    expand(0, theirs)
    hand_on(8)
    loaded("down")

    def own_part(target):
        def body(block, local):
            target[local, :] = dg(r.hidden_own[block, :], r.down_own[...])

        return body

    each(theirs, own_rows, chunk, own_part(r.spare))
    each(mine, own_rows, chunk, own_part(r.second))
    hand_on(9)
    fetched(4, 5, 6, 7)
    expand(1, theirs, 0)
    hand_on(10)
    expand(1, theirs, 1)
    expand(1, mine, 0)
    hand_on(11)
    expand(1, mine, 1)
    fetched(8, 9, 10, 11)

    def other_part(block, local, away):
        kept = r.spare if away else r.second
        return kept[local, :] + dg(r.hidden_other[block, :], r.down_other[...])

    def keep_second(local, value):
        r.second[local, :] = value

    trade_rows(other_part, keep_second)
    loaded("cotangent")
    zero = jnp.zeros((1, wide), F32)

    def second_norm(n, carry):
        block, local = at_rows(mine + n * strip, strip), at_rows(n * strip, strip)
        value = r.first[block, :].astype(F32) + r.second[local, :] + r.partial_in[local, :].astype(F32) + b_outer
        unit, inverse = normalize(value)
        r.output[local, :] = (unit * second_gain + second_shift).astype(BF16)
        upstream = r.grad_tokens[local, :].astype(F32)
        grad = norm_backward(upstream, unit, inverse, second_gain)
        r.second[local, :] = grad
        low = grad.astype(BF16)
        r.feed[block, :] = low
        gain, shift, lows = carry
        return gain + column_sum(upstream * unit), shift + column_sum(upstream), lows + column_sum(low.astype(F32))

    sum_second_gain, sum_second_shift, sum_b_outer = lax.fori_loop(
        0, own_rows // strip, second_norm, (zero, zero, zero)
    )
    feed_copy, feed_wait = gather_rows(r.feed, 1)

    def contract(shard, start, carry):
        weights = (r.down_own, r.down_other)[shard]
        slope = (r.slope_own, r.slope_other)[shard]

        def body(n, total):
            block = at_rows(start + n * chunk, chunk)
            value = dg(r.feed[block, :], weights[...], NT) * slope[block, :].astype(F32)
            low = value.astype(BF16)
            slope[block, :] = low
            return total + column_sum(low.astype(F32))

        return lax.fori_loop(0, own_rows // chunk, body, carry)

    sum_own = contract(0, mine, jnp.zeros((1, units), F32))
    sum_other = contract(1, mine, jnp.zeros((1, units), F32))
    feed_wait.wait_recv()

    def weight_blocks(target, band, left, right, first):
        columns = left.shape[1] // 3

        def body(n, _):
            value = dg(left[:, pl.ds(pl.multiple_of(n * columns, 128), columns)], right[...], TN).astype(BF16)
            for i in range(4):
                at = 4 * n + i
                b, h, j = band + lax.div(at, 6), lax.div(lax.rem(at, 6), 3), lax.rem(at, 3)
                target[b, h, j] = value[i * HD : (i + 1) * HD].reshape(4, HD // 4, value.shape[1])
            if first is not None:

                @pl.when(n == 0)
                def _():
                    rounds.y_start(first)

            return 0

        lax.fori_loop(0, 3, body, 0)

    def send(first, last):
        def body(u, _):
            rounds.y_start(u)
            return 0

        lax.fori_loop(first, last, body, 0)

    weight_blocks(r.grads_other, 0, r.hidden_other, r.feed, 0)
    send(1, 6)
    weight_blocks(r.grads_own, 0, r.hidden_own, r.feed, None)
    sum_own = contract(0, theirs, sum_own)
    sum_other = contract(1, theirs, sum_other)
    rounds.advance(0)

    def keep_first(local, value):
        r.second[local, :] = r.second[local, :] + value

    trade_rows(
        lambda block, local, away: dg(r.slope_own[block, :], r.in_own[...], NT) + dg(r.slope_other[block, :], r.in_other[...], NT),
        keep_first,
    )
    rounds.settle(feed_copy)
    rounds.advance(1)

    def first_back(n, carry):
        block, local = at_rows(mine + n * strip, strip), at_rows(n * strip, strip)
        grad_first = r.second[local, :] + r.partial_in[local, :].astype(F32)
        unit = r.acc[local, :]
        grad = norm_backward(grad_first, unit, r.inverse[local, :], first_gain)
        r.second[local, :] = grad
        low = grad.astype(BF16)
        r.feed[block, :] = low
        gain, shift, lows = carry
        return gain + column_sum(grad_first * unit), shift + column_sum(grad_first), lows + column_sum(low.astype(F32))

    sum_first_gain, sum_first_shift, sum_b_output = lax.fori_loop(0, own_rows // strip, first_back, (zero, zero, zero))
    branch_copy, branch_wait = gather_rows(r.feed, 2)
    rounds.advance(2)
    weight_blocks(r.grads_other, 2, r.first, r.slope_other, None)
    send(6, 12)
    weight_blocks(r.grads_own, 2, r.first, r.slope_own, None)
    rounds.advance(3)
    branch_wait.wait_recv()

    dq = r.hidden_own.at[:, pl.ds(0, both)]
    dk = r.hidden_own.at[:, pl.ds(both, both)]
    dv = r.hidden_other.at[:, pl.ds(0, both)]
    gc = r.hidden_other.at[:, pl.ds(both, both)]

    def context_back(block, _):
        gc[block, :] = dg(r.feed[block, :], pairs_of(3), NT).astype(BF16)

    each(0, rows, chunk, context_back)

    def back_half(j, _):
        lanes = pair_lanes(j)
        at = pl.ds(2 * LEN, HALF)
        stats = [r.lse[pl.ds(j * 2 + h, 1), at] for h in range(2)]
        block = pl.ds(c_start, HALF)
        d_q, d_k, d_v = pair_back(
            r.q[block, lanes], r.kc[:, lanes], r.vc[:, lanes], gc[block, lanes], r.bias[:, at], stats
        )
        dq[block, lanes] = d_q
        dk[block, lanes] = d_k[:HALF]
        dv[block, lanes] = d_v[:HALF]
        r.away[0, :, lanes] = d_k[HALF:]
        r.away[1, :, lanes] = d_v[HALF:]
        return 0

    lax.fori_loop(0, PAIRS, back_half, 0)
    rounds.advance(4)

    grad_out = dg(r.ctx[...], r.feed[...], TN).astype(BF16)
    for j in range(PAIRS):
        for shard, target in ((0, r.grads_own), (1, r.grads_other)):
            lane = (2 * j + shard) * HD
            target[5, 1, j] = grad_out[lane : lane + HD].reshape(4, HD // 4, wide)

    def back_whole(j):
        def body(i, _):
            lanes = pair_lanes(j)
            block = at_rows(side * HALF + i * LEN, LEN)
            at = pl.ds(pl.multiple_of(i * LEN, LEN), LEN)
            stats = [r.lse[pl.ds(j * 2 + h, 1), at] for h in range(2)]
            d_q, d_k, d_v = pair_back(
                r.q[block, lanes], r.k[block, lanes], r.v[block, lanes], gc[block, lanes], r.bias[:, at], stats
            )
            dq[block, lanes] = d_q
            dk[block, lanes] = d_k
            dv[block, lanes] = d_v
            return 0

        lax.fori_loop(0, 2, body, 0)

    def weight_pair(j):
        lanes = pair_lanes(j)
        left = jnp.concatenate([dq[:, lanes], dk[:, lanes], dv[:, lanes]], axis=1)
        value = dg(left, r.x_rows[pl.ds(0, rows), :], TN)
        far_left = jnp.concatenate([r.away[0, :, lanes], r.away[1, :, lanes]], axis=1)
        far = dg(far_left, r.x_rows[pl.ds(rows, HALF), :], TN)
        first = value[: 2 * HD].astype(BF16)
        rest = (value[2 * HD :] + far).astype(BF16)
        at = 12 + 2 * j
        for shard, target in ((0, r.grads_own), (1, r.grads_other)):
            cut = slice(shard * HD, (shard + 1) * HD)
            pieces = [v[cut].reshape(4, HD // 4, wide) for v in (first, rest[: 2 * HD], rest[2 * HD :])]
            target[4, 0, j] = pieces[0]
            target[4, 1, j] = pieces[1]
            target[5, 0, j] = pieces[2]
        rounds.y_start(at)
        rounds.y_start(at + 1)

    def back_pair(j, _):
        back_whole(j)
        rounds.advance(5 + 2 * j, 5)
        weight_pair(j)
        rounds.advance(6 + 2 * j, 6)
        return 0

    lax.fori_loop(0, PAIRS, back_pair, 0)

    rounds.advance(11)

    def bias_sum(*grads):
        total = sum(column_sum(part) for part in grads)
        heads = [total[:, i * HD : (i + 1) * HD] for i in range(2 * PAIRS)]
        return jnp.concatenate(heads[0::2], axis=1), jnp.concatenate(heads[1::2], axis=1)

    sums = (sum_b_output, sum_first_gain, sum_first_shift, sum_b_outer, sum_second_gain, sum_second_shift)
    for t in range(PARTS):
        shares = [value[:, t * width : (t + 1) * width] for value in sums]
        r.tiny[t, 0:1, :] = jnp.concatenate(shares[:4], axis=1)
        r.tiny[t, 1:2, :] = jnp.concatenate(shares[4:] + [jnp.zeros((1, 2 * width), F32)], axis=1)
        r.tiny[t, 2:3, :] = jnp.zeros((1, units), F32)
    queries, values = bias_sum(dq[...].astype(F32)), bias_sum(dv[...].astype(F32), r.away[1].astype(F32))
    for target, n, inner in ((place, 0, sum_own), ((place + 2) % 4, 1, sum_other)):
        r.tiny[target, 1:2, 2 * width :] = jnp.concatenate([queries[n], values[n]], axis=1)
        r.tiny[target, 2:3, :] = inner
    tiny_copies = []
    for step in (1, 2, 3):
        peer = (place + step) % 4
        out, into = r.i_out.at[step - 1], r.i_in.at[step - 1]
        tiny_copies.append(rounds.start(remote(r.tiny.at[peer], r.tiny_side.at[step - 1], out, into, {"tensor": peer})))

    def input_rows(block, local, away):
        value = dg(dq[block, :], pairs_of(0))
        value = value + dg(dk[block, :], pairs_of(1))
        return value + dg(dv[block, :], pairs_of(2))

    r.far_part[...] = (dg(r.away[0], pairs_of(1)) + dg(r.away[1], pairs_of(2))).astype(BF16)
    give = at_rows((1 - core) * quarter, quarter)
    keep = at_rows(core * quarter, quarter)
    far_trade = rounds.start(
        remote(r.far_part.at[give], r.far_half, r.s_out.at[4], r.s_in.at[4], core_peer)
    )
    rounds.advance(12)
    far_trade.wait_recv()
    r.far_send[...] = (r.far_part[keep, :].astype(F32) + r.far_half[...].astype(F32)).astype(BF16)
    owner = {"tensor": (1 - side) * 2 + side}
    rounds.start(remote(r.far_send, r.far_in.at[core], r.o_out, r.o_in.at[core], owner))

    trade_rows(input_rows, keep_first)
    rounds.advance(13)

    total = r.tiny[place]
    for step in (1, 2, 3):
        tiny_copies[step - 1].wait_recv()
        total = total + r.tiny_side[step - 1]
    r.tiny_all[0] = total

    def tell(step, _):
        peer = {"dp": (group + step) % groups}
        remote(r.tiny_all.at[0], r.tiny_all.at[step], r.d_out.at[step], r.d_in.at[step], peer).start()
        return 0

    lax.fori_loop(1, groups, tell, 0)

    def pump(n, _):
        rounds.advance(n, 14)
        return 0

    lax.fori_loop(14, PIECES, pump, 0)
    rounds.advance(PIECES)

    @pl.when(core == 1 - side)
    def _():
        start = (1 - side) * (own_rows - HALF)
        for n in range(2):
            remote(r.far_send, r.far_in.at[n], r.o_out, r.o_in.at[n], owner).wait_recv()
            block = at_rows(start + n * quarter, quarter)
            r.second[block, :] = r.second[block, :] + r.far_in[n].astype(F32)

    def finish(block, local):
        r.grad_tokens[local, :] = (r.second[local, :] + r.partial_in[local, :].astype(F32)).astype(BF16)

    each(mine, own_rows, strip, finish)

    for n in range(PIECES + 1, PIECES + LAGS[0]):
        rounds.advance(n)

    def hear(step, total):
        peer = {"dp": (group + step) % groups}
        copy = remote(r.tiny_all.at[0], r.tiny_all.at[step], r.d_out.at[step], r.d_in.at[step], peer)
        copy.wait()
        return total + r.tiny_all[step]

    r.small[...] = lax.fori_loop(1, groups, hear, r.tiny_all[0])

    rounds.finish()


def layer(groups, named):
    dma = pltpu.SemaphoreType.DMA
    own_rows, wide = named["tokens"].shape
    units = named["w_inner"].shape[1]
    heads = named["w_query"].shape
    rows, both = 2 * own_rows, 2 * heads[0] * heads[1]
    more = groups // OWNERS
    share = wide // 6 // OWNERS
    bands = (6, 2, 3, 4, share, wide)
    outs = {
        "output": ((own_rows, wide), BF16),
        "grad_tokens": ((own_rows, wide), BF16),
        "total": (bands, BF16),
        "small": ((3, wide), F32),
    }
    room = {
        "x_rows": ((rows + HALF, wide), BF16),
        "w_att": ((4, PAIRS, 2, HD, wide), BF16),
        "in_own": ((wide, units), BF16),
        "in_other": ((wide, units), BF16),
        "down_own": ((units, wide), BF16),
        "down_other": ((units, wide), BF16),
        "vectors": ((8, wide), F32),
        "biases": ((8, wide), F32),
        "biases_other": ((8, wide), F32),
        "narrow": ((8, both // 2), F32),
        "narrow_other": ((8, both // 2), F32),
        "segments": ((8, LEN), jnp.int32),
        "bias": ((LEN, rows), F32),
        "q": ((rows, both), BF16),
        "k": ((rows + HALF, both), BF16),
        "v": ((rows + HALF, both), BF16),
        "kc": ((LEN, both), BF16),
        "vc": ((LEN, both), BF16),
        "ctx": ((rows, both), BF16),
        "lse": ((8, rows), F32),
        "partial": ((own_rows, wide), BF16),
        "partial_in": ((own_rows, wide), BF16),
        "acc": ((own_rows, wide), F32),
        "inverse": ((own_rows, 1), F32),
        "first": ((rows, wide), BF16),
        "hidden_own": ((rows, units), BF16),
        "hidden_other": ((rows, units), BF16),
        "slope_own": ((rows, units), BF16),
        "slope_other": ((rows, units), BF16),
        "second": ((own_rows, wide), F32),
        "spare": ((own_rows, wide), F32),
        "feed": ((rows, wide), BF16),
        "away": ((2, HALF, both), BF16),
        "far_part": ((HALF, wide), BF16),
        "far_half": ((HALF // 2, wide), BF16),
        "far_send": ((HALF // 2, wide), BF16),
        "far_in": ((2, HALF // 2, wide), BF16),
        "grads_own": (bands, BF16),
        "grads_other": (bands, BF16),
        "from_side": (bands, BF16),
        "from_x": ((6, 3, 4, share, wide), BF16),
        "from_z": ((6, 3, 3, share, wide), BF16),
        "from_far": ((PIECES, more - 1, share, wide) if more > 1 else (1, 1, 16, 128), BF16),
        "tiny": ((PARTS, 3, wide), F32),
        "tiny_side": ((3, 3, wide), F32),
        "tiny_all": ((groups, 3, wide), F32),
    }
    sems = {
        "l_sem": (22,),
        "s_out": (6,),
        "s_in": (6,),
        "w_out_sem": (12,),
        "w_in_sem": (12,),
        "p_out_sem": (12,),
        "p_in_sem": (12,),
        "t_out": (4,),
        "t_in": (4,),
        "a_out": (3,),
        "a_in": (3,),
        "y_out": (PIECES,),
        "y_in": (PIECES,),
        "x_out": (PIECES,),
        "x_in": (PIECES,),
        "z_out": (PIECES, 3),
        "z_in": (PIECES, 3),
        "g_out": (PIECES, 3),
        "g_in": (PIECES, 3),
        "h_out": (PIECES,),
        "h_in": (PIECES,),
        "f_out": (PIECES, max(more - 1, 1)),
        "f_in": (PIECES, max(more - 1, 1)),
        "i_out": (3,),
        "i_in": (3,),
        "d_out": (groups,),
        "d_in": (groups,),
        "o_out": (),
        "o_in": (2,),
    }
    names = list(named) + list(outs) + list(room) + list(sems)
    in_vmem = pl.BlockSpec(memory_space=pltpu.VMEM)
    spaces = {"lengths": pltpu.SMEM}
    results = pl.pallas_call(
        functools.partial(layer_kernel, groups, names),
        out_shape=[jax.ShapeDtypeStruct(*spec) for spec in outs.values()],
        in_specs=[pl.BlockSpec(memory_space=spaces.get(name, pl.ANY)) for name in named],
        out_specs=[in_vmem] * len(outs),
        scratch_shapes=[pltpu.VMEM(*spec) for spec in room.values()] + [dma(shape) for shape in sems.values()],
        compiler_params=pltpu.CompilerParams(
            collective_id=0, has_side_effects=True, vmem_limit_bytes=67043328
        ),
    )(*named.values())
    return dict(zip(outs, results))


def shards(
    tokens,
    segment_ids,
    lengths,
    w_query,
    b_query,
    w_key,
    w_value,
    b_value,
    w_output,
    b_output,
    first_gain,
    first_shift,
    w_inner,
    b_inner,
    w_outer,
    b_outer,
    second_gain,
    second_shift,
    cotangent,
):
    groups = lax.axis_size("dp")
    wide, width = w_query.shape
    units = w_inner.shape[1]
    by_head = (width // HD, HD, wide)
    done = layer(
        groups,
        {
            "tokens": tokens,
            "w_query": w_query.T.reshape(by_head),
            "w_key": w_key.T.reshape(by_head),
            "w_value": w_value.T.reshape(by_head),
            "w_output": w_output.reshape(by_head),
            "w_inner": w_inner,
            "w_outer": w_outer,
            "cotangent": cotangent,
            "b_query": b_query,
            "b_value": b_value,
            "b_inner": b_inner,
            "b_output": b_output,
            "first_gain": first_gain,
            "first_shift": first_shift,
            "b_outer": b_outer,
            "second_gain": second_gain,
            "second_shift": second_shift,
            "segment_ids": segment_ids,
            "lengths": lengths,
        },
    )
    sums = done["total"]
    query, key = (sums[4, i].reshape(width, wide).astype(F32) for i in range(2))
    value, out = (sums[5, i].reshape(width, wide).astype(F32) for i in range(2))
    small = done["small"]
    shares = [small[0, i * width : (i + 1) * width] for i in range(4)]
    shares += [small[1, i * width : (i + 1) * width] for i in range(4)]
    return (
        done["output"],
        done["grad_tokens"],
        query.T,
        shares[6],
        key.T,
        value.T,
        shares[7],
        out,
        shares[0],
        shares[1],
        shares[2],
        sums[2:4].reshape(wide, units).astype(F32),
        small[2],
        sums[0:2].reshape(units, wide).astype(F32),
        shares[3],
        shares[4],
        shares[5],
    )


def solution(mesh):
    in_specs = (
        P(("dp", "tensor"), None),
        P("dp"),
        P("dp"),
        P(None, "tensor"),
        P("tensor"),
        P(None, "tensor"),
        P(None, "tensor"),
        P("tensor"),
        P("tensor", None),
        P(),
        P(),
        P(),
        P(None, "tensor"),
        P("tensor"),
        P("tensor", None),
        P(),
        P(),
        P(),
        P(("dp", "tensor"), None),
    )
    out_specs = (
        P(("dp", "tensor"), None),
        P(("dp", "tensor"), None),
        P(None, "tensor"),
        P("tensor"),
        P(None, "tensor"),
        P(None, "tensor"),
        P("tensor"),
        P("tensor", None),
        P("tensor"),
        P("tensor"),
        P("tensor"),
        P(None, "tensor"),
        P("tensor"),
        P("tensor", None),
        P("tensor"),
        P("tensor"),
        P("tensor"),
    )
    return jax.shard_map(shards, mesh=mesh, in_specs=in_specs, out_specs=out_specs, check_vma=False)
```

```python
import functools
import math
import types

import jax
import jax.numpy as jnp
from jax import lax
from jax.experimental import pallas as pl
from jax.experimental.pallas import tpu as pltpu
from jax.sharding import PartitionSpec as P

HD = 64
LEN = 512
HALF = LEN // 2
EPSILON = 1e-12
NEGATIVE = -1000000000.0
SCALE = 1.0 / math.sqrt(HD)
LOG2E = math.log2(math.e)
F32 = jnp.float32
BF16 = jnp.bfloat16
NN = (((1,), (0,)), ((), ()))
NT = (((1,), (1,)), ((), ()))
TN = (((0,), (0,)), ((), ()))
MESH = pl.DeviceIdType.MESH
PARTS = 4
OWNERS = 8
PAIRS = 3
PIECES = 18
LAGS = (6, 4, 2, 0)


def dg(left, right, dims=NN):
    return lax.dot_general(left, right, dims, preferred_element_type=F32)


def normalize(value):
    average = jnp.mean(value, axis=-1, keepdims=True)
    centered = value - average
    variance = jnp.mean(centered * centered, axis=-1, keepdims=True)
    inverse = lax.rsqrt(variance + EPSILON)
    return centered * inverse, inverse


def norm_backward(grad, unit, inverse, gain):
    scaled = grad * gain
    first_mean = jnp.mean(scaled, axis=-1, keepdims=True)
    second_mean = jnp.mean(scaled * unit, axis=-1, keepdims=True)
    return inverse * (scaled - first_mean - unit * second_mean)


def gelu_and_slope(inner):
    cumulative = 0.5 * (1.0 + lax.erf(inner * (1.0 / math.sqrt(2.0))))
    slope = cumulative + inner * jnp.exp(-0.5 * inner * inner) * (1.0 / math.sqrt(2.0 * math.pi))
    return inner * cumulative, slope


def column_sum(value):
    return jnp.sum(value, axis=0, keepdims=True)


def attend_front(q, k, v, bias):
    logits = dg(k, q, NT) * (SCALE * LOG2E) + bias
    peak = jnp.max(logits, axis=0, keepdims=True)
    powers = jnp.exp2(logits - peak)
    total = jnp.sum(powers, axis=0, keepdims=True)
    weights = (powers * (1.0 / total)).astype(BF16)
    return dg(weights, v, TN).astype(BF16), peak + jnp.log2(total)


def attend_back(q, k, v, g, bias, row):
    logits = dg(k, q, NT) * (SCALE * LOG2E) + bias
    probs = jnp.exp2(logits - row)
    dprobs = dg(v, g, NT)
    across = jnp.sum(probs * dprobs, axis=0, keepdims=True)
    dscores = (probs * (dprobs - across) * SCALE).astype(BF16)
    dv = dg(probs.astype(BF16), g, NN).astype(BF16)
    dk = dg(dscores, q, NN).astype(BF16)
    dq = dg(dscores, k, TN).astype(BF16)
    return dq, dk, dv


def pair_back(q, k, v, g, bias, rows):
    done = []
    for h in range(2):
        cols = slice(h * HD, (h + 1) * HD)
        done.append(attend_back(q[:, cols], k[:, cols], v[:, cols], g[:, cols], bias, rows[h]))
    return [jnp.concatenate([done[0][i], done[1][i]], axis=1) for i in range(3)]


def swap_halves(value):
    return jnp.concatenate([value[:, HD:], value[:, :HD]], axis=1)


def pair_lanes(j):
    return pl.ds(pl.multiple_of(j * 2 * HD, 2 * HD), 2 * HD)


def remote(source, target, out, into, device):
    return pltpu.make_async_remote_copy(
        src_ref=source, dst_ref=target, send_sem=out, recv_sem=into, device_id=device, device_id_type=MESH
    )


class Rounds:
    def __init__(self, r, groups):
        self.r = r
        self.place = lax.axis_index("tensor")
        group = lax.axis_index("dp")
        self.x, self.z, self.far = group % 2, (group // 2) % 4, group // OWNERS
        self.more = groups // OWNERS
        self.sent = []

    def dp_at(self, x, z):
        return {"dp": self.far * OWNERS + z * 2 + x}

    def start(self, copy):
        copy.start()
        self.sent.append(copy)
        return copy

    def settle(self, copy):
        copy.wait_send()
        self.sent = [other for other in self.sent if other is not copy]

    @staticmethod
    def where(u):
        if isinstance(u, int):
            return 2 * (u // 6) + u % 2, u % 6 // 2
        return 2 * lax.div(u, 6) + lax.rem(u, 2), lax.div(lax.rem(u, 6), 2)

    def y_copy(self, u):
        r = self.r
        b, j = self.where(u)
        side = {"tensor": (self.place + 2) % 4}
        both = pl.ds(0, 2)
        return remote(r.grads_other.at[b, both, j], r.from_side.at[b, both, j], r.y_out.at[u], r.y_in.at[u], side)

    def x_copy(self, u):
        r = self.r
        b, j = self.where(u)
        away = r.grads_own.at[b, 1 - self.x, j]
        return remote(away, r.from_x.at[b, j], r.x_out.at[u], r.x_in.at[u], self.dp_at(1 - self.x, self.z))

    def z_copy(self, u, step):
        r = self.r
        b, j = self.where(u)
        there = (self.z + step) % 4
        away = r.grads_own.at[b, self.x, j, there]
        out, into = r.z_out.at[u, step - 1], r.z_in.at[u, step - 1]
        return remote(away, r.from_z.at[b, j, step - 1], out, into, self.dp_at(self.x, there))

    def f_copy(self, u, step):
        r = self.r
        b, j = self.where(u)
        peer = {"dp": ((self.far + step) % self.more) * OWNERS + self.z * 2 + self.x}
        own = r.grads_own.at[b, self.x, j, self.z]
        return remote(own, r.from_far.at[u, step - 1], r.f_out.at[u, step - 1], r.f_in.at[u, step - 1], peer)

    def g_copy(self, u, step, origin):
        r = self.r
        b, j = self.where(u)
        piece = r.total.at[b, self.x, j, origin]
        out, into = r.g_out.at[u, step - 1], r.g_in.at[u, step - 1]
        return remote(piece, piece, out, into, self.dp_at(self.x, (self.z + step) % 4))

    def h_copy(self, u, half):
        r = self.r
        b, j = self.where(u)
        piece = r.total.at[b, half, j]
        return remote(piece, piece, r.h_out.at[u], r.h_in.at[u], self.dp_at(1 - self.x, self.z))

    def y_start(self, u):
        self.y_copy(u).start()

    def x_start(self, u):
        r = self.r
        b, j = self.where(u)
        self.y_copy(u).wait_recv()
        for half in range(2):
            summed = r.grads_own[b, half, j].astype(F32) + r.from_side[b, half, j].astype(F32)
            r.grads_own[b, half, j] = summed.astype(BF16)
        self.x_copy(u).start()

    def z_start(self, u):
        r = self.r
        b, j = self.where(u)
        self.x_copy(u).wait_recv()
        summed = r.grads_own[b, self.x, j].astype(F32) + r.from_x[b, j].astype(F32)
        r.grads_own[b, self.x, j] = summed.astype(BF16)
        for step in (1, 2, 3):
            self.z_copy(u, step).start()

    def g_start(self, u):
        r = self.r
        b, j = self.where(u)
        value = r.grads_own[b, self.x, j, self.z].astype(F32)
        for step in (1, 2, 3):
            self.z_copy(u, step).wait_recv()
            value = value + r.from_z[b, j, step - 1].astype(F32)
        if self.more > 1:
            r.grads_own[b, self.x, j, self.z] = value.astype(BF16)
            for step in range(1, self.more):
                self.f_copy(u, step).start()
            for step in range(1, self.more):
                self.f_copy(u, step).wait_recv()
                value = value + r.from_far[u, step - 1].astype(F32)
        r.total[b, self.x, j, self.z] = value.astype(BF16)
        for step in (1, 2, 3):
            self.g_copy(u, step, self.z).start()

    def h_start(self, u):
        for step in (1, 2, 3):
            self.g_copy(u, step, (self.z - step + 4) % 4).wait_recv()
        self.h_copy(u, self.x).start()

    def advance(self, n, least=0):
        stages = (self.h_start, self.g_start, self.z_start, self.x_start)
        for behind, stage in zip(LAGS, stages):
            if isinstance(n, int):
                if 0 <= n - behind < PIECES:
                    stage(n - behind)
            elif least >= behind:
                stage(n - behind)
            else:
                pl.when(n >= behind)(functools.partial(stage, n - behind))

    def finish(self):
        def settle(u, _):
            self.h_copy(u, 1 - self.x).wait_recv()
            for copy in (self.y_copy(u), self.x_copy(u), self.h_copy(u, self.x)):
                copy.wait_send()
            for step in (1, 2, 3):
                self.z_copy(u, step).wait_send()
                self.g_copy(u, step, self.z).wait_send()
            for step in range(1, self.more):
                self.f_copy(u, step).wait_send()
            return 0

        lax.fori_loop(0, PIECES, settle, 0)
        for copy in self.sent:
            copy.wait_send()


def layer_kernel(groups, names, *refs):
    r = types.SimpleNamespace(**dict(zip(names, refs)))
    place = lax.axis_index("tensor")
    group = lax.axis_index("dp")
    core, side = place % 2, place // 2
    rows = r.q.shape[0]
    own_rows = rows // 2
    wide = r.x_rows.shape[1]
    both = r.q.shape[1]
    width = both // 2
    units = r.w_inner.shape[1]
    chunk = own_rows // 2
    strip = own_rows // 8
    mine = core * own_rows
    theirs = (1 - core) * own_rows
    c_start = pl.multiple_of((1 - side) * 2 * LEN, HALF)
    core_peer = {"tensor": place + 1 - 2 * core}
    side_peer = {"tensor": (place + 2) % 4}

    barrier = pltpu.get_barrier_semaphore()
    for step in (1, 2, 3):
        pl.semaphore_signal(barrier, inc=1, device_id={"tensor": (place + step) % 4}, device_id_type=MESH)

    def greet(step, _):
        peer = (group + step) % groups
        pl.semaphore_signal(barrier, inc=1, device_id={"dp": peer}, device_id_type=MESH)
        return 0

    lax.fori_loop(1, groups, greet, 0)

    def at_rows(start, count):
        return pl.ds(pl.multiple_of(start, 16), count)

    own_at = at_rows(mine, own_rows)
    loads = {}
    sources = [
        ("tokens", r.tokens, r.x_rows.at[own_at]),
        ("q", r.w_query, r.w_att.at[0, :, 0]),
        ("k", r.w_key, r.w_att.at[1, :, 0]),
        ("v", r.w_value, r.w_att.at[2, :, 0]),
        ("o", r.w_output, r.w_att.at[3, :, 0]),
        ("in", r.w_inner, r.in_own),
        ("down", r.w_outer, r.down_own),
        ("cotangent", r.cotangent, r.grad_tokens),
    ]
    sources += [("shift", r.b_query, r.narrow.at[0]), ("shift", r.b_value, r.narrow.at[1])]
    sources += [("shift", r.b_inner, r.biases.at[0])]
    gains = (r.b_output, r.first_gain, r.first_shift, r.b_outer, r.second_gain, r.second_shift)
    sources += [("gain", ref, r.vectors.at[i]) for i, ref in enumerate(gains)]
    sources += [("segment", r.segment_ids.at[pl.ds(i * LEN, LEN)], r.segments.at[i]) for i in range(5)]
    for n, (name, source, target) in enumerate(sources):
        copy = pltpu.make_async_copy(source, target, r.l_sem.at[n])
        copy.start()
        loads.setdefault(name, []).append(copy)

    def loaded(*wanted):
        for name in wanted:
            for copy in loads[name]:
                copy.wait()

    pl.semaphore_wait(barrier, 3 + groups - 1)
    rounds = Rounds(r, groups)
    x, z = rounds.x, rounds.z
    x_peer = rounds.dp_at(1 - x, z)

    lanes = wide // 2
    block = units // 8

    def by_heads(source, i):
        def view(ref, half):
            return ref.at[:, :, pl.ds(half * lanes, lanes)]

        return source, r.w_att.at[i, :, 1], view

    def by_rows(source, target, n):
        def view(ref, half):
            return ref.at[at_rows((half * 4 + n) * block, block)]

        return source, target, view

    fetches = [by_heads(w, i) for i, w in enumerate((r.w_query, r.w_key, r.w_value, r.w_output))]
    fetches += [by_rows(r.w_inner, r.in_other, n) for n in range(4)]
    fetches += [by_rows(r.w_outer, r.down_other, n) for n in range(4)]

    def fetch_copy(n):
        source, target, view = fetches[n]
        return remote(view(source, x), view(target, x), r.w_out_sem.at[n], r.w_in_sem.at[n], side_peer)

    def pass_copy(n, which):
        _, target, view = fetches[n]
        return remote(view(target, which), view(target, which), r.p_out_sem.at[n], r.p_in_sem.at[n], x_peer)

    def fetch(*which):
        for n in which:
            rounds.start(fetch_copy(n))

    def hand_on(*which):
        for n in which:
            fetch_copy(n).wait_recv()
            rounds.start(pass_copy(n, x))

    def fetched(*which):
        for n in which:
            pass_copy(n, 1 - x).wait_recv()

    token_copy = rounds.start(remote(r.tokens, r.x_rows.at[own_at], r.s_out.at[0], r.s_in.at[0], core_peer))
    token_wait = remote(r.tokens, r.x_rows.at[at_rows(theirs, own_rows)], r.s_out.at[0], r.s_in.at[0], core_peer)
    fetch(0, 1, 2)
    loaded("shift")
    vector_copies = [
        rounds.start(remote(r.biases, r.biases_other, r.s_out.at[1], r.s_in.at[1], side_peer)),
        rounds.start(remote(r.narrow, r.narrow_other, r.s_out.at[5], r.s_in.at[5], side_peer)),
    ]

    def project(shard, which, start, count, size):
        shifts = (r.narrow, r.narrow_other)[shard]
        for i in which:
            target = (r.q, r.k, r.v)[i]
            weights = r.w_att[i, :, shard].reshape(width, wide)

            def body(n, _):
                block = at_rows(start + n * size, size)
                value = dg(r.x_rows[block, :], weights, NT)
                if i == 0:
                    value = value + shifts[0:1, :]
                if i == 2:
                    value = value + shifts[1:2, :]
                value = value.astype(BF16)
                for j in range(PAIRS):
                    lane = (2 * j + shard) * HD
                    target[block, lane : lane + HD] = value[:, j * HD : (j + 1) * HD]
                return 0

            lax.fori_loop(0, count // size, body, 0)

    loaded("tokens")
    loaded("q", "k", "v")
    project(0, (0, 1, 2), mine, own_rows, chunk)

    token_wait.wait_recv()
    quarter = HALF // 2
    far_at = at_rows(rows + core * quarter, quarter)
    far_there = at_rows(rows + (1 - core) * quarter, quarter)
    near_at = at_rows(c_start + core * quarter, quarter)
    far_copy = rounds.start(
        remote(r.x_rows.at[near_at], r.x_rows.at[far_at], r.s_out.at[2], r.s_in.at[2], side_peer)
    )
    fetch(*range(3, 12))
    project(0, (0, 1, 2), theirs, own_rows, chunk)
    hand_on(0)

    loaded("segment")

    def mask_block(at, row, places, length, count):
        column = jnp.transpose(jnp.broadcast_to(row.astype(F32), (128, LEN)))[:, 0:1]
        same = column == row.astype(F32)[:, :count]
        live = places < length
        first = lax.broadcasted_iota(jnp.int32, (LEN, count), 0)
        second = lax.broadcasted_iota(jnp.int32, (LEN, count), 1)
        allowed = same & live | (first == second)
        r.bias[:, at : at + count] = jnp.where(allowed, 0.0, NEGATIVE)

    ahead = lax.broadcasted_iota(jnp.int32, (LEN, 1), 0)
    for which in range(2):
        index = 3 * side + which
        mask_block(which * LEN, r.segments[pl.ds(index, 1), :], ahead, r.lengths[index], LEN)
    near = r.segments[2:3, pl.ds(pl.multiple_of(side * HALF, HALF), HALF)]
    away_row = r.segments[2:3, pl.ds(pl.multiple_of((1 - side) * HALF, HALF), HALF)]
    turned = jnp.where(ahead < HALF, ahead + side * HALF, ahead - side * HALF)
    mask_block(2 * LEN, jnp.concatenate([near, away_row], axis=1), turned, r.lengths[2], HALF)
    hand_on(1)

    def front_store(shard, block, lanes, out):
        if shard == 0:
            r.ctx[block, lanes] = jnp.concatenate([out, jnp.zeros_like(out)], axis=1)
        else:
            r.ctx[block, lanes] = jnp.concatenate([r.ctx[block, lanes][:, :HD], out], axis=1)

    def front_whole(shard, first_pair, last_pair):
        cols = slice(shard * HD, (shard + 1) * HD)

        def body(j, _):
            lanes = pair_lanes(j)
            for i in range(2):
                block = at_rows(side * HALF + i * LEN, LEN)
                at = pl.ds(i * LEN, LEN)
                out, row = attend_front(
                    r.q[block, lanes][:, cols], r.k[block, lanes][:, cols], r.v[block, lanes][:, cols], r.bias[:, at]
                )
                front_store(shard, block, lanes, out)
                r.lse[pl.ds(2 * j + shard, 1), at] = row
            return 0

        lax.fori_loop(first_pair, last_pair, body, 0)

    def front_half():
        def body(j, _):
            lanes = pair_lanes(j)
            block = pl.ds(c_start, HALF)
            at = pl.ds(2 * LEN, HALF)
            q, k, v = r.q[block, lanes], r.kc[:, lanes], r.vc[:, lanes]
            outs = []
            for shard in range(2):
                cols = slice(shard * HD, (shard + 1) * HD)
                out, row = attend_front(q[:, cols], k[:, cols], v[:, cols], r.bias[:, at])
                outs.append(out)
                r.lse[pl.ds(2 * j + shard, 1), at] = row
            r.ctx[block, lanes] = jnp.concatenate(outs, axis=1)
            return 0

        lax.fori_loop(0, PAIRS, body, 0)

    front_whole(0, 0, 2)
    hand_on(2)
    front_whole(0, 2, 3)
    far_copy.wait_recv()
    far_pass = rounds.start(
        remote(r.x_rows.at[far_at], r.x_rows.at[far_at], r.s_out.at[3], r.s_in.at[3], core_peer)
    )
    far_wait = remote(r.x_rows.at[far_there], r.x_rows.at[far_there], r.s_out.at[3], r.s_in.at[3], core_peer)
    for copy in vector_copies:
        copy.wait_recv()
    fetched(0)
    project(1, (0,), 0, rows, chunk)
    fetched(1)
    project(1, (1,), 0, rows, chunk)
    hand_on(3)
    fetched(2)
    project(1, (2,), 0, rows, chunk)
    far_wait.wait_recv()
    for shard in range(2):
        project(shard, (1, 2), rows, HALF, HALF)
    for own, near_far in ((r.k, r.kc), (r.v, r.vc)):
        near_far[pl.ds(0, HALF), :] = own[pl.ds(c_start, HALF), :]
        near_far[pl.ds(HALF, HALF), :] = own[pl.ds(rows, HALF), :]
    front_whole(1, 0, 2)
    hand_on(4)
    front_whole(1, 2, 3)
    hand_on(5)
    front_half()

    loaded("o")
    fetched(3)

    def pairs_of(i):
        return r.w_att[i].reshape(both, wide)

    def each(start, count, size, body):
        def step(n, _):
            body(at_rows(start + n * size, size), at_rows(n * size, size))
            return 0

        lax.fori_loop(0, count // size, step, 0)

    trades = []

    def trade_rows(compute, keep):
        def away_body(block, local):
            r.partial[local, :] = compute(block, local, True).astype(BF16)

        each(theirs, own_rows, chunk, away_body)
        n = len(trades)
        trades.append(
            rounds.start(remote(r.partial, r.partial_in, r.t_out.at[n], r.t_in.at[n], core_peer))
        )

        def own_body(block, local):
            keep(local, compute(block, local, False))

        each(mine, own_rows, chunk, own_body)
        trades[n].wait_recv()
        rounds.settle(trades[n])

    def gather_rows(ref, n):
        copy = rounds.start(remote(ref.at[own_at], ref.at[own_at], r.a_out.at[n], r.a_in.at[n], core_peer))
        there = ref.at[at_rows(theirs, own_rows)]
        return copy, remote(there, there, r.a_out.at[n], r.a_in.at[n], core_peer)

    def keep_acc(local, value):
        r.acc[local, :] = value

    trade_rows(lambda block, local, away: dg(r.ctx[block, :], pairs_of(3)), keep_acc)
    loaded("gain")
    b_output, first_gain, first_shift = (r.vectors[i : i + 1, :] for i in range(3))
    b_outer, second_gain, second_shift = (r.vectors[i : i + 1, :] for i in range(3, 6))

    def first_norm(block, local):
        value = r.x_rows[block, :].astype(F32) + r.acc[local, :] + r.partial_in[local, :].astype(F32) + b_output
        unit, inverse = normalize(value)
        r.acc[local, :] = unit
        r.inverse[local, :] = inverse
        r.first[block, :] = (unit * first_gain + first_shift).astype(BF16)

    each(mine, own_rows, strip, first_norm)
    first_copy, first_wait = gather_rows(r.first, 0)
    hand_on(6)

    def expand(shard, start, part=None):
        weights = (r.in_own, r.in_other)[shard]
        shifts = (r.biases, r.biases_other)[shard]
        hidden, slope = ((r.hidden_own, r.slope_own), (r.hidden_other, r.slope_other))[shard]

        def body(block, _):
            value, gradient = gelu_and_slope(dg(r.first[block, :], weights[...]) + shifts[0:1, :])
            hidden[block, :] = value.astype(BF16)
            slope[block, :] = gradient.astype(BF16)

        if part is None:
            each(start, own_rows, chunk, body)
        else:
            each(start + part * chunk, chunk, chunk, body)

    loaded("in")
    expand(0, mine)
    hand_on(7)
    first_wait.wait_recv()
    expand(0, theirs)
    hand_on(8)
    loaded("down")

    def own_part(target):
        def body(block, local):
            target[local, :] = dg(r.hidden_own[block, :], r.down_own[...])

        return body

    each(theirs, own_rows, chunk, own_part(r.spare))
    each(mine, own_rows, chunk, own_part(r.second))
    hand_on(9)
    fetched(4, 5, 6, 7)
    expand(1, theirs, 0)
    hand_on(10)
    expand(1, theirs, 1)
    expand(1, mine, 0)
    hand_on(11)
    expand(1, mine, 1)
    fetched(8, 9, 10, 11)

    def other_part(block, local, away):
        kept = r.spare if away else r.second
        return kept[local, :] + dg(r.hidden_other[block, :], r.down_other[...])

    def keep_second(local, value):
        r.second[local, :] = value

    trade_rows(other_part, keep_second)
    loaded("cotangent")
    zero = jnp.zeros((1, wide), F32)

    def second_norm(n, carry):
        block, local = at_rows(mine + n * strip, strip), at_rows(n * strip, strip)
        value = r.first[block, :].astype(F32) + r.second[local, :] + r.partial_in[local, :].astype(F32) + b_outer
        unit, inverse = normalize(value)
        r.output[local, :] = (unit * second_gain + second_shift).astype(BF16)
        upstream = r.grad_tokens[local, :].astype(F32)
        grad = norm_backward(upstream, unit, inverse, second_gain)
        r.second[local, :] = grad
        low = grad.astype(BF16)
        r.feed[block, :] = low
        gain, shift, lows = carry
        return gain + column_sum(upstream * unit), shift + column_sum(upstream), lows + column_sum(low.astype(F32))

    sum_second_gain, sum_second_shift, sum_b_outer = lax.fori_loop(
        0, own_rows // strip, second_norm, (zero, zero, zero)
    )
    feed_copy, feed_wait = gather_rows(r.feed, 1)

    def contract(shard, start, carry):
        weights = (r.down_own, r.down_other)[shard]
        slope = (r.slope_own, r.slope_other)[shard]

        def body(n, total):
            block = at_rows(start + n * chunk, chunk)
            value = dg(r.feed[block, :], weights[...], NT) * slope[block, :].astype(F32)
            low = value.astype(BF16)
            slope[block, :] = low
            return total + column_sum(low.astype(F32))

        return lax.fori_loop(0, own_rows // chunk, body, carry)

    sum_own = contract(0, mine, jnp.zeros((1, units), F32))
    sum_other = contract(1, mine, jnp.zeros((1, units), F32))
    feed_wait.wait_recv()

    def weight_blocks(target, band, left, right, first):
        columns = left.shape[1] // 3

        def body(n, _):
            value = dg(left[:, pl.ds(pl.multiple_of(n * columns, 128), columns)], right[...], TN).astype(BF16)
            for i in range(4):
                at = 4 * n + i
                b, h, j = band + lax.div(at, 6), lax.div(lax.rem(at, 6), 3), lax.rem(at, 3)
                target[b, h, j] = value[i * HD : (i + 1) * HD].reshape(4, HD // 4, value.shape[1])
            if first is not None:

                @pl.when(n == 0)
                def _():
                    rounds.y_start(first)

            return 0

        lax.fori_loop(0, 3, body, 0)

    def send(first, last):
        def body(u, _):
            rounds.y_start(u)
            return 0

        lax.fori_loop(first, last, body, 0)

    weight_blocks(r.grads_other, 0, r.hidden_other, r.feed, 0)
    send(1, 6)
    weight_blocks(r.grads_own, 0, r.hidden_own, r.feed, None)
    sum_own = contract(0, theirs, sum_own)
    sum_other = contract(1, theirs, sum_other)
    rounds.advance(0)

    def keep_first(local, value):
        r.second[local, :] = r.second[local, :] + value

    trade_rows(
        lambda block, local, away: dg(r.slope_own[block, :], r.in_own[...], NT) + dg(r.slope_other[block, :], r.in_other[...], NT),
        keep_first,
    )
    rounds.settle(feed_copy)
    rounds.advance(1)

    def first_back(n, carry):
        block, local = at_rows(mine + n * strip, strip), at_rows(n * strip, strip)
        grad_first = r.second[local, :] + r.partial_in[local, :].astype(F32)
        unit = r.acc[local, :]
        grad = norm_backward(grad_first, unit, r.inverse[local, :], first_gain)
        r.second[local, :] = grad
        low = grad.astype(BF16)
        r.feed[block, :] = low
        gain, shift, lows = carry
        return gain + column_sum(grad_first * unit), shift + column_sum(grad_first), lows + column_sum(low.astype(F32))

    sum_first_gain, sum_first_shift, sum_b_output = lax.fori_loop(0, own_rows // strip, first_back, (zero, zero, zero))
    branch_copy, branch_wait = gather_rows(r.feed, 2)
    rounds.advance(2)
    weight_blocks(r.grads_other, 2, r.first, r.slope_other, None)
    send(6, 12)
    weight_blocks(r.grads_own, 2, r.first, r.slope_own, None)
    rounds.advance(3)
    branch_wait.wait_recv()

    dq = r.hidden_own.at[:, pl.ds(0, both)]
    dk = r.hidden_own.at[:, pl.ds(both, both)]
    dv = r.hidden_other.at[:, pl.ds(0, both)]
    gc = r.hidden_other.at[:, pl.ds(both, both)]

    def context_back(block, _):
        gc[block, :] = dg(r.feed[block, :], pairs_of(3), NT).astype(BF16)

    each(0, rows, chunk, context_back)

    def back_half(j, _):
        lanes = pair_lanes(j)
        at = pl.ds(2 * LEN, HALF)
        stats = [r.lse[pl.ds(j * 2 + h, 1), at] for h in range(2)]
        block = pl.ds(c_start, HALF)
        d_q, d_k, d_v = pair_back(
            r.q[block, lanes], r.kc[:, lanes], r.vc[:, lanes], gc[block, lanes], r.bias[:, at], stats
        )
        dq[block, lanes] = d_q
        dk[block, lanes] = d_k[:HALF]
        dv[block, lanes] = d_v[:HALF]
        r.away[0, :, lanes] = d_k[HALF:]
        r.away[1, :, lanes] = d_v[HALF:]
        return 0

    lax.fori_loop(0, PAIRS, back_half, 0)
    rounds.advance(4)

    grad_out = dg(r.ctx[...], r.feed[...], TN).astype(BF16)
    for j in range(PAIRS):
        for shard, target in ((0, r.grads_own), (1, r.grads_other)):
            lane = (2 * j + shard) * HD
            target[5, 1, j] = grad_out[lane : lane + HD].reshape(4, HD // 4, wide)

    def back_whole(j):
        def body(i, _):
            lanes = pair_lanes(j)
            block = at_rows(side * HALF + i * LEN, LEN)
            at = pl.ds(pl.multiple_of(i * LEN, LEN), LEN)
            stats = [r.lse[pl.ds(j * 2 + h, 1), at] for h in range(2)]
            d_q, d_k, d_v = pair_back(
                r.q[block, lanes], r.k[block, lanes], r.v[block, lanes], gc[block, lanes], r.bias[:, at], stats
            )
            dq[block, lanes] = d_q
            dk[block, lanes] = d_k
            dv[block, lanes] = d_v
            return 0

        lax.fori_loop(0, 2, body, 0)

    def weight_pair(j):
        lanes = pair_lanes(j)
        left = jnp.concatenate([dq[:, lanes], dk[:, lanes], dv[:, lanes]], axis=1)
        value = dg(left, r.x_rows[pl.ds(0, rows), :], TN)
        far_left = jnp.concatenate([r.away[0, :, lanes], r.away[1, :, lanes]], axis=1)
        far = dg(far_left, r.x_rows[pl.ds(rows, HALF), :], TN)
        first = value[: 2 * HD].astype(BF16)
        rest = (value[2 * HD :] + far).astype(BF16)
        at = 12 + 2 * j
        for shard, target in ((0, r.grads_own), (1, r.grads_other)):
            cut = slice(shard * HD, (shard + 1) * HD)
            pieces = [v[cut].reshape(4, HD // 4, wide) for v in (first, rest[: 2 * HD], rest[2 * HD :])]
            target[4, 0, j] = pieces[0]
            target[4, 1, j] = pieces[1]
            target[5, 0, j] = pieces[2]
        rounds.y_start(at)
        rounds.y_start(at + 1)

    def back_pair(j, _):
        back_whole(j)
        rounds.advance(5 + 2 * j, 5)
        weight_pair(j)
        rounds.advance(6 + 2 * j, 6)
        return 0

    lax.fori_loop(0, PAIRS, back_pair, 0)

    rounds.advance(11)

    def bias_sum(*grads):
        total = sum(column_sum(part) for part in grads)
        heads = [total[:, i * HD : (i + 1) * HD] for i in range(2 * PAIRS)]
        return jnp.concatenate(heads[0::2], axis=1), jnp.concatenate(heads[1::2], axis=1)

    sums = (sum_b_output, sum_first_gain, sum_first_shift, sum_b_outer, sum_second_gain, sum_second_shift)
    for t in range(PARTS):
        shares = [value[:, t * width : (t + 1) * width] for value in sums]
        r.tiny[t, 0:1, :] = jnp.concatenate(shares[:4], axis=1)
        r.tiny[t, 1:2, :] = jnp.concatenate(shares[4:] + [jnp.zeros((1, 2 * width), F32)], axis=1)
        r.tiny[t, 2:3, :] = jnp.zeros((1, units), F32)
    queries, values = bias_sum(dq[...].astype(F32)), bias_sum(dv[...].astype(F32), r.away[1].astype(F32))
    for target, n, inner in ((place, 0, sum_own), ((place + 2) % 4, 1, sum_other)):
        r.tiny[target, 1:2, 2 * width :] = jnp.concatenate([queries[n], values[n]], axis=1)
        r.tiny[target, 2:3, :] = inner
    tiny_copies = []
    for step in (1, 2, 3):
        peer = (place + step) % 4
        out, into = r.i_out.at[step - 1], r.i_in.at[step - 1]
        tiny_copies.append(rounds.start(remote(r.tiny.at[peer], r.tiny_side.at[step - 1], out, into, {"tensor": peer})))

    def input_rows(block, local, away):
        value = dg(dq[block, :], pairs_of(0))
        value = value + dg(dk[block, :], pairs_of(1))
        return value + dg(dv[block, :], pairs_of(2))

    r.far_part[...] = (dg(r.away[0], pairs_of(1)) + dg(r.away[1], pairs_of(2))).astype(BF16)
    give = at_rows((1 - core) * quarter, quarter)
    keep = at_rows(core * quarter, quarter)
    far_trade = rounds.start(
        remote(r.far_part.at[give], r.far_half, r.s_out.at[4], r.s_in.at[4], core_peer)
    )
    rounds.advance(12)
    far_trade.wait_recv()
    r.far_send[...] = (r.far_part[keep, :].astype(F32) + r.far_half[...].astype(F32)).astype(BF16)
    owner = {"tensor": (1 - side) * 2 + side}
    rounds.start(remote(r.far_send, r.far_in.at[core], r.o_out, r.o_in.at[core], owner))

    trade_rows(input_rows, keep_first)
    rounds.advance(13)

    total = r.tiny[place]
    for step in (1, 2, 3):
        tiny_copies[step - 1].wait_recv()
        total = total + r.tiny_side[step - 1]
    r.tiny_all[0] = total

    def tell(step, _):
        peer = {"dp": (group + step) % groups}
        remote(r.tiny_all.at[0], r.tiny_all.at[step], r.d_out.at[step], r.d_in.at[step], peer).start()
        return 0

    lax.fori_loop(1, groups, tell, 0)

    def pump(n, _):
        rounds.advance(n, 14)
        return 0

    lax.fori_loop(14, PIECES, pump, 0)
    rounds.advance(PIECES)

    for n in range(PIECES + 1, PIECES + LAGS[0] - 2):
        rounds.advance(n)

    @pl.when(core == 1 - side)
    def _():
        start = (1 - side) * (own_rows - HALF)
        for n in range(2):
            remote(r.far_send, r.far_in.at[n], r.o_out, r.o_in.at[n], owner).wait_recv()
            block = at_rows(start + n * quarter, quarter)
            r.second[block, :] = r.second[block, :] + r.far_in[n].astype(F32)

    def finish(block, local):
        r.grad_tokens[local, :] = (r.second[local, :] + r.partial_in[local, :].astype(F32)).astype(BF16)

    each(mine, own_rows, strip, finish)

    for n in range(PIECES + LAGS[0] - 2, PIECES + LAGS[0]):
        rounds.advance(n)

    def hear(step, total):
        peer = {"dp": (group + step) % groups}
        copy = remote(r.tiny_all.at[0], r.tiny_all.at[step], r.d_out.at[step], r.d_in.at[step], peer)
        copy.wait()
        return total + r.tiny_all[step]

    r.small[0:3, :] = lax.fori_loop(1, groups, hear, r.tiny_all[0])
    r.small[3:8, :] = jnp.zeros((5, wide), F32)

    rounds.finish()


def layer(groups, named):
    dma = pltpu.SemaphoreType.DMA
    own_rows, wide = named["tokens"].shape
    units = named["w_inner"].shape[1]
    heads = named["w_query"].shape
    rows, both = 2 * own_rows, 2 * heads[0] * heads[1]
    more = groups // OWNERS
    share = wide // 6 // OWNERS
    bands = (6, 2, 3, 4, share, wide)
    outs = dict(
        output=((own_rows, wide), BF16),
        grad_tokens=((own_rows, wide), BF16),
        total=(bands, BF16),
        small=((8, wide), F32),
    )
    room = dict(
        x_rows=((rows + HALF, wide), BF16),
        w_att=((4, PAIRS, 2, HD, wide), BF16),
        in_own=((wide, units), BF16),
        in_other=((wide, units), BF16),
        down_own=((units, wide), BF16),
        down_other=((units, wide), BF16),
        vectors=((8, wide), F32),
        biases=((8, wide), F32),
        biases_other=((8, wide), F32),
        narrow=((8, both // 2), F32),
        narrow_other=((8, both // 2), F32),
        segments=((8, LEN), jnp.int32),
        bias=((LEN, rows), F32),
        q=((rows, both), BF16),
        k=((rows + HALF, both), BF16),
        v=((rows + HALF, both), BF16),
        kc=((LEN, both), BF16),
        vc=((LEN, both), BF16),
        ctx=((rows, both), BF16),
        lse=((8, rows), F32),
        partial=((own_rows, wide), BF16),
        partial_in=((own_rows, wide), BF16),
        acc=((own_rows, wide), F32),
        inverse=((own_rows, 1), F32),
        first=((rows, wide), BF16),
        hidden_own=((rows, units), BF16),
        hidden_other=((rows, units), BF16),
        slope_own=((rows, units), BF16),
        slope_other=((rows, units), BF16),
        second=((own_rows, wide), F32),
        spare=((own_rows, wide), F32),
        feed=((rows, wide), BF16),
        away=((2, HALF, both), BF16),
        far_part=((HALF, wide), BF16),
        far_half=((HALF // 2, wide), BF16),
        far_send=((HALF // 2, wide), BF16),
        far_in=((2, HALF // 2, wide), BF16),
        grads_own=(bands, BF16),
        grads_other=(bands, BF16),
        from_side=(bands, BF16),
        from_x=((6, 3, 4, share, wide), BF16),
        from_z=((6, 3, 3, share, wide), BF16),
        from_far=((PIECES, more - 1, share, wide) if more > 1 else (1, 1, 16, 128), BF16),
        tiny=((PARTS, 3, wide), F32),
        tiny_side=((3, 3, wide), F32),
        tiny_all=((groups, 3, wide), F32),
    )
    sems = dict(
        l_sem=(22,),
        s_out=(6,),
        s_in=(6,),
        w_out_sem=(12,),
        w_in_sem=(12,),
        p_out_sem=(12,),
        p_in_sem=(12,),
        t_out=(4,),
        t_in=(4,),
        a_out=(3,),
        a_in=(3,),
        y_out=(PIECES,),
        y_in=(PIECES,),
        x_out=(PIECES,),
        x_in=(PIECES,),
        z_out=(PIECES, 3),
        z_in=(PIECES, 3),
        g_out=(PIECES, 3),
        g_in=(PIECES, 3),
        h_out=(PIECES,),
        h_in=(PIECES,),
        f_out=(PIECES, max(more - 1, 1)),
        f_in=(PIECES, max(more - 1, 1)),
        i_out=(3,),
        i_in=(3,),
        d_out=(groups,),
        d_in=(groups,),
        o_out=(),
        o_in=(2,),
    )
    names = list(named) + list(outs) + list(room) + list(sems)
    in_vmem = pl.BlockSpec(memory_space=pltpu.VMEM)
    spaces = {"lengths": pltpu.SMEM}
    results = pl.pallas_call(
        functools.partial(layer_kernel, groups, names),
        out_shape=[jax.ShapeDtypeStruct(*spec) for spec in outs.values()],
        in_specs=[pl.BlockSpec(memory_space=spaces.get(name, pl.ANY)) for name in named],
        out_specs=[in_vmem] * len(outs),
        scratch_shapes=[pltpu.VMEM(*spec) for spec in room.values()] + [dma(shape) for shape in sems.values()],
        compiler_params=pltpu.CompilerParams(
            collective_id=0, has_side_effects=True, vmem_limit_bytes=67043328
        ),
    )(*named.values())
    return dict(zip(outs, results))


def last_kernel(total, output, grad_tokens, small, *refs):
    results, (low, full, rows, sums, narrow, load_sem, store_sem) = refs[:17], refs[17:]
    loads = [pltpu.make_async_copy(small, sums, load_sem.at[14])]
    loads += [pltpu.make_async_copy(source, rows.at[i], load_sem.at[12 + i]) for i, source in enumerate((output, grad_tokens))]
    loads += [pltpu.make_async_copy(total.at[i], low.at[i], load_sem.at[i]) for i in range(12)]
    for copy in loads:
        copy.start()
    stores = []

    def store(source, target):
        stores.append(pltpu.make_async_copy(source, target, store_sem.at[len(stores)]))
        stores[-1].start()

    loads[0].wait()
    width = narrow.shape[1]
    for i in range(8):
        lane = i % 4 * width
        narrow[i : i + 1, :] = sums[i // 4 : i // 4 + 1, lane : lane + width]
        store(narrow.at[i], results[8 + i])
    store(sums.at[2], results[16])
    for i in range(2):
        loads[1 + i].wait()
        store(rows.at[i], results[i])
    count = low.shape[1]
    for i in range(12):
        loads[3 + i].wait()
        full[i] = low[i].astype(F32)
        target = results[2 + i // 4].at[pl.ds(i % 4 * count, count)] if i < 8 else results[4 + i - 8]
        store(full.at[i], target)
    for copy in stores:
        copy.wait()


def last(done):
    own_rows, wide = done["output"].shape
    total = done["total"].reshape(12, -1, wide)
    count = total.shape[1]
    rows = jax.ShapeDtypeStruct((own_rows, wide), BF16)
    large = jax.ShapeDtypeStruct((4 * count, wide), F32)
    slim = jax.ShapeDtypeStruct((count, wide), F32)
    outs = [rows] * 2 + [large] * 2 + [slim] * 4
    outs += [jax.ShapeDtypeStruct((wide // PARTS,), F32)] * 8 + [jax.ShapeDtypeStruct((wide,), F32)]
    anywhere = pl.BlockSpec(memory_space=pl.ANY)
    return pl.pallas_call(
        last_kernel,
        out_shape=outs,
        in_specs=[anywhere] * 4,
        out_specs=[anywhere] * len(outs),
        scratch_shapes=[
            pltpu.VMEM(total.shape, BF16),
            pltpu.VMEM(total.shape, F32),
            pltpu.VMEM((2, own_rows, wide), BF16),
            pltpu.VMEM((8, wide), F32),
            pltpu.VMEM((8, wide // PARTS), F32),
            pltpu.SemaphoreType.DMA((15,)),
            pltpu.SemaphoreType.DMA((23,)),
        ],
        compiler_params=pltpu.CompilerParams(vmem_limit_bytes=67043328),
    )(total, done["output"], done["grad_tokens"], done["small"])


def shards(
    tokens,
    segment_ids,
    lengths,
    w_query,
    b_query,
    w_key,
    w_value,
    b_value,
    w_output,
    b_output,
    first_gain,
    first_shift,
    w_inner,
    b_inner,
    w_outer,
    b_outer,
    second_gain,
    second_shift,
    cotangent,
):
    groups = lax.axis_size("dp")
    wide, width = w_query.shape
    units = w_inner.shape[1]
    by_head = (width // HD, HD, wide)
    done = layer(
        groups,
        dict(
            tokens=tokens,
            w_query=w_query.T.reshape(by_head),
            w_key=w_key.T.reshape(by_head),
            w_value=w_value.T.reshape(by_head),
            w_output=w_output.reshape(by_head),
            w_inner=w_inner,
            w_outer=w_outer,
            cotangent=cotangent,
            b_query=b_query,
            b_value=b_value,
            b_inner=b_inner,
            b_output=b_output,
            first_gain=first_gain,
            first_shift=first_shift,
            b_outer=b_outer,
            second_gain=second_gain,
            second_shift=second_shift,
            segment_ids=segment_ids,
            lengths=lengths,
        ),
    )
    output, grad_tokens, outer, inner, query, key, value, out, *shares, inner_shift = last(done)
    return (
        output,
        grad_tokens,
        query.T,
        shares[6],
        key.T,
        value.T,
        shares[7],
        out,
        shares[0],
        shares[1],
        shares[2],
        inner,
        inner_shift,
        outer,
        shares[3],
        shares[4],
        shares[5],
    )


def solution(mesh):
    in_specs = (
        P(("dp", "tensor"), None),
        P("dp"),
        P("dp"),
        P(None, "tensor"),
        P("tensor"),
        P(None, "tensor"),
        P(None, "tensor"),
        P("tensor"),
        P("tensor", None),
        P(),
        P(),
        P(),
        P(None, "tensor"),
        P("tensor"),
        P("tensor", None),
        P(),
        P(),
        P(),
        P(("dp", "tensor"), None),
    )
    out_specs = (
        P(("dp", "tensor"), None),
        P(("dp", "tensor"), None),
        P(None, "tensor"),
        P("tensor"),
        P(None, "tensor"),
        P(None, "tensor"),
        P("tensor"),
        P("tensor", None),
        P("tensor"),
        P("tensor"),
        P("tensor"),
        P(None, "tensor"),
        P("tensor"),
        P("tensor", None),
        P("tensor"),
        P("tensor"),
        P("tensor"),
    )
    return jax.shard_map(shards, mesh=mesh, in_specs=in_specs, out_specs=out_specs, check_vma=False)
```

```python
import functools
import math
import types

import jax
import jax.numpy as jnp
from jax import lax
from jax.experimental import pallas as pl
from jax.experimental.pallas import tpu as pltpu
from jax.sharding import PartitionSpec as P

HD = 64
LEN = 512
HALF = LEN // 2
EPSILON = 1e-12
NEGATIVE = -1000000000.0
SCALE = 1.0 / math.sqrt(HD)
LOG2E = math.log2(math.e)
F32 = jnp.float32
BF16 = jnp.bfloat16
NN = (((1,), (0,)), ((), ()))
NT = (((1,), (1,)), ((), ()))
TN = (((0,), (0,)), ((), ()))
MESH = pl.DeviceIdType.MESH
PARTS = 4
OWNERS = 8
PAIRS = 3
PIECES = 18
LAGS = (6, 4, 2, 0)


def dg(left, right, dims=NN):
    return lax.dot_general(left, right, dims, preferred_element_type=F32)


def normalize(value):
    average = jnp.mean(value, axis=-1, keepdims=True)
    centered = value - average
    variance = jnp.mean(centered * centered, axis=-1, keepdims=True)
    inverse = lax.rsqrt(variance + EPSILON)
    return centered * inverse, inverse


def norm_backward(grad, unit, inverse, gain):
    scaled = grad * gain
    first_mean = jnp.mean(scaled, axis=-1, keepdims=True)
    second_mean = jnp.mean(scaled * unit, axis=-1, keepdims=True)
    return inverse * (scaled - first_mean - unit * second_mean)


def gelu_and_slope(inner):
    cumulative = 0.5 * (1.0 + lax.erf(inner * (1.0 / math.sqrt(2.0))))
    slope = cumulative + inner * jnp.exp(-0.5 * inner * inner) * (1.0 / math.sqrt(2.0 * math.pi))
    return inner * cumulative, slope


def column_sum(value):
    return jnp.sum(value, axis=0, keepdims=True)


def attend_front(q, k, v, bias):
    logits = dg(k, q, NT) * (SCALE * LOG2E) + bias
    peak = jnp.max(logits, axis=0, keepdims=True)
    powers = jnp.exp2(logits - peak)
    total = jnp.sum(powers, axis=0, keepdims=True)
    weights = (powers * (1.0 / total)).astype(BF16)
    return dg(weights, v, TN).astype(BF16), peak + jnp.log2(total)


def attend_back(q, k, v, g, bias, row):
    logits = dg(k, q, NT) * (SCALE * LOG2E) + bias
    probs = jnp.exp2(logits - row)
    dprobs = dg(v, g, NT)
    across = jnp.sum(probs * dprobs, axis=0, keepdims=True)
    dscores = (probs * (dprobs - across) * SCALE).astype(BF16)
    dv = dg(probs.astype(BF16), g, NN).astype(BF16)
    dk = dg(dscores, q, NN).astype(BF16)
    dq = dg(dscores, k, TN).astype(BF16)
    return dq, dk, dv


def pair_back(q, k, v, g, bias, rows):
    done = []
    for h in range(2):
        cols = slice(h * HD, (h + 1) * HD)
        done.append(attend_back(q[:, cols], k[:, cols], v[:, cols], g[:, cols], bias, rows[h]))
    return [jnp.concatenate([done[0][i], done[1][i]], axis=1) for i in range(3)]


def swap_halves(value):
    return jnp.concatenate([value[:, HD:], value[:, :HD]], axis=1)


def pair_lanes(j):
    return pl.ds(pl.multiple_of(j * 2 * HD, 2 * HD), 2 * HD)


def remote(source, target, out, into, device):
    return pltpu.make_async_remote_copy(
        src_ref=source, dst_ref=target, send_sem=out, recv_sem=into, device_id=device, device_id_type=MESH
    )


class Rounds:
    def __init__(self, r, groups):
        self.r = r
        self.place = lax.axis_index("tensor")
        group = lax.axis_index("dp")
        self.x, self.z, self.far = group % 2, (group // 2) % 4, group // OWNERS
        self.more = groups // OWNERS
        self.sent = []

    def dp_at(self, x, z):
        return {"dp": self.far * OWNERS + z * 2 + x}

    def start(self, copy):
        copy.start()
        self.sent.append(copy)
        return copy

    def settle(self, copy):
        copy.wait_send()
        self.sent = [other for other in self.sent if other is not copy]

    @staticmethod
    def where(u):
        if isinstance(u, int):
            return 2 * (u // 6) + u % 2, u % 6 // 2
        return 2 * lax.div(u, 6) + lax.rem(u, 2), lax.div(lax.rem(u, 6), 2)

    def y_copy(self, u):
        r = self.r
        b, j = self.where(u)
        side = {"tensor": (self.place + 2) % 4}
        both = pl.ds(0, 2)
        return remote(r.grads_other.at[b, both, j], r.from_side.at[b, both, j], r.y_out.at[u], r.y_in.at[u], side)

    def x_copy(self, u):
        r = self.r
        b, j = self.where(u)
        away = r.grads_own.at[b, 1 - self.x, j]
        return remote(away, r.from_x.at[b, j], r.x_out.at[u], r.x_in.at[u], self.dp_at(1 - self.x, self.z))

    def z_copy(self, u, step):
        r = self.r
        b, j = self.where(u)
        there = (self.z + step) % 4
        away = r.grads_own.at[b, self.x, j, there]
        out, into = r.z_out.at[u, step - 1], r.z_in.at[u, step - 1]
        return remote(away, r.from_z.at[b, j, step - 1], out, into, self.dp_at(self.x, there))

    def f_copy(self, u, step):
        r = self.r
        b, j = self.where(u)
        peer = {"dp": ((self.far + step) % self.more) * OWNERS + self.z * 2 + self.x}
        own = r.grads_own.at[b, self.x, j, self.z]
        return remote(own, r.from_far.at[u, step - 1], r.f_out.at[u, step - 1], r.f_in.at[u, step - 1], peer)

    def g_copy(self, u, step, origin):
        r = self.r
        b, j = self.where(u)
        piece = r.total.at[b, self.x, j, origin]
        out, into = r.g_out.at[u, step - 1], r.g_in.at[u, step - 1]
        return remote(piece, piece, out, into, self.dp_at(self.x, (self.z + step) % 4))

    def h_copy(self, u, half):
        r = self.r
        b, j = self.where(u)
        piece = r.total.at[b, half, j]
        return remote(piece, piece, r.h_out.at[u], r.h_in.at[u], self.dp_at(1 - self.x, self.z))

    def y_start(self, u):
        self.y_copy(u).start()

    def x_start(self, u):
        r = self.r
        b, j = self.where(u)
        self.y_copy(u).wait_recv()
        for half in range(2):
            summed = r.grads_own[b, half, j].astype(F32) + r.from_side[b, half, j].astype(F32)
            r.grads_own[b, half, j] = summed.astype(BF16)
        self.x_copy(u).start()

    def z_start(self, u):
        r = self.r
        b, j = self.where(u)
        self.x_copy(u).wait_recv()
        summed = r.grads_own[b, self.x, j].astype(F32) + r.from_x[b, j].astype(F32)
        r.grads_own[b, self.x, j] = summed.astype(BF16)
        for step in (1, 2, 3):
            self.z_copy(u, step).start()

    def g_start(self, u):
        r = self.r
        b, j = self.where(u)
        value = r.grads_own[b, self.x, j, self.z].astype(F32)
        for step in (1, 2, 3):
            self.z_copy(u, step).wait_recv()
            value = value + r.from_z[b, j, step - 1].astype(F32)
        if self.more > 1:
            r.grads_own[b, self.x, j, self.z] = value.astype(BF16)
            for step in range(1, self.more):
                self.f_copy(u, step).start()
            for step in range(1, self.more):
                self.f_copy(u, step).wait_recv()
                value = value + r.from_far[u, step - 1].astype(F32)
        r.total[b, self.x, j, self.z] = value.astype(BF16)
        for step in (1, 2, 3):
            self.g_copy(u, step, self.z).start()

    def h_start(self, u):
        for step in (1, 2, 3):
            self.g_copy(u, step, (self.z - step + 4) % 4).wait_recv()
        self.h_copy(u, self.x).start()

    def advance(self, n, least=0):
        stages = (self.h_start, self.g_start, self.z_start, self.x_start)
        for behind, stage in zip(LAGS, stages):
            if isinstance(n, int):
                if 0 <= n - behind < PIECES:
                    stage(n - behind)
            elif least >= behind:
                stage(n - behind)
            else:
                pl.when(n >= behind)(functools.partial(stage, n - behind))

    def finish(self):
        def settle(u, _):
            self.h_copy(u, 1 - self.x).wait_recv()
            for copy in (self.y_copy(u), self.x_copy(u), self.h_copy(u, self.x)):
                copy.wait_send()
            for step in (1, 2, 3):
                self.z_copy(u, step).wait_send()
                self.g_copy(u, step, self.z).wait_send()
            for step in range(1, self.more):
                self.f_copy(u, step).wait_send()
            return 0

        lax.fori_loop(0, PIECES, settle, 0)
        for copy in self.sent:
            copy.wait_send()


def layer_kernel(groups, names, *refs):
    r = types.SimpleNamespace(**dict(zip(names, refs)))
    place = lax.axis_index("tensor")
    group = lax.axis_index("dp")
    core, side = place % 2, place // 2
    rows = r.q.shape[0]
    own_rows = rows // 2
    wide = r.x_rows.shape[1]
    both = r.q.shape[1]
    width = both // 2
    units = r.w_inner.shape[1]
    chunk = own_rows // 2
    strip = own_rows // 8
    mine = core * own_rows
    theirs = (1 - core) * own_rows
    c_start = pl.multiple_of((1 - side) * 2 * LEN, HALF)
    core_peer = {"tensor": place + 1 - 2 * core}
    side_peer = {"tensor": (place + 2) % 4}

    barrier = pltpu.get_barrier_semaphore()
    for step in (1, 2, 3):
        pl.semaphore_signal(barrier, inc=1, device_id={"tensor": (place + step) % 4}, device_id_type=MESH)

    def greet(step, _):
        peer = (group + step) % groups
        pl.semaphore_signal(barrier, inc=1, device_id={"dp": peer}, device_id_type=MESH)
        return 0

    lax.fori_loop(1, groups, greet, 0)

    def at_rows(start, count):
        return pl.ds(pl.multiple_of(start, 16), count)

    own_at = at_rows(mine, own_rows)
    loads = {}
    sources = [
        ("tokens", r.tokens, r.x_rows.at[own_at]),
        ("q", r.w_query, r.w_att.at[0, :, 0]),
        ("k", r.w_key, r.w_att.at[1, :, 0]),
        ("v", r.w_value, r.w_att.at[2, :, 0]),
        ("o", r.w_output, r.w_att.at[3, :, 0]),
        ("in", r.w_inner, r.in_own),
        ("down", r.w_outer, r.down_own),
        ("cotangent", r.cotangent, r.grad_tokens),
    ]
    sources += [("shift", r.b_query, r.narrow.at[0]), ("shift", r.b_value, r.narrow.at[1])]
    sources += [("shift", r.b_inner, r.biases.at[0])]
    gains = (r.b_output, r.first_gain, r.first_shift, r.b_outer, r.second_gain, r.second_shift)
    sources += [("gain", ref, r.vectors.at[i]) for i, ref in enumerate(gains)]
    sources += [("segment", r.segment_ids.at[pl.ds(i * LEN, LEN)], r.segments.at[i]) for i in range(5)]
    for n, (name, source, target) in enumerate(sources):
        copy = pltpu.make_async_copy(source, target, r.l_sem.at[n])
        copy.start()
        loads.setdefault(name, []).append(copy)

    def loaded(*wanted):
        for name in wanted:
            for copy in loads[name]:
                copy.wait()

    pl.semaphore_wait(barrier, 3 + groups - 1)
    rounds = Rounds(r, groups)
    x, z = rounds.x, rounds.z
    x_peer = rounds.dp_at(1 - x, z)

    lanes = wide // 2
    block = units // 8

    def by_heads(source, i):
        def view(ref, half):
            return ref.at[:, :, pl.ds(half * lanes, lanes)]

        return source, r.w_att.at[i, :, 1], view

    def by_rows(source, target, n):
        def view(ref, half):
            return ref.at[at_rows((half * 4 + n) * block, block)]

        return source, target, view

    fetches = [by_heads(w, i) for i, w in enumerate((r.w_query, r.w_key, r.w_value, r.w_output))]
    fetches += [by_rows(r.w_inner, r.in_other, n) for n in range(4)]
    fetches += [by_rows(r.w_outer, r.down_other, n) for n in range(4)]

    def fetch_copy(n):
        source, target, view = fetches[n]
        return remote(view(source, x), view(target, x), r.w_out_sem.at[n], r.w_in_sem.at[n], side_peer)

    def pass_copy(n, which):
        _, target, view = fetches[n]
        return remote(view(target, which), view(target, which), r.p_out_sem.at[n], r.p_in_sem.at[n], x_peer)

    def fetch(*which):
        for n in which:
            rounds.start(fetch_copy(n))

    def hand_on(*which):
        for n in which:
            fetch_copy(n).wait_recv()
            rounds.start(pass_copy(n, x))

    def fetched(*which):
        for n in which:
            pass_copy(n, 1 - x).wait_recv()

    token_copy = rounds.start(remote(r.tokens, r.x_rows.at[own_at], r.s_out.at[0], r.s_in.at[0], core_peer))
    token_wait = remote(r.tokens, r.x_rows.at[at_rows(theirs, own_rows)], r.s_out.at[0], r.s_in.at[0], core_peer)
    fetch(0, 1, 2)
    loaded("shift")
    vector_copies = [
        rounds.start(remote(r.biases, r.biases_other, r.s_out.at[1], r.s_in.at[1], side_peer)),
        rounds.start(remote(r.narrow, r.narrow_other, r.s_out.at[5], r.s_in.at[5], side_peer)),
    ]

    def project(shard, which, start, count, size):
        shifts = (r.narrow, r.narrow_other)[shard]
        for i in which:
            target = (r.q, r.k, r.v)[i]
            weights = r.w_att[i, :, shard].reshape(width, wide)

            def body(n, _):
                block = at_rows(start + n * size, size)
                value = dg(r.x_rows[block, :], weights, NT)
                if i == 0:
                    value = value + shifts[0:1, :]
                if i == 2:
                    value = value + shifts[1:2, :]
                value = value.astype(BF16)
                for j in range(PAIRS):
                    lane = (2 * j + shard) * HD
                    target[block, lane : lane + HD] = value[:, j * HD : (j + 1) * HD]
                return 0

            lax.fori_loop(0, count // size, body, 0)

    loaded("tokens")
    loaded("q", "k", "v")
    project(0, (0, 1, 2), mine, own_rows, chunk)

    token_wait.wait_recv()
    quarter = HALF // 2
    far_at = at_rows(rows + core * quarter, quarter)
    far_there = at_rows(rows + (1 - core) * quarter, quarter)
    near_at = at_rows(c_start + core * quarter, quarter)
    far_copy = rounds.start(
        remote(r.x_rows.at[near_at], r.x_rows.at[far_at], r.s_out.at[2], r.s_in.at[2], side_peer)
    )
    fetch(*range(3, 12))
    project(0, (0, 1, 2), theirs, own_rows, chunk)
    hand_on(0)

    loaded("segment")

    def mask_block(at, row, places, length, count):
        column = jnp.transpose(jnp.broadcast_to(row.astype(F32), (128, LEN)))[:, 0:1]
        same = column == row.astype(F32)[:, :count]
        live = places < length
        first = lax.broadcasted_iota(jnp.int32, (LEN, count), 0)
        second = lax.broadcasted_iota(jnp.int32, (LEN, count), 1)
        allowed = same & live | (first == second)
        r.bias[:, at : at + count] = jnp.where(allowed, 0.0, NEGATIVE)

    ahead = lax.broadcasted_iota(jnp.int32, (LEN, 1), 0)
    for which in range(2):
        index = 3 * side + which
        mask_block(which * LEN, r.segments[pl.ds(index, 1), :], ahead, r.lengths[index], LEN)
    near = r.segments[2:3, pl.ds(pl.multiple_of(side * HALF, HALF), HALF)]
    away_row = r.segments[2:3, pl.ds(pl.multiple_of((1 - side) * HALF, HALF), HALF)]
    turned = jnp.where(ahead < HALF, ahead + side * HALF, ahead - side * HALF)
    mask_block(2 * LEN, jnp.concatenate([near, away_row], axis=1), turned, r.lengths[2], HALF)
    hand_on(1)

    def front_store(shard, block, lanes, out):
        if shard == 0:
            r.ctx[block, lanes] = jnp.concatenate([out, jnp.zeros_like(out)], axis=1)
        else:
            r.ctx[block, lanes] = jnp.concatenate([r.ctx[block, lanes][:, :HD], out], axis=1)

    def front_whole(shard, first_pair, last_pair):
        cols = slice(shard * HD, (shard + 1) * HD)

        def body(j, _):
            lanes = pair_lanes(j)
            for i in range(2):
                block = at_rows(side * HALF + i * LEN, LEN)
                at = pl.ds(i * LEN, LEN)
                out, row = attend_front(
                    r.q[block, lanes][:, cols], r.k[block, lanes][:, cols], r.v[block, lanes][:, cols], r.bias[:, at]
                )
                front_store(shard, block, lanes, out)
                r.lse[pl.ds(2 * j + shard, 1), at] = row
            return 0

        lax.fori_loop(first_pair, last_pair, body, 0)

    def front_half():
        def body(j, _):
            lanes = pair_lanes(j)
            block = pl.ds(c_start, HALF)
            at = pl.ds(2 * LEN, HALF)
            q, k, v = r.q[block, lanes], r.kc[:, lanes], r.vc[:, lanes]
            outs = []
            for shard in range(2):
                cols = slice(shard * HD, (shard + 1) * HD)
                out, row = attend_front(q[:, cols], k[:, cols], v[:, cols], r.bias[:, at])
                outs.append(out)
                r.lse[pl.ds(2 * j + shard, 1), at] = row
            r.ctx[block, lanes] = jnp.concatenate(outs, axis=1)
            return 0

        lax.fori_loop(0, PAIRS, body, 0)

    front_whole(0, 0, 2)
    hand_on(2)
    front_whole(0, 2, 3)
    far_copy.wait_recv()
    far_pass = rounds.start(
        remote(r.x_rows.at[far_at], r.x_rows.at[far_at], r.s_out.at[3], r.s_in.at[3], core_peer)
    )
    far_wait = remote(r.x_rows.at[far_there], r.x_rows.at[far_there], r.s_out.at[3], r.s_in.at[3], core_peer)
    for copy in vector_copies:
        copy.wait_recv()
    fetched(0)
    project(1, (0,), 0, rows, chunk)
    fetched(1)
    project(1, (1,), 0, rows, chunk)
    hand_on(3)
    fetched(2)
    project(1, (2,), 0, rows, chunk)
    far_wait.wait_recv()
    for shard in range(2):
        project(shard, (1, 2), rows, HALF, HALF)
    for own, near_far in ((r.k, r.kc), (r.v, r.vc)):
        near_far[pl.ds(0, HALF), :] = own[pl.ds(c_start, HALF), :]
        near_far[pl.ds(HALF, HALF), :] = own[pl.ds(rows, HALF), :]
    front_whole(1, 0, 2)
    hand_on(4)
    front_whole(1, 2, 3)
    hand_on(5)
    front_half()

    loaded("o")
    fetched(3)

    def pairs_of(i):
        return r.w_att[i].reshape(both, wide)

    def each(start, count, size, body):
        def step(n, _):
            body(at_rows(start + n * size, size), at_rows(n * size, size))
            return 0

        lax.fori_loop(0, count // size, step, 0)

    trades = []

    def trade_rows(compute, keep):
        def away_body(block, local):
            r.partial[local, :] = compute(block, local, True).astype(BF16)

        each(theirs, own_rows, chunk, away_body)
        n = len(trades)
        trades.append(
            rounds.start(remote(r.partial, r.partial_in, r.t_out.at[n], r.t_in.at[n], core_peer))
        )

        def own_body(block, local):
            keep(local, compute(block, local, False))

        each(mine, own_rows, chunk, own_body)
        trades[n].wait_recv()
        rounds.settle(trades[n])

    def gather_rows(ref, n):
        copy = rounds.start(remote(ref.at[own_at], ref.at[own_at], r.a_out.at[n], r.a_in.at[n], core_peer))
        there = ref.at[at_rows(theirs, own_rows)]
        return copy, remote(there, there, r.a_out.at[n], r.a_in.at[n], core_peer)

    def keep_acc(local, value):
        r.acc[local, :] = value

    trade_rows(lambda block, local, away: dg(r.ctx[block, :], pairs_of(3)), keep_acc)
    loaded("gain")
    b_output, first_gain, first_shift = (r.vectors[i : i + 1, :] for i in range(3))
    b_outer, second_gain, second_shift = (r.vectors[i : i + 1, :] for i in range(3, 6))

    def first_norm(block, local):
        value = r.x_rows[block, :].astype(F32) + r.acc[local, :] + r.partial_in[local, :].astype(F32) + b_output
        unit, inverse = normalize(value)
        r.acc[local, :] = unit
        r.inverse[local, :] = inverse
        r.first[block, :] = (unit * first_gain + first_shift).astype(BF16)

    each(mine, own_rows, strip, first_norm)
    first_copy, first_wait = gather_rows(r.first, 0)
    hand_on(6)

    def expand(shard, start, part=None):
        weights = (r.in_own, r.in_other)[shard]
        shifts = (r.biases, r.biases_other)[shard]
        hidden, slope = ((r.hidden_own, r.slope_own), (r.hidden_other, r.slope_other))[shard]

        def body(block, _):
            value, gradient = gelu_and_slope(dg(r.first[block, :], weights[...]) + shifts[0:1, :])
            hidden[block, :] = value.astype(BF16)
            slope[block, :] = gradient.astype(BF16)

        if part is None:
            each(start, own_rows, chunk, body)
        else:
            each(start + part * chunk, chunk, chunk, body)

    loaded("in")
    expand(0, mine)
    hand_on(7)
    first_wait.wait_recv()
    expand(0, theirs, 0)
    hand_on(8)
    expand(0, theirs, 1)
    hand_on(9)
    loaded("down")

    def own_part(target):
        def body(block, local):
            target[local, :] = dg(r.hidden_own[block, :], r.down_own[...])

        return body

    each(theirs, own_rows, chunk, own_part(r.spare))
    hand_on(10)
    each(mine, own_rows, chunk, own_part(r.second))
    hand_on(11)
    fetched(4, 5, 6, 7)
    expand(1, theirs)
    expand(1, mine)
    fetched(8, 9, 10, 11)

    def other_part(block, local, away):
        kept = r.spare if away else r.second
        return kept[local, :] + dg(r.hidden_other[block, :], r.down_other[...])

    def keep_second(local, value):
        r.second[local, :] = value

    trade_rows(other_part, keep_second)
    loaded("cotangent")
    zero = jnp.zeros((1, wide), F32)

    def second_norm(n, carry):
        block, local = at_rows(mine + n * strip, strip), at_rows(n * strip, strip)
        value = r.first[block, :].astype(F32) + r.second[local, :] + r.partial_in[local, :].astype(F32) + b_outer
        unit, inverse = normalize(value)
        r.output[local, :] = (unit * second_gain + second_shift).astype(BF16)
        upstream = r.grad_tokens[local, :].astype(F32)
        grad = norm_backward(upstream, unit, inverse, second_gain)
        r.second[local, :] = grad
        low = grad.astype(BF16)
        r.feed[block, :] = low
        gain, shift, lows = carry
        return gain + column_sum(upstream * unit), shift + column_sum(upstream), lows + column_sum(low.astype(F32))

    sum_second_gain, sum_second_shift, sum_b_outer = lax.fori_loop(
        0, own_rows // strip, second_norm, (zero, zero, zero)
    )
    feed_copy, feed_wait = gather_rows(r.feed, 1)

    def contract(shard, start, carry):
        weights = (r.down_own, r.down_other)[shard]
        slope = (r.slope_own, r.slope_other)[shard]

        def body(n, total):
            block = at_rows(start + n * chunk, chunk)
            value = dg(r.feed[block, :], weights[...], NT) * slope[block, :].astype(F32)
            low = value.astype(BF16)
            slope[block, :] = low
            return total + column_sum(low.astype(F32))

        return lax.fori_loop(0, own_rows // chunk, body, carry)

    sum_own = contract(0, mine, jnp.zeros((1, units), F32))
    sum_other = contract(1, mine, jnp.zeros((1, units), F32))
    feed_wait.wait_recv()

    def weight_blocks(target, band, left, right, first):
        columns = left.shape[1] // 3

        def body(n, _):
            value = dg(left[:, pl.ds(pl.multiple_of(n * columns, 128), columns)], right[...], TN).astype(BF16)
            for i in range(4):
                at = 4 * n + i
                b, h, j = band + lax.div(at, 6), lax.div(lax.rem(at, 6), 3), lax.rem(at, 3)
                target[b, h, j] = value[i * HD : (i + 1) * HD].reshape(4, HD // 4, value.shape[1])
            if first is not None:

                @pl.when(n == 0)
                def _():
                    rounds.y_start(first)

            return 0

        lax.fori_loop(0, 3, body, 0)

    def send(first, last):
        def body(u, _):
            rounds.y_start(u)
            return 0

        lax.fori_loop(first, last, body, 0)

    weight_blocks(r.grads_other, 0, r.hidden_other, r.feed, 0)
    send(1, 6)
    weight_blocks(r.grads_own, 0, r.hidden_own, r.feed, None)
    sum_own = contract(0, theirs, sum_own)
    sum_other = contract(1, theirs, sum_other)
    rounds.advance(0)

    def keep_first(local, value):
        r.second[local, :] = r.second[local, :] + value

    trade_rows(
        lambda block, local, away: dg(r.slope_own[block, :], r.in_own[...], NT) + dg(r.slope_other[block, :], r.in_other[...], NT),
        keep_first,
    )
    rounds.settle(feed_copy)
    rounds.advance(1)

    def first_back(n, carry):
        block, local = at_rows(mine + n * strip, strip), at_rows(n * strip, strip)
        grad_first = r.second[local, :] + r.partial_in[local, :].astype(F32)
        unit = r.acc[local, :]
        grad = norm_backward(grad_first, unit, r.inverse[local, :], first_gain)
        r.second[local, :] = grad
        low = grad.astype(BF16)
        r.feed[block, :] = low
        gain, shift, lows = carry
        return gain + column_sum(grad_first * unit), shift + column_sum(grad_first), lows + column_sum(low.astype(F32))

    sum_first_gain, sum_first_shift, sum_b_output = lax.fori_loop(0, own_rows // strip, first_back, (zero, zero, zero))
    branch_copy, branch_wait = gather_rows(r.feed, 2)
    rounds.advance(2)
    weight_blocks(r.grads_other, 2, r.first, r.slope_other, None)
    send(6, 12)
    weight_blocks(r.grads_own, 2, r.first, r.slope_own, None)
    rounds.advance(3)
    branch_wait.wait_recv()

    dq = r.hidden_own.at[:, pl.ds(0, both)]
    dk = r.hidden_own.at[:, pl.ds(both, both)]
    dv = r.hidden_other.at[:, pl.ds(0, both)]
    gc = r.hidden_other.at[:, pl.ds(both, both)]

    def context_back(block, _):
        gc[block, :] = dg(r.feed[block, :], pairs_of(3), NT).astype(BF16)

    each(0, rows, chunk, context_back)

    def back_half(j, _):
        lanes = pair_lanes(j)
        at = pl.ds(2 * LEN, HALF)
        stats = [r.lse[pl.ds(j * 2 + h, 1), at] for h in range(2)]
        block = pl.ds(c_start, HALF)
        d_q, d_k, d_v = pair_back(
            r.q[block, lanes], r.kc[:, lanes], r.vc[:, lanes], gc[block, lanes], r.bias[:, at], stats
        )
        dq[block, lanes] = d_q
        dk[block, lanes] = d_k[:HALF]
        dv[block, lanes] = d_v[:HALF]
        r.away[0, :, lanes] = d_k[HALF:]
        r.away[1, :, lanes] = d_v[HALF:]
        return 0

    lax.fori_loop(0, PAIRS, back_half, 0)
    rounds.advance(4)

    grad_out = dg(r.ctx[...], r.feed[...], TN).astype(BF16)
    for j in range(PAIRS):
        for shard, target in ((0, r.grads_own), (1, r.grads_other)):
            lane = (2 * j + shard) * HD
            target[5, 1, j] = grad_out[lane : lane + HD].reshape(4, HD // 4, wide)

    def back_whole(j):
        def body(i, _):
            lanes = pair_lanes(j)
            block = at_rows(side * HALF + i * LEN, LEN)
            at = pl.ds(pl.multiple_of(i * LEN, LEN), LEN)
            stats = [r.lse[pl.ds(j * 2 + h, 1), at] for h in range(2)]
            d_q, d_k, d_v = pair_back(
                r.q[block, lanes], r.k[block, lanes], r.v[block, lanes], gc[block, lanes], r.bias[:, at], stats
            )
            dq[block, lanes] = d_q
            dk[block, lanes] = d_k
            dv[block, lanes] = d_v
            return 0

        lax.fori_loop(0, 2, body, 0)

    def weight_pair(j):
        lanes = pair_lanes(j)
        left = jnp.concatenate([dq[:, lanes], dk[:, lanes], dv[:, lanes]], axis=1)
        value = dg(left, r.x_rows[pl.ds(0, rows), :], TN)
        far_left = jnp.concatenate([r.away[0, :, lanes], r.away[1, :, lanes]], axis=1)
        far = dg(far_left, r.x_rows[pl.ds(rows, HALF), :], TN)
        first = value[: 2 * HD].astype(BF16)
        rest = (value[2 * HD :] + far).astype(BF16)
        at = 12 + 2 * j
        for shard, target in ((0, r.grads_own), (1, r.grads_other)):
            cut = slice(shard * HD, (shard + 1) * HD)
            pieces = [v[cut].reshape(4, HD // 4, wide) for v in (first, rest[: 2 * HD], rest[2 * HD :])]
            target[4, 0, j] = pieces[0]
            target[4, 1, j] = pieces[1]
            target[5, 0, j] = pieces[2]
        rounds.y_start(at)
        rounds.y_start(at + 1)

    def back_pair(j, _):
        back_whole(j)
        rounds.advance(5 + 2 * j, 5)
        weight_pair(j)
        rounds.advance(6 + 2 * j, 6)
        return 0

    lax.fori_loop(0, PAIRS, back_pair, 0)

    rounds.advance(11)

    def bias_sum(*grads):
        total = sum(column_sum(part) for part in grads)
        heads = [total[:, i * HD : (i + 1) * HD] for i in range(2 * PAIRS)]
        return jnp.concatenate(heads[0::2], axis=1), jnp.concatenate(heads[1::2], axis=1)

    sums = (sum_b_output, sum_first_gain, sum_first_shift, sum_b_outer, sum_second_gain, sum_second_shift)
    for t in range(PARTS):
        shares = [value[:, t * width : (t + 1) * width] for value in sums]
        r.tiny[t, 0:1, :] = jnp.concatenate(shares[:4], axis=1)
        r.tiny[t, 1:2, :] = jnp.concatenate(shares[4:] + [jnp.zeros((1, 2 * width), F32)], axis=1)
        r.tiny[t, 2:3, :] = jnp.zeros((1, units), F32)
    queries, values = bias_sum(dq[...].astype(F32)), bias_sum(dv[...].astype(F32), r.away[1].astype(F32))
    for target, n, inner in ((place, 0, sum_own), ((place + 2) % 4, 1, sum_other)):
        r.tiny[target, 1:2, 2 * width :] = jnp.concatenate([queries[n], values[n]], axis=1)
        r.tiny[target, 2:3, :] = inner
    tiny_copies = []
    for step in (1, 2, 3):
        peer = (place + step) % 4
        out, into = r.i_out.at[step - 1], r.i_in.at[step - 1]
        tiny_copies.append(rounds.start(remote(r.tiny.at[peer], r.tiny_side.at[step - 1], out, into, {"tensor": peer})))

    def input_rows(block, local, away):
        value = dg(dq[block, :], pairs_of(0))
        value = value + dg(dk[block, :], pairs_of(1))
        return value + dg(dv[block, :], pairs_of(2))

    r.far_part[...] = (dg(r.away[0], pairs_of(1)) + dg(r.away[1], pairs_of(2))).astype(BF16)
    give = at_rows((1 - core) * quarter, quarter)
    keep = at_rows(core * quarter, quarter)
    far_trade = rounds.start(
        remote(r.far_part.at[give], r.far_half, r.s_out.at[4], r.s_in.at[4], core_peer)
    )
    rounds.advance(12)
    far_trade.wait_recv()
    r.far_send[...] = (r.far_part[keep, :].astype(F32) + r.far_half[...].astype(F32)).astype(BF16)
    owner = {"tensor": (1 - side) * 2 + side}
    rounds.start(remote(r.far_send, r.far_in.at[core], r.o_out, r.o_in.at[core], owner))

    trade_rows(input_rows, keep_first)
    rounds.advance(13)

    total = r.tiny[place]
    for step in (1, 2, 3):
        tiny_copies[step - 1].wait_recv()
        total = total + r.tiny_side[step - 1]
    r.tiny_all[0] = total

    def tell(step, _):
        peer = {"dp": (group + step) % groups}
        remote(r.tiny_all.at[0], r.tiny_all.at[step], r.d_out.at[step], r.d_in.at[step], peer).start()
        return 0

    lax.fori_loop(1, groups, tell, 0)

    def pump(n, _):
        rounds.advance(n, 14)
        return 0

    lax.fori_loop(14, PIECES, pump, 0)
    rounds.advance(PIECES)

    for n in range(PIECES + 1, PIECES + LAGS[0] - 2):
        rounds.advance(n)

    @pl.when(core == 1 - side)
    def _():
        start = (1 - side) * (own_rows - HALF)
        for n in range(2):
            remote(r.far_send, r.far_in.at[n], r.o_out, r.o_in.at[n], owner).wait_recv()
            block = at_rows(start + n * quarter, quarter)
            r.second[block, :] = r.second[block, :] + r.far_in[n].astype(F32)

    def finish(block, local):
        r.grad_tokens[local, :] = (r.second[local, :] + r.partial_in[local, :].astype(F32)).astype(BF16)

    each(mine, own_rows, strip, finish)

    for n in range(PIECES + LAGS[0] - 2, PIECES + LAGS[0]):
        rounds.advance(n)

    def hear(step, total):
        peer = {"dp": (group + step) % groups}
        copy = remote(r.tiny_all.at[0], r.tiny_all.at[step], r.d_out.at[step], r.d_in.at[step], peer)
        copy.wait()
        return total + r.tiny_all[step]

    r.small[0:3, :] = lax.fori_loop(1, groups, hear, r.tiny_all[0])
    r.small[3:8, :] = jnp.zeros((5, wide), F32)

    rounds.finish()


def layer(groups, named):
    dma = pltpu.SemaphoreType.DMA
    own_rows, wide = named["tokens"].shape
    units = named["w_inner"].shape[1]
    heads = named["w_query"].shape
    rows, both = 2 * own_rows, 2 * heads[0] * heads[1]
    more = groups // OWNERS
    share = wide // 6 // OWNERS
    bands = (6, 2, 3, 4, share, wide)
    outs = dict(
        output=((own_rows, wide), BF16),
        grad_tokens=((own_rows, wide), BF16),
        total=(bands, BF16),
        small=((8, wide), F32),
    )
    room = dict(
        x_rows=((rows + HALF, wide), BF16),
        w_att=((4, PAIRS, 2, HD, wide), BF16),
        in_own=((wide, units), BF16),
        in_other=((wide, units), BF16),
        down_own=((units, wide), BF16),
        down_other=((units, wide), BF16),
        vectors=((8, wide), F32),
        biases=((8, wide), F32),
        biases_other=((8, wide), F32),
        narrow=((8, both // 2), F32),
        narrow_other=((8, both // 2), F32),
        segments=((8, LEN), jnp.int32),
        bias=((LEN, rows), F32),
        q=((rows, both), BF16),
        k=((rows + HALF, both), BF16),
        v=((rows + HALF, both), BF16),
        kc=((LEN, both), BF16),
        vc=((LEN, both), BF16),
        ctx=((rows, both), BF16),
        lse=((8, rows), F32),
        partial=((own_rows, wide), BF16),
        partial_in=((own_rows, wide), BF16),
        acc=((own_rows, wide), F32),
        inverse=((own_rows, 1), F32),
        first=((rows, wide), BF16),
        hidden_own=((rows, units), BF16),
        hidden_other=((rows, units), BF16),
        slope_own=((rows, units), BF16),
        slope_other=((rows, units), BF16),
        second=((own_rows, wide), F32),
        spare=((own_rows, wide), F32),
        feed=((rows, wide), BF16),
        away=((2, HALF, both), BF16),
        far_part=((HALF, wide), BF16),
        far_half=((HALF // 2, wide), BF16),
        far_send=((HALF // 2, wide), BF16),
        far_in=((2, HALF // 2, wide), BF16),
        grads_own=(bands, BF16),
        grads_other=(bands, BF16),
        from_side=(bands, BF16),
        from_x=((6, 3, 4, share, wide), BF16),
        from_z=((6, 3, 3, share, wide), BF16),
        from_far=((PIECES, more - 1, share, wide) if more > 1 else (1, 1, 16, 128), BF16),
        tiny=((PARTS, 3, wide), F32),
        tiny_side=((3, 3, wide), F32),
        tiny_all=((groups, 3, wide), F32),
    )
    sems = dict(
        l_sem=(22,),
        s_out=(6,),
        s_in=(6,),
        w_out_sem=(12,),
        w_in_sem=(12,),
        p_out_sem=(12,),
        p_in_sem=(12,),
        t_out=(4,),
        t_in=(4,),
        a_out=(3,),
        a_in=(3,),
        y_out=(PIECES,),
        y_in=(PIECES,),
        x_out=(PIECES,),
        x_in=(PIECES,),
        z_out=(PIECES, 3),
        z_in=(PIECES, 3),
        g_out=(PIECES, 3),
        g_in=(PIECES, 3),
        h_out=(PIECES,),
        h_in=(PIECES,),
        f_out=(PIECES, max(more - 1, 1)),
        f_in=(PIECES, max(more - 1, 1)),
        i_out=(3,),
        i_in=(3,),
        d_out=(groups,),
        d_in=(groups,),
        o_out=(),
        o_in=(2,),
    )
    names = list(named) + list(outs) + list(room) + list(sems)
    in_vmem = pl.BlockSpec(memory_space=pltpu.VMEM)
    spaces = {"lengths": pltpu.SMEM}
    results = pl.pallas_call(
        functools.partial(layer_kernel, groups, names),
        out_shape=[jax.ShapeDtypeStruct(*spec) for spec in outs.values()],
        in_specs=[pl.BlockSpec(memory_space=spaces.get(name, pl.ANY)) for name in named],
        out_specs=[in_vmem] * len(outs),
        scratch_shapes=[pltpu.VMEM(*spec) for spec in room.values()] + [dma(shape) for shape in sems.values()],
        compiler_params=pltpu.CompilerParams(
            collective_id=0, has_side_effects=True, vmem_limit_bytes=67043328
        ),
    )(*named.values())
    return dict(zip(outs, results))


def last_kernel(total, output, grad_tokens, small, *refs):
    results, (low, full, rows, sums, narrow, load_sem, store_sem) = refs[:17], refs[17:]
    loads = [pltpu.make_async_copy(small, sums, load_sem.at[14])]
    loads += [pltpu.make_async_copy(source, rows.at[i], load_sem.at[12 + i]) for i, source in enumerate((output, grad_tokens))]
    loads += [pltpu.make_async_copy(total.at[i], low.at[i], load_sem.at[i]) for i in range(12)]
    for copy in loads:
        copy.start()
    stores = []

    def store(source, target):
        stores.append(pltpu.make_async_copy(source, target, store_sem.at[len(stores)]))
        stores[-1].start()

    loads[0].wait()
    width = narrow.shape[1]
    for i in range(8):
        lane = i % 4 * width
        narrow[i : i + 1, :] = sums[i // 4 : i // 4 + 1, lane : lane + width]
        store(narrow.at[i], results[8 + i])
    store(sums.at[2], results[16])
    for i in range(2):
        loads[1 + i].wait()
        store(rows.at[i], results[i])
    count = low.shape[1]
    for i in range(12):
        loads[3 + i].wait()
        full[i] = low[i].astype(F32)
        target = results[2 + i // 4].at[pl.ds(i % 4 * count, count)] if i < 8 else results[4 + i - 8]
        store(full.at[i], target)
    for copy in stores:
        copy.wait()


def last(done):
    own_rows, wide = done["output"].shape
    total = done["total"].reshape(12, -1, wide)
    count = total.shape[1]
    rows = jax.ShapeDtypeStruct((own_rows, wide), BF16)
    large = jax.ShapeDtypeStruct((4 * count, wide), F32)
    slim = jax.ShapeDtypeStruct((count, wide), F32)
    outs = [rows] * 2 + [large] * 2 + [slim] * 4
    outs += [jax.ShapeDtypeStruct((wide // PARTS,), F32)] * 8 + [jax.ShapeDtypeStruct((wide,), F32)]
    anywhere = pl.BlockSpec(memory_space=pl.ANY)
    return pl.pallas_call(
        last_kernel,
        out_shape=outs,
        in_specs=[anywhere] * 4,
        out_specs=[anywhere] * len(outs),
        scratch_shapes=[
            pltpu.VMEM(total.shape, BF16),
            pltpu.VMEM(total.shape, F32),
            pltpu.VMEM((2, own_rows, wide), BF16),
            pltpu.VMEM((8, wide), F32),
            pltpu.VMEM((8, wide // PARTS), F32),
            pltpu.SemaphoreType.DMA((15,)),
            pltpu.SemaphoreType.DMA((23,)),
        ],
        compiler_params=pltpu.CompilerParams(vmem_limit_bytes=67043328),
    )(total, done["output"], done["grad_tokens"], done["small"])


def shards(
    tokens,
    segment_ids,
    lengths,
    w_query,
    b_query,
    w_key,
    w_value,
    b_value,
    w_output,
    b_output,
    first_gain,
    first_shift,
    w_inner,
    b_inner,
    w_outer,
    b_outer,
    second_gain,
    second_shift,
    cotangent,
):
    groups = lax.axis_size("dp")
    wide, width = w_query.shape
    units = w_inner.shape[1]
    by_head = (width // HD, HD, wide)
    done = layer(
        groups,
        dict(
            tokens=tokens,
            w_query=w_query.T.reshape(by_head),
            w_key=w_key.T.reshape(by_head),
            w_value=w_value.T.reshape(by_head),
            w_output=w_output.reshape(by_head),
            w_inner=w_inner,
            w_outer=w_outer,
            cotangent=cotangent,
            b_query=b_query,
            b_value=b_value,
            b_inner=b_inner,
            b_output=b_output,
            first_gain=first_gain,
            first_shift=first_shift,
            b_outer=b_outer,
            second_gain=second_gain,
            second_shift=second_shift,
            segment_ids=segment_ids,
            lengths=lengths,
        ),
    )
    output, grad_tokens, outer, inner, query, key, value, out, *shares, inner_shift = last(done)
    return (
        output,
        grad_tokens,
        query.T,
        shares[6],
        key.T,
        value.T,
        shares[7],
        out,
        shares[0],
        shares[1],
        shares[2],
        inner,
        inner_shift,
        outer,
        shares[3],
        shares[4],
        shares[5],
    )


def solution(mesh):
    in_specs = (
        P(("dp", "tensor"), None),
        P("dp"),
        P("dp"),
        P(None, "tensor"),
        P("tensor"),
        P(None, "tensor"),
        P(None, "tensor"),
        P("tensor"),
        P("tensor", None),
        P(),
        P(),
        P(),
        P(None, "tensor"),
        P("tensor"),
        P("tensor", None),
        P(),
        P(),
        P(),
        P(("dp", "tensor"), None),
    )
    out_specs = (
        P(("dp", "tensor"), None),
        P(("dp", "tensor"), None),
        P(None, "tensor"),
        P("tensor"),
        P(None, "tensor"),
        P(None, "tensor"),
        P("tensor"),
        P("tensor", None),
        P("tensor"),
        P("tensor"),
        P("tensor"),
        P(None, "tensor"),
        P("tensor"),
        P("tensor", None),
        P("tensor"),
        P("tensor"),
        P("tensor"),
    )
    return jax.shard_map(shards, mesh=mesh, in_specs=in_specs, out_specs=out_specs, check_vma=False)
```

```python
import functools
import math
import types

import jax
import jax.numpy as jnp
from jax import lax
from jax.experimental import pallas as pl
from jax.experimental.pallas import tpu as pltpu
from jax.sharding import PartitionSpec as P

HD = 64
LEN = 512
HALF = LEN // 2
EPSILON = 1e-12
NEGATIVE = -1000000000.0
SCALE = 1.0 / math.sqrt(HD)
LOG2E = math.log2(math.e)
F32 = jnp.float32
BF16 = jnp.bfloat16
NN = (((1,), (0,)), ((), ()))
NT = (((1,), (1,)), ((), ()))
TN = (((0,), (0,)), ((), ()))
MESH = pl.DeviceIdType.MESH
PARTS = 4
OWNERS = 8
PAIRS = 3
PIECES = 18
LAGS = (6, 4, 2, 0)


def dg(left, right, dims=NN):
    return lax.dot_general(left, right, dims, preferred_element_type=F32)


def normalize(value):
    average = jnp.mean(value, axis=-1, keepdims=True)
    centered = value - average
    variance = jnp.mean(centered * centered, axis=-1, keepdims=True)
    inverse = lax.rsqrt(variance + EPSILON)
    return centered * inverse, inverse


def norm_backward(grad, unit, inverse, gain):
    scaled = grad * gain
    first_mean = jnp.mean(scaled, axis=-1, keepdims=True)
    second_mean = jnp.mean(scaled * unit, axis=-1, keepdims=True)
    return inverse * (scaled - first_mean - unit * second_mean)


def gelu_and_slope(inner):
    cumulative = 0.5 * (1.0 + lax.erf(inner * (1.0 / math.sqrt(2.0))))
    slope = cumulative + inner * jnp.exp(-0.5 * inner * inner) * (1.0 / math.sqrt(2.0 * math.pi))
    return inner * cumulative, slope


def column_sum(value):
    return jnp.sum(value, axis=0, keepdims=True)


def attend_front(q, k, v, bias):
    logits = dg(k, q, NT) * (SCALE * LOG2E) + bias
    peak = jnp.max(logits, axis=0, keepdims=True)
    powers = jnp.exp2(logits - peak)
    total = jnp.sum(powers, axis=0, keepdims=True)
    weights = (powers * (1.0 / total)).astype(BF16)
    return dg(weights, v, TN).astype(BF16), peak + jnp.log2(total)


def attend_back(q, k, v, g, bias, row):
    logits = dg(k, q, NT) * (SCALE * LOG2E) + bias
    probs = jnp.exp2(logits - row)
    dprobs = dg(v, g, NT)
    across = jnp.sum(probs * dprobs, axis=0, keepdims=True)
    dscores = (probs * (dprobs - across) * SCALE).astype(BF16)
    dv = dg(probs.astype(BF16), g, NN).astype(BF16)
    dk = dg(dscores, q, NN).astype(BF16)
    dq = dg(dscores, k, TN).astype(BF16)
    return dq, dk, dv


def pair_back(q, k, v, g, bias, rows):
    done = []
    for h in range(2):
        cols = slice(h * HD, (h + 1) * HD)
        done.append(attend_back(q[:, cols], k[:, cols], v[:, cols], g[:, cols], bias, rows[h]))
    return [jnp.concatenate([done[0][i], done[1][i]], axis=1) for i in range(3)]


def swap_halves(value):
    return jnp.concatenate([value[:, HD:], value[:, :HD]], axis=1)


def pair_lanes(j):
    return pl.ds(pl.multiple_of(j * 2 * HD, 2 * HD), 2 * HD)


def remote(source, target, out, into, device):
    return pltpu.make_async_remote_copy(
        src_ref=source, dst_ref=target, send_sem=out, recv_sem=into, device_id=device, device_id_type=MESH
    )


class Rounds:
    def __init__(self, r, groups):
        self.r = r
        self.place = lax.axis_index("tensor")
        group = lax.axis_index("dp")
        self.x, self.z, self.far = group % 2, (group // 2) % 4, group // OWNERS
        self.more = groups // OWNERS
        self.sent = []

    def dp_at(self, x, z):
        return {"dp": self.far * OWNERS + z * 2 + x}

    def start(self, copy):
        copy.start()
        self.sent.append(copy)
        return copy

    def settle(self, copy):
        copy.wait_send()
        self.sent = [other for other in self.sent if other is not copy]

    @staticmethod
    def where(u):
        if isinstance(u, int):
            return 2 * (u // 6) + u % 2, u % 6 // 2
        return 2 * lax.div(u, 6) + lax.rem(u, 2), lax.div(lax.rem(u, 6), 2)

    def y_copy(self, u):
        r = self.r
        b, j = self.where(u)
        side = {"tensor": (self.place + 2) % 4}
        both = pl.ds(0, 2)
        return remote(r.grads_other.at[b, both, j], r.from_side.at[b, both, j], r.y_out.at[u], r.y_in.at[u], side)

    def x_copy(self, u):
        r = self.r
        b, j = self.where(u)
        away = r.grads_own.at[b, 1 - self.x, j]
        return remote(away, r.from_x.at[b, j], r.x_out.at[u], r.x_in.at[u], self.dp_at(1 - self.x, self.z))

    def z_copy(self, u, step):
        r = self.r
        b, j = self.where(u)
        there = (self.z + step) % 4
        away = r.grads_own.at[b, self.x, j, there]
        out, into = r.z_out.at[u, step - 1], r.z_in.at[u, step - 1]
        return remote(away, r.from_z.at[b, j, step - 1], out, into, self.dp_at(self.x, there))

    def f_copy(self, u, step):
        r = self.r
        b, j = self.where(u)
        peer = {"dp": ((self.far + step) % self.more) * OWNERS + self.z * 2 + self.x}
        own = r.grads_own.at[b, self.x, j, self.z]
        return remote(own, r.from_far.at[u, step - 1], r.f_out.at[u, step - 1], r.f_in.at[u, step - 1], peer)

    def g_copy(self, u, step, origin):
        r = self.r
        b, j = self.where(u)
        piece = r.total.at[b, self.x, j, origin]
        out, into = r.g_out.at[u, step - 1], r.g_in.at[u, step - 1]
        return remote(piece, piece, out, into, self.dp_at(self.x, (self.z + step) % 4))

    def h_copy(self, u, half):
        r = self.r
        b, j = self.where(u)
        piece = r.total.at[b, half, j]
        return remote(piece, piece, r.h_out.at[u], r.h_in.at[u], self.dp_at(1 - self.x, self.z))

    def y_start(self, u):
        self.y_copy(u).start()

    def x_start(self, u):
        r = self.r
        b, j = self.where(u)
        self.y_copy(u).wait_recv()
        for half in range(2):
            summed = r.grads_own[b, half, j].astype(F32) + r.from_side[b, half, j].astype(F32)
            r.grads_own[b, half, j] = summed.astype(BF16)
        self.x_copy(u).start()

    def z_start(self, u):
        r = self.r
        b, j = self.where(u)
        self.x_copy(u).wait_recv()
        summed = r.grads_own[b, self.x, j].astype(F32) + r.from_x[b, j].astype(F32)
        r.grads_own[b, self.x, j] = summed.astype(BF16)
        for step in (1, 2, 3):
            self.z_copy(u, step).start()

    def g_start(self, u):
        r = self.r
        b, j = self.where(u)
        value = r.grads_own[b, self.x, j, self.z].astype(F32)
        for step in (1, 2, 3):
            self.z_copy(u, step).wait_recv()
            value = value + r.from_z[b, j, step - 1].astype(F32)
        if self.more > 1:
            r.grads_own[b, self.x, j, self.z] = value.astype(BF16)
            for step in range(1, self.more):
                self.f_copy(u, step).start()
            for step in range(1, self.more):
                self.f_copy(u, step).wait_recv()
                value = value + r.from_far[u, step - 1].astype(F32)
        r.total[b, self.x, j, self.z] = value.astype(BF16)
        for step in (1, 2, 3):
            self.g_copy(u, step, self.z).start()

    def h_start(self, u):
        for step in (1, 2, 3):
            self.g_copy(u, step, (self.z - step + 4) % 4).wait_recv()
        self.h_copy(u, self.x).start()

    def advance(self, n, least=0):
        stages = (self.h_start, self.g_start, self.z_start, self.x_start)
        for behind, stage in zip(LAGS, stages):
            if isinstance(n, int):
                if 0 <= n - behind < PIECES:
                    stage(n - behind)
            elif least >= behind:
                stage(n - behind)
            else:
                pl.when(n >= behind)(functools.partial(stage, n - behind))

    def finish(self):
        def settle(u, _):
            self.h_copy(u, 1 - self.x).wait_recv()
            for copy in (self.y_copy(u), self.x_copy(u), self.h_copy(u, self.x)):
                copy.wait_send()
            for step in (1, 2, 3):
                self.z_copy(u, step).wait_send()
                self.g_copy(u, step, self.z).wait_send()
            for step in range(1, self.more):
                self.f_copy(u, step).wait_send()
            return 0

        lax.fori_loop(0, PIECES, settle, 0)
        for copy in self.sent:
            copy.wait_send()


def layer_kernel(groups, names, *refs):
    r = types.SimpleNamespace(**dict(zip(names, refs)))
    place = lax.axis_index("tensor")
    group = lax.axis_index("dp")
    core, side = place % 2, place // 2
    rows = r.q.shape[0]
    own_rows = rows // 2
    wide = r.x_rows.shape[1]
    both = r.q.shape[1]
    width = both // 2
    units = r.w_inner.shape[1]
    chunk = own_rows // 2
    strip = own_rows // 8
    mine = core * own_rows
    theirs = (1 - core) * own_rows
    c_start = pl.multiple_of((1 - side) * 2 * LEN, HALF)
    core_peer = {"tensor": place + 1 - 2 * core}
    side_peer = {"tensor": (place + 2) % 4}

    barrier = pltpu.get_barrier_semaphore()
    for step in (1, 2, 3):
        pl.semaphore_signal(barrier, inc=1, device_id={"tensor": (place + step) % 4}, device_id_type=MESH)

    def greet(step, _):
        peer = (group + step) % groups
        pl.semaphore_signal(barrier, inc=1, device_id={"dp": peer}, device_id_type=MESH)
        return 0

    lax.fori_loop(1, groups, greet, 0)

    def at_rows(start, count):
        return pl.ds(pl.multiple_of(start, 16), count)

    own_at = at_rows(mine, own_rows)
    loads = {}
    sources = [
        ("tokens", r.tokens, r.x_rows.at[own_at]),
        ("q", r.w_query, r.w_att.at[0, :, 0]),
        ("k", r.w_key, r.w_att.at[1, :, 0]),
        ("v", r.w_value, r.w_att.at[2, :, 0]),
        ("o", r.w_output, r.w_att.at[3, :, 0]),
        ("in", r.w_inner, r.in_own),
        ("down", r.w_outer, r.down_own),
        ("cotangent", r.cotangent, r.grad_tokens),
    ]
    sources += [("shift", r.b_query, r.narrow.at[0]), ("shift", r.b_value, r.narrow.at[1])]
    sources += [("shift", r.b_inner, r.biases.at[0])]
    gains = (r.b_output, r.first_gain, r.first_shift, r.b_outer, r.second_gain, r.second_shift)
    sources += [("gain", ref, r.vectors.at[i]) for i, ref in enumerate(gains)]
    sources += [("segment", r.segment_ids.at[pl.ds(i * LEN, LEN)], r.segments.at[i]) for i in range(5)]
    for n, (name, source, target) in enumerate(sources):
        copy = pltpu.make_async_copy(source, target, r.l_sem.at[n])
        copy.start()
        loads.setdefault(name, []).append(copy)

    def loaded(*wanted):
        for name in wanted:
            for copy in loads[name]:
                copy.wait()

    pl.semaphore_wait(barrier, 3 + groups - 1)
    rounds = Rounds(r, groups)
    x, z = rounds.x, rounds.z
    x_peer = rounds.dp_at(1 - x, z)

    lanes = wide // 2
    block = units // 8

    def by_heads(source, i):
        def view(ref, half):
            return ref.at[:, :, pl.ds(half * lanes, lanes)]

        return source, r.w_att.at[i, :, 1], view

    def by_rows(source, target, n):
        def view(ref, half):
            return ref.at[at_rows((half * 4 + n) * block, block)]

        return source, target, view

    fetches = [by_heads(w, i) for i, w in enumerate((r.w_query, r.w_key, r.w_value, r.w_output))]
    fetches += [by_rows(r.w_inner, r.in_other, n) for n in range(4)]
    fetches += [by_rows(r.w_outer, r.down_other, n) for n in range(4)]

    def fetch_copy(n):
        source, target, view = fetches[n]
        return remote(view(source, x), view(target, x), r.w_out_sem.at[n], r.w_in_sem.at[n], side_peer)

    def pass_copy(n, which):
        _, target, view = fetches[n]
        return remote(view(target, which), view(target, which), r.p_out_sem.at[n], r.p_in_sem.at[n], x_peer)

    def fetch(*which):
        for n in which:
            rounds.start(fetch_copy(n))

    def hand_on(*which):
        for n in which:
            fetch_copy(n).wait_recv()
            rounds.start(pass_copy(n, x))

    def fetched(*which):
        for n in which:
            pass_copy(n, 1 - x).wait_recv()

    token_copy = rounds.start(remote(r.tokens, r.x_rows.at[own_at], r.s_out.at[0], r.s_in.at[0], core_peer))
    token_wait = remote(r.tokens, r.x_rows.at[at_rows(theirs, own_rows)], r.s_out.at[0], r.s_in.at[0], core_peer)
    fetch(0, 1, 2)
    loaded("shift")
    vector_copies = [
        rounds.start(remote(r.biases, r.biases_other, r.s_out.at[1], r.s_in.at[1], side_peer)),
        rounds.start(remote(r.narrow, r.narrow_other, r.s_out.at[5], r.s_in.at[5], side_peer)),
    ]

    def project(shard, which, start, count, size):
        shifts = (r.narrow, r.narrow_other)[shard]
        for i in which:
            target = (r.q, r.k, r.v)[i]
            weights = r.w_att[i, :, shard].reshape(width, wide)

            def body(n, _):
                block = at_rows(start + n * size, size)
                value = dg(r.x_rows[block, :], weights, NT)
                if i == 0:
                    value = value + shifts[0:1, :]
                if i == 2:
                    value = value + shifts[1:2, :]
                value = value.astype(BF16)
                for j in range(PAIRS):
                    lane = (2 * j + shard) * HD
                    target[block, lane : lane + HD] = value[:, j * HD : (j + 1) * HD]
                return 0

            lax.fori_loop(0, count // size, body, 0)

    loaded("tokens")
    loaded("q", "k", "v")
    project(0, (0, 1, 2), mine, own_rows, chunk)

    token_wait.wait_recv()
    quarter = HALF // 2
    far_at = at_rows(rows + core * quarter, quarter)
    far_there = at_rows(rows + (1 - core) * quarter, quarter)
    near_at = at_rows(c_start + core * quarter, quarter)
    far_copy = rounds.start(
        remote(r.x_rows.at[near_at], r.x_rows.at[far_at], r.s_out.at[2], r.s_in.at[2], side_peer)
    )
    fetch(*range(3, 12))
    project(0, (0, 1, 2), theirs, own_rows, chunk)
    hand_on(0)

    loaded("segment")

    def mask_block(at, row, places, length, count):
        column = jnp.transpose(jnp.broadcast_to(row.astype(F32), (128, LEN)))[:, 0:1]
        same = column == row.astype(F32)[:, :count]
        live = places < length
        first = lax.broadcasted_iota(jnp.int32, (LEN, count), 0)
        second = lax.broadcasted_iota(jnp.int32, (LEN, count), 1)
        allowed = same & live | (first == second)
        r.bias[:, at : at + count] = jnp.where(allowed, 0.0, NEGATIVE)

    ahead = lax.broadcasted_iota(jnp.int32, (LEN, 1), 0)
    for which in range(2):
        index = 3 * side + which
        mask_block(which * LEN, r.segments[pl.ds(index, 1), :], ahead, r.lengths[index], LEN)
    near = r.segments[2:3, pl.ds(pl.multiple_of(side * HALF, HALF), HALF)]
    away_row = r.segments[2:3, pl.ds(pl.multiple_of((1 - side) * HALF, HALF), HALF)]
    turned = jnp.where(ahead < HALF, ahead + side * HALF, ahead - side * HALF)
    mask_block(2 * LEN, jnp.concatenate([near, away_row], axis=1), turned, r.lengths[2], HALF)
    hand_on(1)

    def front_store(shard, block, lanes, out):
        if shard == 0:
            r.ctx[block, lanes] = jnp.concatenate([out, jnp.zeros_like(out)], axis=1)
        else:
            r.ctx[block, lanes] = jnp.concatenate([r.ctx[block, lanes][:, :HD], out], axis=1)

    def front_whole(shard, first_pair, last_pair):
        cols = slice(shard * HD, (shard + 1) * HD)

        def body(j, _):
            lanes = pair_lanes(j)
            for i in range(2):
                block = at_rows(side * HALF + i * LEN, LEN)
                at = pl.ds(i * LEN, LEN)
                out, row = attend_front(
                    r.q[block, lanes][:, cols], r.k[block, lanes][:, cols], r.v[block, lanes][:, cols], r.bias[:, at]
                )
                front_store(shard, block, lanes, out)
                r.lse[pl.ds(2 * j + shard, 1), at] = row
            return 0

        lax.fori_loop(first_pair, last_pair, body, 0)

    def front_half():
        def body(j, _):
            lanes = pair_lanes(j)
            block = pl.ds(c_start, HALF)
            at = pl.ds(2 * LEN, HALF)
            q, k, v = r.q[block, lanes], r.kc[:, lanes], r.vc[:, lanes]
            outs = []
            for shard in range(2):
                cols = slice(shard * HD, (shard + 1) * HD)
                out, row = attend_front(q[:, cols], k[:, cols], v[:, cols], r.bias[:, at])
                outs.append(out)
                r.lse[pl.ds(2 * j + shard, 1), at] = row
            r.ctx[block, lanes] = jnp.concatenate(outs, axis=1)
            return 0

        lax.fori_loop(0, PAIRS, body, 0)

    front_whole(0, 0, 2)
    hand_on(2)
    front_whole(0, 2, 3)
    far_copy.wait_recv()
    far_pass = rounds.start(
        remote(r.x_rows.at[far_at], r.x_rows.at[far_at], r.s_out.at[3], r.s_in.at[3], core_peer)
    )
    far_wait = remote(r.x_rows.at[far_there], r.x_rows.at[far_there], r.s_out.at[3], r.s_in.at[3], core_peer)
    for copy in vector_copies:
        copy.wait_recv()
    fetched(0)
    project(1, (0,), 0, rows, chunk)
    fetched(1)
    project(1, (1,), 0, rows, chunk)
    hand_on(3)
    fetched(2)
    project(1, (2,), 0, rows, chunk)
    far_wait.wait_recv()
    for shard in range(2):
        project(shard, (1, 2), rows, HALF, HALF)
    for own, near_far in ((r.k, r.kc), (r.v, r.vc)):
        near_far[pl.ds(0, HALF), :] = own[pl.ds(c_start, HALF), :]
        near_far[pl.ds(HALF, HALF), :] = own[pl.ds(rows, HALF), :]
    front_whole(1, 0, 2)
    hand_on(4)
    front_whole(1, 2, 3)
    hand_on(5)
    front_half()

    loaded("o")
    fetched(3)

    def pairs_of(i):
        return r.w_att[i].reshape(both, wide)

    def each(start, count, size, body):
        def step(n, _):
            body(at_rows(start + n * size, size), at_rows(n * size, size))
            return 0

        lax.fori_loop(0, count // size, step, 0)

    trades = []

    def trade_rows(compute, keep):
        def away_body(block, local):
            r.partial[local, :] = compute(block, local, True).astype(BF16)

        each(theirs, own_rows, chunk, away_body)
        n = len(trades)
        trades.append(
            rounds.start(remote(r.partial, r.partial_in, r.t_out.at[n], r.t_in.at[n], core_peer))
        )

        def own_body(block, local):
            keep(local, compute(block, local, False))

        each(mine, own_rows, chunk, own_body)
        trades[n].wait_recv()
        rounds.settle(trades[n])

    def gather_rows(ref, n):
        copy = rounds.start(remote(ref.at[own_at], ref.at[own_at], r.a_out.at[n], r.a_in.at[n], core_peer))
        there = ref.at[at_rows(theirs, own_rows)]
        return copy, remote(there, there, r.a_out.at[n], r.a_in.at[n], core_peer)

    def keep_acc(local, value):
        r.acc[local, :] = value

    trade_rows(lambda block, local, away: dg(r.ctx[block, :], pairs_of(3)), keep_acc)
    loaded("gain")
    b_output, first_gain, first_shift = (r.vectors[i : i + 1, :] for i in range(3))
    b_outer, second_gain, second_shift = (r.vectors[i : i + 1, :] for i in range(3, 6))

    def first_norm(block, local):
        value = r.x_rows[block, :].astype(F32) + r.acc[local, :] + r.partial_in[local, :].astype(F32) + b_output
        unit, inverse = normalize(value)
        r.acc[local, :] = unit
        r.inverse[local, :] = inverse
        r.first[block, :] = (unit * first_gain + first_shift).astype(BF16)

    each(mine, own_rows, strip, first_norm)
    first_copy, first_wait = gather_rows(r.first, 0)
    hand_on(6)

    def expand(shard, start, part=None):
        weights = (r.in_own, r.in_other)[shard]
        shifts = (r.biases, r.biases_other)[shard]
        hidden, slope = ((r.hidden_own, r.slope_own), (r.hidden_other, r.slope_other))[shard]

        def body(block, _):
            value, gradient = gelu_and_slope(dg(r.first[block, :], weights[...]) + shifts[0:1, :])
            hidden[block, :] = value.astype(BF16)
            slope[block, :] = gradient.astype(BF16)

        if part is None:
            each(start, own_rows, chunk, body)
        else:
            each(start + part * chunk, chunk, chunk, body)

    loaded("in")
    expand(0, mine)
    hand_on(7)
    first_wait.wait_recv()
    expand(0, theirs, 0)
    hand_on(8)
    expand(0, theirs, 1)
    hand_on(9)
    loaded("down")

    def own_part(target):
        def body(block, local):
            target[local, :] = dg(r.hidden_own[block, :], r.down_own[...])

        return body

    each(theirs, own_rows, chunk, own_part(r.spare))
    hand_on(10)
    each(mine, own_rows, chunk, own_part(r.second))
    hand_on(11)
    fetched(4, 5, 6, 7)
    expand(1, theirs)
    expand(1, mine)
    fetched(8, 9, 10, 11)

    def other_part(block, local, away):
        kept = r.spare if away else r.second
        return kept[local, :] + dg(r.hidden_other[block, :], r.down_other[...])

    def keep_second(local, value):
        r.second[local, :] = value

    trade_rows(other_part, keep_second)
    loaded("cotangent")
    zero = jnp.zeros((1, wide), F32)

    def second_norm(n, carry):
        block, local = at_rows(mine + n * strip, strip), at_rows(n * strip, strip)
        value = r.first[block, :].astype(F32) + r.second[local, :] + r.partial_in[local, :].astype(F32) + b_outer
        unit, inverse = normalize(value)
        r.output[local, :] = (unit * second_gain + second_shift).astype(BF16)
        upstream = r.grad_tokens[local, :].astype(F32)
        grad = norm_backward(upstream, unit, inverse, second_gain)
        r.second[local, :] = grad
        low = grad.astype(BF16)
        r.feed[block, :] = low
        gain, shift, lows = carry
        return gain + column_sum(upstream * unit), shift + column_sum(upstream), lows + column_sum(low.astype(F32))

    sum_second_gain, sum_second_shift, sum_b_outer = lax.fori_loop(
        0, own_rows // strip, second_norm, (zero, zero, zero)
    )
    feed_copy, feed_wait = gather_rows(r.feed, 1)

    def contract(shard, start, carry):
        weights = (r.down_own, r.down_other)[shard]
        slope = (r.slope_own, r.slope_other)[shard]

        def body(n, total):
            block = at_rows(start + n * chunk, chunk)
            value = dg(r.feed[block, :], weights[...], NT) * slope[block, :].astype(F32)
            low = value.astype(BF16)
            slope[block, :] = low
            return total + column_sum(low.astype(F32))

        return lax.fori_loop(0, own_rows // chunk, body, carry)

    sum_own = contract(0, mine, jnp.zeros((1, units), F32))
    sum_other = contract(1, mine, jnp.zeros((1, units), F32))
    feed_wait.wait_recv()

    def weight_blocks(target, band, left, right, first):
        columns = left.shape[1] // 3

        def body(n, _):
            value = dg(left[:, pl.ds(pl.multiple_of(n * columns, 128), columns)], right[...], TN).astype(BF16)
            for i in range(4):
                at = 4 * n + i
                b, h, j = band + lax.div(at, 6), lax.div(lax.rem(at, 6), 3), lax.rem(at, 3)
                target[b, h, j] = value[i * HD : (i + 1) * HD].reshape(4, HD // 4, value.shape[1])
            if first is not None:

                @pl.when(n == 0)
                def _():
                    rounds.y_start(first)

            return 0

        lax.fori_loop(0, 3, body, 0)

    def send(first, last):
        def body(u, _):
            rounds.y_start(u)
            return 0

        lax.fori_loop(first, last, body, 0)

    weight_blocks(r.grads_other, 0, r.hidden_other, r.feed, 0)
    send(1, 6)
    weight_blocks(r.grads_own, 0, r.hidden_own, r.feed, None)
    sum_own = contract(0, theirs, sum_own)
    sum_other = contract(1, theirs, sum_other)
    rounds.advance(0)

    def keep_first(local, value):
        r.second[local, :] = r.second[local, :] + value

    trade_rows(
        lambda block, local, away: dg(r.slope_own[block, :], r.in_own[...], NT) + dg(r.slope_other[block, :], r.in_other[...], NT),
        keep_first,
    )
    rounds.settle(feed_copy)
    rounds.advance(1)

    def first_back(n, carry):
        block, local = at_rows(mine + n * strip, strip), at_rows(n * strip, strip)
        grad_first = r.second[local, :] + r.partial_in[local, :].astype(F32)
        unit = r.acc[local, :]
        grad = norm_backward(grad_first, unit, r.inverse[local, :], first_gain)
        r.second[local, :] = grad
        low = grad.astype(BF16)
        r.feed[block, :] = low
        gain, shift, lows = carry
        return gain + column_sum(grad_first * unit), shift + column_sum(grad_first), lows + column_sum(low.astype(F32))

    sum_first_gain, sum_first_shift, sum_b_output = lax.fori_loop(0, own_rows // strip, first_back, (zero, zero, zero))
    branch_copy, branch_wait = gather_rows(r.feed, 2)
    rounds.advance(2)
    weight_blocks(r.grads_other, 2, r.first, r.slope_other, None)
    send(6, 12)
    weight_blocks(r.grads_own, 2, r.first, r.slope_own, None)
    rounds.advance(3)
    branch_wait.wait_recv()

    dq = r.hidden_own.at[:, pl.ds(0, both)]
    dk = r.hidden_own.at[:, pl.ds(both, both)]
    dv = r.hidden_other.at[:, pl.ds(0, both)]
    gc = r.hidden_other.at[:, pl.ds(both, both)]

    def context_back(block, _):
        gc[block, :] = dg(r.feed[block, :], pairs_of(3), NT).astype(BF16)

    each(0, rows, chunk, context_back)

    def back_half(j, _):
        lanes = pair_lanes(j)
        at = pl.ds(2 * LEN, HALF)
        stats = [r.lse[pl.ds(j * 2 + h, 1), at] for h in range(2)]
        block = pl.ds(c_start, HALF)
        d_q, d_k, d_v = pair_back(
            r.q[block, lanes], r.kc[:, lanes], r.vc[:, lanes], gc[block, lanes], r.bias[:, at], stats
        )
        dq[block, lanes] = d_q
        dk[block, lanes] = d_k[:HALF]
        dv[block, lanes] = d_v[:HALF]
        r.away[0, :, lanes] = d_k[HALF:]
        r.away[1, :, lanes] = d_v[HALF:]
        return 0

    lax.fori_loop(0, PAIRS, back_half, 0)
    rounds.advance(4)

    grad_out = dg(r.ctx[...], r.feed[...], TN).astype(BF16)
    for j in range(PAIRS):
        for shard, target in ((0, r.grads_own), (1, r.grads_other)):
            lane = (2 * j + shard) * HD
            target[5, 1, j] = grad_out[lane : lane + HD].reshape(4, HD // 4, wide)

    def back_whole(j):
        def body(i, _):
            lanes = pair_lanes(j)
            block = at_rows(side * HALF + i * LEN, LEN)
            at = pl.ds(pl.multiple_of(i * LEN, LEN), LEN)
            stats = [r.lse[pl.ds(j * 2 + h, 1), at] for h in range(2)]
            d_q, d_k, d_v = pair_back(
                r.q[block, lanes], r.k[block, lanes], r.v[block, lanes], gc[block, lanes], r.bias[:, at], stats
            )
            dq[block, lanes] = d_q
            dk[block, lanes] = d_k
            dv[block, lanes] = d_v
            return 0

        lax.fori_loop(0, 2, body, 0)

    def weight_pair(j):
        lanes = pair_lanes(j)
        left = jnp.concatenate([dq[:, lanes], dk[:, lanes], dv[:, lanes]], axis=1)
        value = dg(left, r.x_rows[pl.ds(0, rows), :], TN)
        far_left = jnp.concatenate([r.away[0, :, lanes], r.away[1, :, lanes]], axis=1)
        far = dg(far_left, r.x_rows[pl.ds(rows, HALF), :], TN)
        first = value[: 2 * HD].astype(BF16)
        rest = (value[2 * HD :] + far).astype(BF16)
        at = 12 + 2 * j
        for shard, target in ((0, r.grads_own), (1, r.grads_other)):
            cut = slice(shard * HD, (shard + 1) * HD)
            pieces = [v[cut].reshape(4, HD // 4, wide) for v in (first, rest[: 2 * HD], rest[2 * HD :])]
            target[4, 0, j] = pieces[0]
            target[4, 1, j] = pieces[1]
            target[5, 0, j] = pieces[2]
        rounds.y_start(at)
        rounds.y_start(at + 1)

    def back_pair(j, _):
        back_whole(j)
        rounds.advance(5 + 2 * j, 5)
        weight_pair(j)
        rounds.advance(6 + 2 * j, 6)
        return 0

    lax.fori_loop(0, PAIRS, back_pair, 0)

    rounds.advance(11)
    rounds.advance(12)

    def bias_sum(*grads):
        total = sum(column_sum(part) for part in grads)
        heads = [total[:, i * HD : (i + 1) * HD] for i in range(2 * PAIRS)]
        return jnp.concatenate(heads[0::2], axis=1), jnp.concatenate(heads[1::2], axis=1)

    sums = (sum_b_output, sum_first_gain, sum_first_shift, sum_b_outer, sum_second_gain, sum_second_shift)
    for t in range(PARTS):
        shares = [value[:, t * width : (t + 1) * width] for value in sums]
        r.tiny[t, 0:1, :] = jnp.concatenate(shares[:4], axis=1)
        r.tiny[t, 1:2, :] = jnp.concatenate(shares[4:] + [jnp.zeros((1, 2 * width), F32)], axis=1)
        r.tiny[t, 2:3, :] = jnp.zeros((1, units), F32)
    queries, values = bias_sum(dq[...].astype(F32)), bias_sum(dv[...].astype(F32), r.away[1].astype(F32))
    for target, n, inner in ((place, 0, sum_own), ((place + 2) % 4, 1, sum_other)):
        r.tiny[target, 1:2, 2 * width :] = jnp.concatenate([queries[n], values[n]], axis=1)
        r.tiny[target, 2:3, :] = inner
    tiny_copies = []
    for step in (1, 2, 3):
        peer = (place + step) % 4
        out, into = r.i_out.at[step - 1], r.i_in.at[step - 1]
        tiny_copies.append(rounds.start(remote(r.tiny.at[peer], r.tiny_side.at[step - 1], out, into, {"tensor": peer})))

    def input_rows(block, local, away):
        value = dg(dq[block, :], pairs_of(0))
        value = value + dg(dk[block, :], pairs_of(1))
        return value + dg(dv[block, :], pairs_of(2))

    r.far_part[...] = (dg(r.away[0], pairs_of(1)) + dg(r.away[1], pairs_of(2))).astype(BF16)
    give = at_rows((1 - core) * quarter, quarter)
    keep = at_rows(core * quarter, quarter)
    far_trade = rounds.start(
        remote(r.far_part.at[give], r.far_half, r.s_out.at[4], r.s_in.at[4], core_peer)
    )
    rounds.advance(13)
    far_trade.wait_recv()
    r.far_send[...] = (r.far_part[keep, :].astype(F32) + r.far_half[...].astype(F32)).astype(BF16)
    owner = {"tensor": (1 - side) * 2 + side}
    rounds.start(remote(r.far_send, r.far_in.at[core], r.o_out, r.o_in.at[core], owner))

    rounds.advance(14)
    trade_rows(input_rows, keep_first)
    rounds.advance(15)

    total = r.tiny[place]
    for step in (1, 2, 3):
        tiny_copies[step - 1].wait_recv()
        total = total + r.tiny_side[step - 1]
    r.tiny_all[0] = total

    def tell(step, _):
        peer = {"dp": (group + step) % groups}
        remote(r.tiny_all.at[0], r.tiny_all.at[step], r.d_out.at[step], r.d_in.at[step], peer).start()
        return 0

    lax.fori_loop(1, groups, tell, 0)

    def pump(n, _):
        rounds.advance(n, 16)
        return 0

    lax.fori_loop(16, PIECES, pump, 0)
    rounds.advance(PIECES)

    for n in range(PIECES + 1, PIECES + LAGS[0] - 2):
        rounds.advance(n)

    @pl.when(core == 1 - side)
    def _():
        start = (1 - side) * (own_rows - HALF)
        for n in range(2):
            remote(r.far_send, r.far_in.at[n], r.o_out, r.o_in.at[n], owner).wait_recv()
            block = at_rows(start + n * quarter, quarter)
            r.second[block, :] = r.second[block, :] + r.far_in[n].astype(F32)

    def finish(block, local):
        r.grad_tokens[local, :] = (r.second[local, :] + r.partial_in[local, :].astype(F32)).astype(BF16)

    each(mine, own_rows, strip, finish)

    for n in range(PIECES + LAGS[0] - 2, PIECES + LAGS[0]):
        rounds.advance(n)

    def hear(step, total):
        peer = {"dp": (group + step) % groups}
        copy = remote(r.tiny_all.at[0], r.tiny_all.at[step], r.d_out.at[step], r.d_in.at[step], peer)
        copy.wait()
        return total + r.tiny_all[step]

    r.small[0:3, :] = lax.fori_loop(1, groups, hear, r.tiny_all[0])
    r.small[3:8, :] = jnp.zeros((5, wide), F32)

    rounds.finish()


def layer(groups, named):
    dma = pltpu.SemaphoreType.DMA
    own_rows, wide = named["tokens"].shape
    units = named["w_inner"].shape[1]
    heads = named["w_query"].shape
    rows, both = 2 * own_rows, 2 * heads[0] * heads[1]
    more = groups // OWNERS
    share = wide // 6 // OWNERS
    bands = (6, 2, 3, 4, share, wide)
    outs = dict(
        output=((own_rows, wide), BF16),
        grad_tokens=((own_rows, wide), BF16),
        total=(bands, BF16),
        small=((8, wide), F32),
    )
    room = dict(
        x_rows=((rows + HALF, wide), BF16),
        w_att=((4, PAIRS, 2, HD, wide), BF16),
        in_own=((wide, units), BF16),
        in_other=((wide, units), BF16),
        down_own=((units, wide), BF16),
        down_other=((units, wide), BF16),
        vectors=((8, wide), F32),
        biases=((8, wide), F32),
        biases_other=((8, wide), F32),
        narrow=((8, both // 2), F32),
        narrow_other=((8, both // 2), F32),
        segments=((8, LEN), jnp.int32),
        bias=((LEN, rows), F32),
        q=((rows, both), BF16),
        k=((rows + HALF, both), BF16),
        v=((rows + HALF, both), BF16),
        kc=((LEN, both), BF16),
        vc=((LEN, both), BF16),
        ctx=((rows, both), BF16),
        lse=((8, rows), F32),
        partial=((own_rows, wide), BF16),
        partial_in=((own_rows, wide), BF16),
        acc=((own_rows, wide), F32),
        inverse=((own_rows, 1), F32),
        first=((rows, wide), BF16),
        hidden_own=((rows, units), BF16),
        hidden_other=((rows, units), BF16),
        slope_own=((rows, units), BF16),
        slope_other=((rows, units), BF16),
        second=((own_rows, wide), F32),
        spare=((own_rows, wide), F32),
        feed=((rows, wide), BF16),
        away=((2, HALF, both), BF16),
        far_part=((HALF, wide), BF16),
        far_half=((HALF // 2, wide), BF16),
        far_send=((HALF // 2, wide), BF16),
        far_in=((2, HALF // 2, wide), BF16),
        grads_own=(bands, BF16),
        grads_other=(bands, BF16),
        from_side=(bands, BF16),
        from_x=((6, 3, 4, share, wide), BF16),
        from_z=((6, 3, 3, share, wide), BF16),
        from_far=((PIECES, more - 1, share, wide) if more > 1 else (1, 1, 16, 128), BF16),
        tiny=((PARTS, 3, wide), F32),
        tiny_side=((3, 3, wide), F32),
        tiny_all=((groups, 3, wide), F32),
    )
    sems = dict(
        l_sem=(22,),
        s_out=(6,),
        s_in=(6,),
        w_out_sem=(12,),
        w_in_sem=(12,),
        p_out_sem=(12,),
        p_in_sem=(12,),
        t_out=(4,),
        t_in=(4,),
        a_out=(3,),
        a_in=(3,),
        y_out=(PIECES,),
        y_in=(PIECES,),
        x_out=(PIECES,),
        x_in=(PIECES,),
        z_out=(PIECES, 3),
        z_in=(PIECES, 3),
        g_out=(PIECES, 3),
        g_in=(PIECES, 3),
        h_out=(PIECES,),
        h_in=(PIECES,),
        f_out=(PIECES, max(more - 1, 1)),
        f_in=(PIECES, max(more - 1, 1)),
        i_out=(3,),
        i_in=(3,),
        d_out=(groups,),
        d_in=(groups,),
        o_out=(),
        o_in=(2,),
    )
    names = list(named) + list(outs) + list(room) + list(sems)
    in_vmem = pl.BlockSpec(memory_space=pltpu.VMEM)
    spaces = {"lengths": pltpu.SMEM}
    results = pl.pallas_call(
        functools.partial(layer_kernel, groups, names),
        out_shape=[jax.ShapeDtypeStruct(*spec) for spec in outs.values()],
        in_specs=[pl.BlockSpec(memory_space=spaces.get(name, pl.ANY)) for name in named],
        out_specs=[in_vmem] * len(outs),
        scratch_shapes=[pltpu.VMEM(*spec) for spec in room.values()] + [dma(shape) for shape in sems.values()],
        compiler_params=pltpu.CompilerParams(
            collective_id=0, has_side_effects=True, vmem_limit_bytes=67043328
        ),
    )(*named.values())
    return dict(zip(outs, results))


def last_kernel(total, output, grad_tokens, small, *refs):
    results, (low, full, rows, sums, narrow, load_sem, store_sem) = refs[:17], refs[17:]
    loads = [pltpu.make_async_copy(small, sums, load_sem.at[14])]
    loads += [pltpu.make_async_copy(source, rows.at[i], load_sem.at[12 + i]) for i, source in enumerate((output, grad_tokens))]
    loads += [pltpu.make_async_copy(total.at[i], low.at[i], load_sem.at[i]) for i in range(12)]
    for copy in loads:
        copy.start()
    stores = []

    def store(source, target):
        stores.append(pltpu.make_async_copy(source, target, store_sem.at[len(stores)]))
        stores[-1].start()

    loads[0].wait()
    width = narrow.shape[1]
    for i in range(8):
        lane = i % 4 * width
        narrow[i : i + 1, :] = sums[i // 4 : i // 4 + 1, lane : lane + width]
        store(narrow.at[i], results[8 + i])
    store(sums.at[2], results[16])
    for i in range(2):
        loads[1 + i].wait()
        store(rows.at[i], results[i])
    count = low.shape[1]
    for i in range(12):
        loads[3 + i].wait()
        full[i] = low[i].astype(F32)
        target = results[2 + i // 4].at[pl.ds(i % 4 * count, count)] if i < 8 else results[4 + i - 8]
        store(full.at[i], target)
    for copy in stores:
        copy.wait()


def last(done):
    own_rows, wide = done["output"].shape
    total = done["total"].reshape(12, -1, wide)
    count = total.shape[1]
    rows = jax.ShapeDtypeStruct((own_rows, wide), BF16)
    large = jax.ShapeDtypeStruct((4 * count, wide), F32)
    slim = jax.ShapeDtypeStruct((count, wide), F32)
    outs = [rows] * 2 + [large] * 2 + [slim] * 4
    outs += [jax.ShapeDtypeStruct((wide // PARTS,), F32)] * 8 + [jax.ShapeDtypeStruct((wide,), F32)]
    anywhere = pl.BlockSpec(memory_space=pl.ANY)
    return pl.pallas_call(
        last_kernel,
        out_shape=outs,
        in_specs=[anywhere] * 4,
        out_specs=[anywhere] * len(outs),
        scratch_shapes=[
            pltpu.VMEM(total.shape, BF16),
            pltpu.VMEM(total.shape, F32),
            pltpu.VMEM((2, own_rows, wide), BF16),
            pltpu.VMEM((8, wide), F32),
            pltpu.VMEM((8, wide // PARTS), F32),
            pltpu.SemaphoreType.DMA((15,)),
            pltpu.SemaphoreType.DMA((23,)),
        ],
        compiler_params=pltpu.CompilerParams(vmem_limit_bytes=67043328),
    )(total, done["output"], done["grad_tokens"], done["small"])


def shards(
    tokens,
    segment_ids,
    lengths,
    w_query,
    b_query,
    w_key,
    w_value,
    b_value,
    w_output,
    b_output,
    first_gain,
    first_shift,
    w_inner,
    b_inner,
    w_outer,
    b_outer,
    second_gain,
    second_shift,
    cotangent,
):
    groups = lax.axis_size("dp")
    wide, width = w_query.shape
    units = w_inner.shape[1]
    by_head = (width // HD, HD, wide)
    done = layer(
        groups,
        dict(
            tokens=tokens,
            w_query=w_query.T.reshape(by_head),
            w_key=w_key.T.reshape(by_head),
            w_value=w_value.T.reshape(by_head),
            w_output=w_output.reshape(by_head),
            w_inner=w_inner,
            w_outer=w_outer,
            cotangent=cotangent,
            b_query=b_query,
            b_value=b_value,
            b_inner=b_inner,
            b_output=b_output,
            first_gain=first_gain,
            first_shift=first_shift,
            b_outer=b_outer,
            second_gain=second_gain,
            second_shift=second_shift,
            segment_ids=segment_ids,
            lengths=lengths,
        ),
    )
    output, grad_tokens, outer, inner, query, key, value, out, *shares, inner_shift = last(done)
    return (
        output,
        grad_tokens,
        query.T,
        shares[6],
        key.T,
        value.T,
        shares[7],
        out,
        shares[0],
        shares[1],
        shares[2],
        inner,
        inner_shift,
        outer,
        shares[3],
        shares[4],
        shares[5],
    )


def solution(mesh):
    in_specs = (
        P(("dp", "tensor"), None),
        P("dp"),
        P("dp"),
        P(None, "tensor"),
        P("tensor"),
        P(None, "tensor"),
        P(None, "tensor"),
        P("tensor"),
        P("tensor", None),
        P(),
        P(),
        P(),
        P(None, "tensor"),
        P("tensor"),
        P("tensor", None),
        P(),
        P(),
        P(),
        P(("dp", "tensor"), None),
    )
    out_specs = (
        P(("dp", "tensor"), None),
        P(("dp", "tensor"), None),
        P(None, "tensor"),
        P("tensor"),
        P(None, "tensor"),
        P(None, "tensor"),
        P("tensor"),
        P("tensor", None),
        P("tensor"),
        P("tensor"),
        P("tensor"),
        P(None, "tensor"),
        P("tensor"),
        P("tensor", None),
        P("tensor"),
        P("tensor"),
        P("tensor"),
    )
    return jax.shard_map(shards, mesh=mesh, in_specs=in_specs, out_specs=out_specs, check_vma=False)
```
